32 devices in a mesh: dp: 8 (over z, y), seq: 4 (over x, core).
Axes of the slice: x: 2, y: 2, z: 4, core: 2. Of those that a mesh axis runs over, the one named last changes fastest.
Arguments:
- frames: bfloat16 [16, 1024, 1536], P('dp', 'seq'), may hold values from -6 to 6
- text: bfloat16 [16, 64, 1536], P('dp', 'seq'), may hold values from -6 to 6
- cotangent: bfloat16 [16, 1024, 1536], P('dp', 'seq'), may hold values from -6 to 6
- norm_gains: bfloat16 [3, 1536], P(None, 'dp'), may hold values from 0.25 to 1.75
- norm_biases: bfloat16 [3, 1536], P(None, 'dp'), may hold values from -1.796875 to 1.796875
- qkv_weight: bfloat16 [1536, 4608], P('dp'), may hold values from -0.21875 to 0.21875
- self_out: bfloat16 [1536, 1536], P('dp'), may hold values from -0.625 to 0.625
- cross_query: bfloat16 [1536, 1536], P('dp'), may hold values from -0.21875 to 0.21875
- cross_kv: bfloat16 [1536, 3072], P('dp'), may hold values from -0.21875 to 0.21875
- cross_out: bfloat16 [1536, 1536], P('dp'), may hold values from -0.4375 to 0.4375
- up_weight: bfloat16 [1536, 6144], P('dp'), may hold values from -0.15625 to 0.15625
- down_weight: bfloat16 [6144, 1536], P('dp'), may hold values from -0.078125 to 0.078125
Outputs:
- block_output: bfloat16 [16, 1024, 1536], P('dp', 'seq')
- frame_grad: float32 [16, 1024, 1536], P('dp', 'seq')
- text_grad: float32 [16, 64, 1536], P('dp', 'seq')
- gain_grad: float32 [3, 1536], P(None, ('dp', 'seq'))
- bias_grad: float32 [3, 1536], P(None, ('dp', 'seq'))
- qkv_grad: float32 [1536, 4608], P(('dp', 'seq'))
- self_out_grad: float32 [1536, 1536], P(('dp', 'seq'))
- cross_query_grad: float32 [1536, 1536], P(('dp', 'seq'))
- cross_kv_grad: float32 [1536, 3072], P(('dp', 'seq'))
- cross_out_grad: float32 [1536, 1536], P(('dp', 'seq'))
- up_grad: float32 [1536, 6144], P(('dp', 'seq'))
- down_grad: float32 [6144, 1536], P(('dp', 'seq'))
The draws below stay inside these ranges and needn't reach their ends.
All inputs are finite; a program needn't handle non-finite values.
Results may differ from the reference program's by a relative error of at most 0.022.
The reference program's roundings to bfloat16 on the way count: a program that leaves them out, or rounds other values in their place, can miss the bound.
Values may be sent and summed in bfloat16 or wider, within the bound.
A program may use at most 512 MiB of HBM per device.

```python
import jax
import jax.numpy as jnp
from jax import lax

D = 1536
HEAD_DIM = 64
FF = 6144
FRAMES = 1024
TEXT = 64
CLIPS = 16


def with_spikes(array, own_key, source, target, shards_of, factor):
    def block_of(dim):
        return (jnp.arange(array.shape[dim]) // (array.shape[dim] // shards_of)).reshape((-1,) + (1,) * (array.ndim - 1 - dim))

    near = jax.random.permutation(own_key, shards_of)[block_of(target)]
    other_side = (block_of(target) + shards_of // 2) % shards_of
    return jnp.where((block_of(source) == near) | (block_of(source) == other_side), factor * array, array)


def block_scale(rng, dims, shards, smallest, top_value):
    level = 1.0
    for axis_at, shards_of in shards:
        steps = jax.random.uniform(jax.random.fold_in(jax.random.fold_in(rng, 6), axis_at), (shards_of,), jnp.float32, smallest / len(shards), top_value / len(shards))
        level = level * jnp.repeat(jnp.exp(steps), dims[axis_at] // shards_of).reshape((-1,) + (1,) * (len(dims) - 1 - axis_at))
    return level


def bell_draw(own_key, shape, scale, bound, split=(), held_as=jnp.bfloat16):
    array = scale * jax.random.normal(own_key, shape, jnp.float32)
    if split:
        array = array * block_scale(own_key, shape, split, -0.22, 0.18)
    return jnp.clip(array, -bound, bound).astype(held_as)


def gaussian_with(stream_key, dims, scale, bound, split, heavy, held_as=jnp.bfloat16):
    values = scale * jax.random.normal(stream_key, dims, jnp.float32)
    if split:
        values = values * block_scale(stream_key, dims, split, -0.22, 0.18)
    return jnp.clip(with_spikes(values, jax.random.fold_in(stream_key, 3), *heavy), -bound, bound).astype(held_as)


def setup_inputs(seed: int = 0) -> dict:
    streams_of = jax.random.split(jax.random.key(seed), 13)
    return {
        "frames": bell_draw(streams_of[0], (CLIPS, FRAMES, D), 1.0, 6.0, ((0, 8), (1, 4))),
        "text": bell_draw(streams_of[1], (CLIPS, TEXT, D), 1.0, 6.0, ((0, 8), (1, 4))),
        "cotangent": gaussian_with(streams_of[2], (CLIPS, FRAMES, D), 1.0, 6.0, ((0, 8), (1, 4)), (0, 2, 8, 2.0)),
        "norm_gains": jnp.clip(1.0 + 0.15 * jax.random.normal(streams_of[3], (3, D), jnp.float32), 0.25, 1.75).astype(jnp.bfloat16),
        "norm_biases": bell_draw(streams_of[4], (3, D), 0.3, 1.796875, ((1, 8),)),
        "qkv_weight": bell_draw(streams_of[5], (D, 3 * D), (D // 2) ** -0.5, 0.21875, ((0, 8),)),
        "self_out": bell_draw(streams_of[6], (D, D), (D // 16) ** -0.5, 0.625, ((0, 8),)),
        "cross_query": bell_draw(streams_of[7], (D, D), (D // 2) ** -0.5, 0.21875, ((0, 8),)),
        "cross_kv": bell_draw(streams_of[8], (D, 2 * D), (D // 2) ** -0.5, 0.21875, ((0, 8),)),
        "cross_out": bell_draw(streams_of[9], (D, D), (D // 8) ** -0.5, 0.4375, ((0, 8),)),
        "up_weight": bell_draw(streams_of[10], (D, FF), D ** -0.5, 0.15625, ((0, 8),)),
        "down_weight": bell_draw(streams_of[11], (FF, D), FF ** -0.5, 0.078125, ((0, 8),)),
    }


EPSILON = 1e-05
NEGATIVE = -1e+30

@jax.custom_vjp
def low(v):
    return lax.optimization_barrier(v.astype(jnp.bfloat16)).astype(jnp.float32)

@jax.custom_vjp
def low_back(v):
    return v

def low_keep(v):
    return (low(v), None)

def low_pass(kept, grad):
    return (grad,)

def back_keep(v):
    return (v, None)

def back_low(kept, grad):
    return (low(grad),)
low.defvjp(low_keep, low_pass)
low_back.defvjp(back_keep, back_low)

def layer_norm(values, norm_gain, norm_shift):
    center = lax.optimization_barrier(jnp.mean(values, axis=-1, keepdims=True))
    centered = values - center
    spread = lax.optimization_barrier(jnp.mean(centered * centered, axis=-1, keepdims=True))
    return centered * lax.rsqrt(spread + EPSILON) * norm_gain + norm_shift

def matmul_exact(left_side, right_side):
    return jnp.dot(left_side, right_side, precision=lax.Precision.HIGHEST)

def attend(query_heads, key_heads, value_heads, causal):
    factor = HEAD_DIM ** (-0.5)
    scores = jnp.einsum('qhd,khd->hqk', query_heads, key_heads, precision=lax.Precision.HIGHEST) * factor
    scores = low_back(scores)
    if causal:
        rows_here = lax.broadcasted_iota(jnp.int32, scores.shape[1:], 0)
        columns = lax.broadcasted_iota(jnp.int32, scores.shape[1:], 1)
        scores = jnp.where((columns <= rows_here)[None], scores, NEGATIVE)
    shares = jax.nn.softmax(scores, axis=-1)
    return jnp.einsum('hqk,khd->qhd', low(shares), value_heads, precision=lax.Precision.HIGHEST)

def clip_forward(weights, frame_rows, text_rows):
    gain_rows, bias_rows, w_qkv, w_self, w_query, w_pair, w_cross, w_up, w_down = weights
    length = frame_rows.shape[0]
    text_count = text_rows.shape[0]
    normed_one = low(layer_norm(frame_rows, gain_rows[0], bias_rows[0]))
    triple = low_back(low(matmul_exact(normed_one, w_qkv))).reshape(length, 3, -1, HEAD_DIM)
    self_mix = low_back(low(attend(triple[:, 0], triple[:, 1], triple[:, 2], True))).reshape(length, -1)
    first_sum = frame_rows + low_back(matmul_exact(self_mix, w_self))
    normed_two = low(layer_norm(first_sum, gain_rows[1], bias_rows[1]))
    cross_q = low_back(low(matmul_exact(normed_two, w_query))).reshape(length, -1, HEAD_DIM)
    text_kv = low_back(low(matmul_exact(text_rows, w_pair))).reshape(text_count, 2, -1, HEAD_DIM)
    cross_mix = low_back(low(attend(cross_q, text_kv[:, 0], text_kv[:, 1], False))).reshape(length, -1)
    second_sum = first_sum + low_back(matmul_exact(cross_mix, w_cross))
    normed_three = low(layer_norm(second_sum, gain_rows[2], bias_rows[2]))
    hidden_pre = low_back(matmul_exact(normed_three, w_up))
    activated = low(jax.nn.gelu(hidden_pre, approximate=False))
    return second_sum + low_back(matmul_exact(activated, w_down))

def reference(frames, text, cotangent, norm_gains, norm_biases, qkv_weight, self_out, cross_query, cross_kv, cross_out, up_weight, down_weight):
    weights = tuple((matrix.astype(jnp.float32) for matrix in (norm_gains, norm_biases, qkv_weight, self_out, cross_query, cross_kv, cross_out, up_weight, down_weight)))
    frame_rows = frames.astype(jnp.float32)
    text_rows = text.astype(jnp.float32)

    def forward(weight_set, frame_set, text_set):
        stepper = jax.checkpoint(clip_forward)
        return lax.map(lambda clip_pair: stepper(weight_set, clip_pair[0], clip_pair[1]), (frame_set, text_set))
    result, pullback = jax.vjp(forward, weights, frame_rows, text_rows)
    weight_grads, frame_grad, text_grad = pullback(cotangent.astype(jnp.float32))
    gain_grad, bias_grad, qkv_grad, self_out_grad, cross_query_grad, cross_kv_grad, cross_out_grad, up_grad, down_grad = weight_grads
    return (result.astype(jnp.bfloat16), frame_grad, text_grad, gain_grad, bias_grad, qkv_grad, self_out_grad, cross_query_grad, cross_kv_grad, cross_out_grad, up_grad, down_grad)
```

```python
import functools

import jax
import jax.numpy as jnp
from jax import lax
from jax.experimental import pallas as pl
from jax.experimental.pallas import tpu as pltpu
from jax.sharding import PartitionSpec as P

HEAD_DIM = 64
EPSILON = 1e-05
NEGATIVE = -1e30
BF = jnp.bfloat16
F32 = jnp.float32

REL = (0, 2, 3, 1)
PLACE = (0, 3, 1, 2)


def dot_nn(a, b):
    return lax.dot_general(a, b, (((1,), (0,)), ((), ())), preferred_element_type=F32)


def dot_nt(a, b):
    return lax.dot_general(a, b, (((1,), (1,)), ((), ())), preferred_element_type=F32)


def dot_tn(a, b):
    return lax.dot_general(a, b, (((0,), (0,)), ((), ())), preferred_element_type=F32)


def after(value, *others):
    return lax.optimization_barrier((value,) + others)[0]


def self_forward_kernel(place_ref, q_ref, k_ref, v_ref, o_ref, l_ref):
    parts, rows = q_ref.shape[0], q_ref.shape[2]
    heads = q_ref.shape[3] // HEAD_DIM
    keys_at = lax.broadcasted_iota(jnp.int32, (rows, rows), 0)
    rows_at = lax.broadcasted_iota(jnp.int32, (rows, rows), 1)
    visible = keys_at <= rows_at
    for a in range(parts):
        here = place_ref[a]
        mixed = []
        for h in range(heads):
            cols = slice(h * HEAD_DIM, (h + 1) * HEAD_DIM)
            q = q_ref[here, 0, :, cols] * (HEAD_DIM**-0.5)
            scores = []
            for b in range(a + 1):
                s = dot_nt(k_ref[place_ref[b], 0, :, cols], q)
                if a == b:
                    s = jnp.where(visible, s, NEGATIVE)
                scores.append(s)
            top = functools.reduce(jnp.maximum, [jnp.max(s, axis=0, keepdims=True) for s in scores])
            raised = [jnp.exp(s - top) for s in scores]
            total = functools.reduce(jnp.add, [jnp.sum(e, axis=0, keepdims=True) for e in raised])
            share = 1.0 / total
            out = None
            for b in range(a + 1):
                p = (raised[b] * share).astype(BF)
                term = dot_tn(v_ref[place_ref[b], 0, :, cols], p)
                out = term if out is None else out + term
            mixed.append(out)
            l_ref[0, h, a : a + 1, :] = top + jnp.log(total)
        o_ref[here, 0] = jnp.concatenate(mixed, axis=0).T.astype(BF)


def self_forward(place, triple, width):
    parts, clips, rows, _ = triple.shape
    groups = width // 128
    block = (parts, 1, rows, 128)
    return pl.pallas_call(
        self_forward_kernel,
        out_shape=(
            jax.ShapeDtypeStruct((parts, clips, rows, width), BF),
            jax.ShapeDtypeStruct((clips, width // HEAD_DIM, parts, rows), F32),
        ),
        grid_spec=pltpu.PrefetchScalarGridSpec(
            num_scalar_prefetch=1,
            grid=(clips, groups),
            in_specs=[
                pl.BlockSpec(block, lambda i, j, p: (0, i, 0, j)),
                pl.BlockSpec(block, lambda i, j, p: (0, i, 0, groups + j)),
                pl.BlockSpec(block, lambda i, j, p: (0, i, 0, 2 * groups + j)),
            ],
            out_specs=[
                pl.BlockSpec(block, lambda i, j, p: (0, i, 0, j)),
                pl.BlockSpec((1, 2, parts, rows), lambda i, j, p: (i, j, 0, 0)),
            ],
        ),
        compiler_params=pltpu.CompilerParams(vmem_limit_bytes=40 << 20),
        cost_estimate=pl.CostEstimate(
            flops=clips * width * rows * rows * 10 * 4,
            bytes_accessed=clips * rows * parts * width * 8,
            transcendentals=clips * (width // HEAD_DIM) * rows * rows * 10,
        ),
        name="self_forward",
    )(place, triple, triple, triple)


def self_backward_kernel(place_ref, q_ref, k_ref, v_ref, g0, g1, g2, g3, l_ref, out_ref, gk_ref, gv_ref):
    parts, rows = q_ref.shape[0], q_ref.shape[2]
    heads = q_ref.shape[3] // HEAD_DIM
    width = out_ref.shape[3] // 3
    scale = HEAD_DIM**-0.5
    column = pl.multiple_of(pl.program_id(1) * 128, 128)
    keys_at = lax.broadcasted_iota(jnp.int32, (rows, rows), 0)
    rows_at = lax.broadcasted_iota(jnp.int32, (rows, rows), 1)
    visible = keys_at <= rows_at
    g_refs = (g0, g1, g2, g3)
    for a in range(parts):
        here = place_ref[a]
        grads_q = []
        for h in range(heads):
            cols = slice(h * HEAD_DIM, (h + 1) * HEAD_DIM)
            q = q_ref[here, 0, :, cols] * scale
            grad = g_refs[0][0, :, cols]
            for i in range(1, parts):
                grad = jnp.where(here == i, g_refs[i][0, :, cols], grad)
            level = l_ref[0, h, a : a + 1, :]
            probs, slopes = [], []
            inner = None
            for b in range(a + 1):
                s = dot_nt(k_ref[place_ref[b], 0, :, cols], q)
                if a == b:
                    s = jnp.where(visible, s, NEGATIVE)
                p = jnp.exp(s - level)
                dp = dot_nt(v_ref[place_ref[b], 0, :, cols], grad)
                term = jnp.sum(p * dp, axis=0, keepdims=True)
                inner = term if inner is None else inner + term
                probs.append(p)
                slopes.append(dp)
            gq = None
            for b in range(a + 1):
                ds = (probs[b] * (slopes[b] - inner)).astype(BF)
                term = dot_tn(k_ref[place_ref[b], 0, :, cols], ds)
                gq = term if gq is None else gq + term
                gk = dot_nn(ds, q)
                gv = dot_nn(probs[b].astype(BF), grad)
                if a == b:
                    gk_ref[b, :, cols] = gk
                    gv_ref[b, :, cols] = gv
                else:
                    gk_ref[b, :, cols] += gk
                    gv_ref[b, :, cols] += gv
            grads_q.append(gq * scale)
        out_ref[here, 0, :, pl.ds(column, 128)] = jnp.concatenate(grads_q, axis=0).T.astype(BF)
    for b in range(parts):
        here = place_ref[b]
        out_ref[here, 0, :, pl.ds(width + column, 128)] = gk_ref[b].astype(BF)
        out_ref[here, 0, :, pl.ds(2 * width + column, 128)] = gv_ref[b].astype(BF)


def self_backward(place, triple, grads, levels, width):
    parts, clips, rows, _ = triple.shape
    groups = width // 128
    block = (parts, 1, rows, 128)
    grad_spec = pl.BlockSpec((1, rows, 128), lambda i, j, p: (i, 0, j))
    return pl.pallas_call(
        self_backward_kernel,
        out_shape=jax.ShapeDtypeStruct((parts, clips, rows, 3 * width), BF),
        grid_spec=pltpu.PrefetchScalarGridSpec(
            num_scalar_prefetch=1,
            grid=(clips, groups),
            in_specs=[
                pl.BlockSpec(block, lambda i, j, p: (0, i, 0, j)),
                pl.BlockSpec(block, lambda i, j, p: (0, i, 0, groups + j)),
                pl.BlockSpec(block, lambda i, j, p: (0, i, 0, 2 * groups + j)),
                grad_spec,
                grad_spec,
                grad_spec,
                grad_spec,
                pl.BlockSpec((1, 2, parts, rows), lambda i, j, p: (i, j, 0, 0)),
            ],
            out_specs=pl.BlockSpec((parts, 1, rows, 3 * width), lambda i, j, p: (0, i, 0, 0)),
            scratch_shapes=[
                pltpu.VMEM((parts, rows, 128), F32),
                pltpu.VMEM((parts, rows, 128), F32),
            ],
        ),
        compiler_params=pltpu.CompilerParams(vmem_limit_bytes=48 << 20),
        cost_estimate=pl.CostEstimate(
            flops=clips * width * rows * rows * 10 * 10,
            bytes_accessed=clips * rows * parts * width * 14,
            transcendentals=clips * (width // HEAD_DIM) * rows * rows * 10,
        ),
        name="self_backward",
    )(place, triple, triple, triple, *grads, levels)


def cross_forward_kernel(q_ref, k_ref, v_ref, o_ref):
    width = q_ref.shape[2]
    k_all = k_ref[0, :, 0].reshape(-1, width)
    v_all = v_ref[0, :, 0].reshape(-1, width)
    for pair in range(width // 128):
        mixed = []
        for h in (2 * pair, 2 * pair + 1):
            cols = slice(h * HEAD_DIM, (h + 1) * HEAD_DIM)
            s = dot_nt(k_all[:, cols], q_ref[0, :, cols] * (HEAD_DIM**-0.5))
            e = jnp.exp(s - jnp.max(s, axis=0, keepdims=True))
            p = e * (1.0 / jnp.sum(e, axis=0, keepdims=True))
            mixed.append(dot_tn(v_all[:, cols], p.astype(BF)))
        o_ref[0, :, pair * 128 : (pair + 1) * 128] = jnp.concatenate(mixed, axis=0).T.astype(BF)


def cross_forward(query, text_kv):
    clips, rows, width = query.shape
    _, parts, _, tokens, _ = text_kv.shape
    step = 512
    groups = width // step
    return pl.pallas_call(
        cross_forward_kernel,
        out_shape=jax.ShapeDtypeStruct(query.shape, BF),
        grid=(clips, groups),
        in_specs=[
            pl.BlockSpec((1, rows, step), lambda i, j: (i, 0, j)),
            pl.BlockSpec((1, parts, 1, tokens, step), lambda i, j: (0, 0, i, 0, j)),
            pl.BlockSpec((1, parts, 1, tokens, step), lambda i, j: (1, 0, i, 0, j)),
        ],
        out_specs=pl.BlockSpec((1, rows, step), lambda i, j: (i, 0, j)),
        cost_estimate=pl.CostEstimate(
            flops=clips * rows * width * parts * tokens * 4,
            bytes_accessed=clips * rows * width * 4,
            transcendentals=clips * rows * parts * tokens * (width // HEAD_DIM),
        ),
        name="cross_forward",
    )(query, text_kv, text_kv)


def cross_backward_kernel(q_ref, k_ref, v_ref, g_ref, gq_ref, gk_ref, gv_ref):
    width = q_ref.shape[2]
    _, parts, _, tokens, _ = k_ref.shape
    scale = HEAD_DIM**-0.5
    k_all = k_ref[0, :, 0].reshape(-1, width)
    v_all = v_ref[0, :, 0].reshape(-1, width)
    for pair in range(width // 128):
        rows_q, rows_k, rows_v = [], [], []
        for h in (2 * pair, 2 * pair + 1):
            cols = slice(h * HEAD_DIM, (h + 1) * HEAD_DIM)
            q = q_ref[0, :, cols] * scale
            grad = g_ref[0, :, cols]
            s = dot_nt(k_all[:, cols], q)
            e = jnp.exp(s - jnp.max(s, axis=0, keepdims=True))
            p = e * (1.0 / jnp.sum(e, axis=0, keepdims=True))
            dp = dot_nt(v_all[:, cols], grad)
            inner = jnp.sum(p * dp, axis=0, keepdims=True)
            ds = (p * (dp - inner)).astype(BF)
            rows_q.append(dot_tn(k_all[:, cols], ds) * scale)
            rows_k.append(dot_nn(ds, q))
            rows_v.append(dot_nn(p.astype(BF), grad))
        span = slice(pair * 128, (pair + 1) * 128)
        gq_ref[0, :, span] = jnp.concatenate(rows_q, axis=0).T.astype(BF)
        gk_ref[:, 0, :, span] = jnp.concatenate(rows_k, axis=1).reshape(parts, tokens, 128)
        gv_ref[:, 0, :, span] = jnp.concatenate(rows_v, axis=1).reshape(parts, tokens, 128)


def cross_backward(query, text_kv, grads):
    clips, rows, width = query.shape
    _, parts, _, tokens, _ = text_kv.shape
    step = 512
    groups = width // step
    row_spec = pl.BlockSpec((1, rows, step), lambda i, j: (i, 0, j))
    text_block = (parts, 1, tokens, step)
    return pl.pallas_call(
        cross_backward_kernel,
        out_shape=(
            jax.ShapeDtypeStruct(query.shape, BF),
            jax.ShapeDtypeStruct((parts, clips, tokens, width), F32),
            jax.ShapeDtypeStruct((parts, clips, tokens, width), F32),
        ),
        grid=(clips, groups),
        in_specs=[
            row_spec,
            pl.BlockSpec((1,) + text_block, lambda i, j: (0, 0, i, 0, j)),
            pl.BlockSpec((1,) + text_block, lambda i, j: (1, 0, i, 0, j)),
            row_spec,
        ],
        out_specs=[
            row_spec,
            pl.BlockSpec(text_block, lambda i, j: (0, i, 0, j)),
            pl.BlockSpec(text_block, lambda i, j: (0, i, 0, j)),
        ],
        cost_estimate=pl.CostEstimate(
            flops=clips * rows * width * parts * tokens * 10,
            bytes_accessed=clips * rows * width * 6,
            transcendentals=clips * rows * parts * tokens * (width // HEAD_DIM),
        ),
        name="cross_backward",
    )(query, text_kv, text_kv, grads)


def place_kernel(count, axis, starts_ref, *refs):
    pieces, out_ref, sems = refs[:count], refs[count], refs[count + 1]
    copies = []
    for i in range(count):
        size = pieces[i].shape[axis]
        where = [slice(None)] * len(out_ref.shape)
        where[axis] = pl.ds(pl.multiple_of(starts_ref[i] * size, size), size)
        copies.append(pltpu.make_async_copy(pieces[i], out_ref.at[tuple(where)], sems.at[i]))
    for copy in copies:
        copy.start()
    for copy in copies:
        copy.wait()


def place_pieces(pieces, starts, axis):
    shape = list(pieces[0].shape)
    shape[axis] *= len(pieces)
    any_spec = pl.BlockSpec(memory_space=pl.ANY)
    size = pieces[0].size * len(pieces) * pieces[0].dtype.itemsize
    return pl.pallas_call(
        functools.partial(place_kernel, len(pieces), axis),
        out_shape=jax.ShapeDtypeStruct(tuple(shape), pieces[0].dtype),
        in_specs=[pl.BlockSpec(memory_space=pltpu.SMEM)]
        + [pl.BlockSpec(memory_space=pltpu.VMEM)] * len(pieces),
        out_specs=any_spec,
        scratch_shapes=[pltpu.SemaphoreType.DMA((len(pieces),))],
        compiler_params=pltpu.CompilerParams(vmem_limit_bytes=2 * size + (4 << 20)),
        cost_estimate=pl.CostEstimate(flops=0, bytes_accessed=2 * size, transcendentals=0),
        name="place_pieces",
    )(jnp.stack([jnp.asarray(s, jnp.int32) for s in starts]), *pieces)


class Group:
    def __init__(self, count):
        self.count = count
        self.line = count // 2
        self.dp = lax.axis_index("dp")
        self.seq = lax.axis_index("seq")
        self.a = self.dp // 2
        self.b = self.dp % 2
        self.direct = self.line <= 4

    def core(self, value):
        return lax.ppermute(value, "seq", [(i, i ^ 1) for i in range(4)])

    def across(self, value):
        return lax.ppermute(value, "seq", [(i, i ^ 2) for i in range(4)])

    def side(self, value):
        return lax.ppermute(value, "dp", [(i, i ^ 1) for i in range(self.count)])

    def turn(self, value, step):
        pairs = [(i, ((i // 2 - step) % self.line) * 2 + i % 2) for i in range(self.count)]
        return lax.ppermute(value, "dp", pairs)

    def gather_seq(self, value):
        over = self.across(value)
        near = self.core(value)
        return [value, over, self.core(over), near]

    def swap_seq(self, sends):
        near = self.core(sends[3])
        over = self.across(jnp.stack([sends[1], sends[2]]))
        return [sends[0], over[0], self.core(over[1]), near]

    def sum_seq(self, own, over, far):
        got = self.core(far)
        half = got.shape[0] // 2
        crossed = self.across((over + got[:half].astype(F32)).astype(BF))
        return own + got[half:].astype(F32) + crossed.astype(F32)

    def gather_dp(self, value, gate=None):
        if gate is not None:
            value = after(value, gate)
        if not self.direct:
            whole = lax.all_gather(value, "dp", axis=0, tiled=True)
            return whole, whole
        turned = [value] + [self.turn(value, r) for r in range(1, self.line)]
        sided = [self.side(t) for t in turned]
        starts = [((self.a + r) % self.line) * 2 + self.b for r in range(self.line)]
        others = [((self.a + r) % self.line) * 2 + 1 - self.b for r in range(self.line)]
        return place_pieces(turned + sided, starts + others, 0), turned[-1]

    def sum_dp(self, value):
        rows = value.shape[0] // self.count
        if not self.direct:
            return lax.psum_scatter(value, "dp", scatter_dimension=0, tiled=True).astype(F32)
        cut = value.reshape(self.line, 2, rows, -1)
        away = lax.dynamic_index_in_dim(cut, 1 - self.b, axis=1, keepdims=False)
        got = self.side(away)

        def added(at):
            mine = lax.dynamic_slice(cut, (at, self.b, 0, 0), (1, 1) + cut.shape[2:])[0, 0]
            return mine.astype(F32) + lax.dynamic_index_in_dim(got, at, axis=0, keepdims=False).astype(F32)

        total = added(self.a)
        for r in range(1, self.line):
            total = total + self.turn(added((self.a - r) % self.line).astype(BF), r).astype(F32)
        return total

    def sum_all_small(self, value):
        value = value + self.core(value)
        value = value + self.across(value)
        if not self.direct:
            return lax.psum(value, "dp")
        value = value + self.side(value)
        return functools.reduce(jnp.add, [self.turn(value, r) for r in range(1, self.line)], value)

    def gather_small(self, value):
        if not self.direct:
            return lax.all_gather(value, "dp", axis=1, tiled=True)
        whole = jnp.zeros((value.shape[0], value.shape[1] * self.count), F32)
        whole = lax.dynamic_update_slice(whole, value.astype(F32), (0, self.dp * value.shape[1]))
        whole = whole + self.side(whole)
        return functools.reduce(jnp.add, [self.turn(whole, r) for r in range(1, self.line)], whole)


def normalized(values):
    center = jnp.mean(values, axis=-1, keepdims=True)
    centered = values - center
    spread = jnp.mean(centered * centered, axis=-1, keepdims=True)
    scale = lax.rsqrt(spread + EPSILON)
    return centered * scale, scale


def norm_input_grad(upstream, gain, xhat, scale):
    weighted = upstream * gain
    first = jnp.mean(weighted, axis=-1, keepdims=True)
    second = jnp.mean(weighted * xhat, axis=-1, keepdims=True)
    return scale * (weighted - first - xhat * second)


def gelu_and_slope(v):
    phi = 0.5 * lax.erfc(-v * (0.5**0.5))
    density = jnp.exp(-0.5 * v * v) * (2.0 * jnp.pi) ** -0.5
    return v * phi, phi + v * density


def local(
    count,
    frames,
    text,
    cotangent,
    norm_gains,
    norm_biases,
    qkv_weight,
    self_out,
    cross_query,
    cross_kv,
    cross_out,
    up_weight,
    down_weight,
):
    g = Group(count)
    clips, rows, width = frames.shape
    tokens = text.shape[1]
    part = width // 4
    held = width // count
    ff = up_weight.shape[1]
    ff_rows = down_weight.shape[0] // 4
    ff_part = ff // 4
    local_rows = clips * rows
    seq = g.seq
    place = jnp.stack([jnp.asarray(PLACE, jnp.int32)[a ^ seq] for a in range(4)])
    orders = [seq ^ r for r in REL]

    frames_in = frames.reshape(local_rows, width)
    cot_in = cotangent.reshape(local_rows, width)
    text_in = text.reshape(clips * tokens, width)
    frames_all = jnp.concatenate(g.gather_seq(frames_in), axis=0)
    text_all = place_pieces(g.gather_seq(text_in), orders, 0)
    cot_all = jnp.concatenate(g.gather_seq(cot_in), axis=0)

    norms = g.gather_small(jnp.concatenate([norm_gains, norm_biases], axis=0)).astype(F32)
    gains, biases = norms[:3], norms[3:]

    def columns(weight, outer, inner):
        cut = weight.reshape(weight.shape[0], outer, 4, inner)
        return lax.dynamic_index_in_dim(cut, seq, axis=2, keepdims=False).reshape(weight.shape[0], outer * inner)

    def own_rows(weight):
        size = weight.shape[0] // 4
        return lax.dynamic_slice_in_dim(weight, seq * size, size, axis=0)

    w_qkv, gate = g.gather_dp(columns(qkv_weight, 3, part))

    def whole(weight, gate):
        quarter, gate = g.gather_dp(own_rows(weight), gate)
        size = weight.shape[0] // 4
        pieces = g.gather_seq(quarter.reshape(count, 1, size, width))
        return place_pieces(pieces, orders, 1).reshape(width, width), gate

    w_self, gate = whole(self_out, gate)
    w_query, gate = whole(cross_query, gate)
    w_pair, gate = g.gather_dp(columns(cross_kv, 2, part), gate)
    w_cross, gate = whole(cross_out, gate)
    w_up, gate = g.gather_dp(columns(up_weight, count, ff_rows), gate)
    w_down, gate = g.gather_dp(own_rows(down_weight), gate)

    hat_all, _ = normalized(frames_all.astype(F32))
    first_low = (hat_all * gains[0] + biases[0]).astype(BF)
    triple = dot_nn(first_low, w_qkv).astype(BF).reshape(4, clips, rows, 3 * part)
    heads_out, levels = self_forward(place, triple, part)
    heads_rows = heads_out.reshape(4, local_rows, part)
    self_mix = place_pieces(g.swap_seq([heads_rows[i] for i in range(4)]), orders, 1)

    pair_part = dot_nn(text_all, w_pair).astype(BF).reshape(4 * clips * tokens, 2, part).swapaxes(0, 1)
    pair_all = place_pieces(g.gather_seq(pair_part), orders, 2).reshape(2, 4, clips, tokens, width)

    residual = frames_in.astype(F32)
    first_sum = residual + dot_nn(self_mix, w_self)
    hat_two, scale_two = normalized(first_sum)
    second_low = (hat_two * gains[1] + biases[1]).astype(BF)
    cross_q = dot_nn(second_low, w_query).astype(BF).reshape(clips, rows, width)
    cross_mix = cross_forward(cross_q, pair_all).reshape(local_rows, width)
    second_sum = first_sum + dot_nn(cross_mix, w_cross)
    hat_three, scale_three = normalized(second_sum)
    third_own = (hat_three * gains[2] + biases[2]).astype(BF)
    third_low = jnp.concatenate(g.gather_seq(third_own), axis=0)

    active, slope = gelu_and_slope(dot_nn(third_low, w_up))
    active_low = active.astype(BF)
    hidden_low = (dot_nt(cot_all, w_down) * slope).astype(BF)

    def summed(product_of, left):
        far = product_of(left[2 * local_rows :]).astype(BF)
        over = product_of(left[local_rows : 2 * local_rows])
        own = product_of(left[:local_rows])
        return g.sum_seq(own, over, far)

    third_up = summed(lambda left: dot_nt(left, w_up), hidden_low)
    block_output = (second_sum + summed(lambda left: dot_nn(left, w_down), active_low)).astype(BF)
    up_shard = g.sum_dp(dot_tn(third_low, hidden_low).astype(BF))
    down_shard = g.sum_dp(dot_tn(active_low, cot_all).astype(BF))

    def norm_sums(upstream, xhat):
        return jnp.sum(upstream * xhat, axis=0), jnp.sum(upstream, axis=0)

    second_grad = cot_in.astype(F32) + norm_input_grad(third_up, gains[2], hat_three, scale_three)
    gain_third, bias_third = norm_sums(third_up, hat_three)

    def sum_rows(value):
        size = held // 4
        cut = value.reshape(count, 4, size, width)

        def piece(i):
            return lax.dynamic_index_in_dim(cut, orders[i], axis=1, keepdims=False)

        got = g.core(jnp.stack([piece(2), piece(3)]))
        over = (piece(1).astype(F32) + got[0].astype(F32)).astype(BF)
        own = piece(0).astype(F32) + got[1].astype(F32) + g.across(over).astype(F32)
        return g.sum_dp(own.astype(BF).reshape(count * size, width))

    second_in = second_grad.astype(BF)
    mix_grad = dot_nt(second_in, w_cross).astype(BF).reshape(clips, rows, width)
    query_back, key_sums, value_sums = cross_backward(cross_q, pair_all, mix_grad)
    query_back = query_back.reshape(local_rows, width)
    cross_shard = sum_rows(dot_tn(cross_mix, second_in).astype(BF))
    query_shard = sum_rows(dot_tn(second_low, query_back).astype(BF))

    pair_sums = jnp.stack([key_sums, value_sums], axis=3).reshape(4 * clips * tokens, 2, 4, part)

    def pair_piece(i):
        return lax.dynamic_index_in_dim(pair_sums, orders[i], axis=2, keepdims=False).reshape(-1, 2 * part)

    pair_back = g.sum_seq(
        pair_piece(0), pair_piece(1), jnp.concatenate([pair_piece(2), pair_piece(3)], axis=0).astype(BF)
    ).astype(BF)
    pair_shard = g.sum_dp(dot_tn(text_all, pair_back).astype(BF))
    text_part = dot_nt(pair_back, w_pair).reshape(4, clips * tokens, width)

    def text_piece(i):
        return lax.dynamic_index_in_dim(text_part, orders[i], axis=0, keepdims=False)

    text_grad = g.sum_seq(
        text_piece(0), text_piece(1), jnp.concatenate([text_piece(2), text_piece(3)], axis=0).astype(BF)
    ).reshape(clips, tokens, width)

    second_up = dot_nt(query_back, w_query)
    first_grad = second_grad + norm_input_grad(second_up, gains[1], hat_two, scale_two)
    gain_second, bias_second = norm_sums(second_up, hat_two)

    first_in = first_grad.astype(BF)
    self_grad = dot_nt(first_in, w_self).astype(BF).reshape(local_rows, 4, part)
    grads = g.swap_seq([lax.dynamic_index_in_dim(self_grad, o, axis=1, keepdims=False) for o in orders])
    self_shard = sum_rows(dot_tn(self_mix, first_in).astype(BF))
    triple_back = self_backward(
        place, triple, [p.reshape(clips, rows, part) for p in grads], levels, part
    ).reshape(4 * local_rows, 3 * part)

    first_over = lambda left: dot_nt(left, w_qkv)
    far = first_over(triple_back[2 * local_rows :])
    over = first_over(triple_back[local_rows : 2 * local_rows])
    own = first_over(triple_back[:local_rows])
    first_up = g.sum_seq(own, over, far.astype(BF))
    qkv_shard = g.sum_dp(dot_tn(first_low, triple_back).astype(BF))
    hat_one, scale_one = normalized(residual)
    frame_grad = first_grad + norm_input_grad(first_up, gains[0], hat_one, scale_one)

    gain_first = (
        jnp.sum(own * hat_all[:local_rows], axis=0)
        + jnp.sum(over * hat_all[local_rows : 2 * local_rows], axis=0)
        + jnp.sum(far * hat_all[2 * local_rows :], axis=0)
    )
    bias_first = jnp.sum(own, axis=0) + jnp.sum(over, axis=0) + jnp.sum(far, axis=0)
    norm_all = g.sum_all_small(
        jnp.stack([gain_first, gain_second, gain_third, bias_first, bias_second, bias_third])
    )
    small = width // (4 * count)
    norm_shard = lax.dynamic_slice_in_dim(norm_all, (g.dp * 4 + seq) * small, small, axis=1)

    def regroup(value, outer, inner):
        size = value.shape[0] // 4
        low = value.astype(BF)
        sends = [lax.dynamic_slice_in_dim(low, o * size, size, axis=0) for o in orders]
        out = jnp.zeros((size, outer, 4, inner), F32)
        for got, order in zip(g.swap_seq(sends), orders):
            out = lax.dynamic_update_slice(
                out, got.astype(F32).reshape(size, outer, 1, inner), (0, 0, order, 0)
            )
        return out.reshape(size, outer * 4 * inner)

    return (
        block_output.reshape(clips, rows, width),
        frame_grad.reshape(clips, rows, width),
        text_grad,
        norm_shard[:3],
        norm_shard[3:],
        regroup(qkv_shard, 3, part),
        self_shard,
        query_shard,
        regroup(pair_shard, 2, part),
        cross_shard,
        regroup(up_shard, count, ff_rows),
        down_shard,
    )


def solution(mesh):
    rows = P("dp", "seq", None)
    both = P(("dp", "seq"), None)
    return jax.shard_map(
        functools.partial(local, mesh.shape["dp"]),
        mesh=mesh,
        in_specs=(rows, rows, rows, P(None, "dp"), P(None, "dp")) + (P("dp", None),) * 7,
        out_specs=(rows, rows, rows, P(None, ("dp", "seq")), P(None, ("dp", "seq"))) + (both,) * 7,
        check_vma=False,
    )
```

```python
import functools

import jax
import jax.numpy as jnp
from jax import lax
from jax.experimental import pallas as pl
from jax.experimental.pallas import tpu as pltpu
from jax.sharding import PartitionSpec as P

HEAD_DIM = 64
EPSILON = 1e-05
NEGATIVE = -1e30
BF = jnp.bfloat16
F32 = jnp.float32

REL = (0, 2, 3, 1)
PLACE = (0, 3, 1, 2)


def dot_nn(a, b):
    return lax.dot_general(a, b, (((1,), (0,)), ((), ())), preferred_element_type=F32)


def dot_nt(a, b):
    return lax.dot_general(a, b, (((1,), (1,)), ((), ())), preferred_element_type=F32)


def dot_tn(a, b):
    return lax.dot_general(a, b, (((0,), (0,)), ((), ())), preferred_element_type=F32)


def after(value, *others):
    return lax.optimization_barrier((value,) + others)[0]


def self_forward_kernel(place_ref, q_ref, k_ref, v_ref, o_ref, l_ref):
    parts, rows = q_ref.shape[0], q_ref.shape[2]
    heads = q_ref.shape[3] // HEAD_DIM
    keys_at = lax.broadcasted_iota(jnp.int32, (rows, rows), 0)
    rows_at = lax.broadcasted_iota(jnp.int32, (rows, rows), 1)
    visible = keys_at <= rows_at
    for a in range(parts):
        here = place_ref[a]
        mixed = []
        for h in range(heads):
            cols = slice(h * HEAD_DIM, (h + 1) * HEAD_DIM)
            q = q_ref[here, 0, :, cols] * (HEAD_DIM**-0.5)
            scores = []
            for b in range(a + 1):
                s = dot_nt(k_ref[place_ref[b], 0, :, cols], q)
                if a == b:
                    s = jnp.where(visible, s, NEGATIVE)
                scores.append(s)
            top = functools.reduce(jnp.maximum, [jnp.max(s, axis=0, keepdims=True) for s in scores])
            raised = [jnp.exp(s - top) for s in scores]
            total = functools.reduce(jnp.add, [jnp.sum(e, axis=0, keepdims=True) for e in raised])
            share = 1.0 / total
            out = None
            for b in range(a + 1):
                p = (raised[b] * share).astype(BF)
                term = dot_tn(v_ref[place_ref[b], 0, :, cols], p)
                out = term if out is None else out + term
            mixed.append(out)
            l_ref[0, h, a : a + 1, :] = top + jnp.log(total)
        o_ref[here, 0] = jnp.concatenate(mixed, axis=0).T.astype(BF)


def self_forward(place, triple, width):
    parts, clips, rows, _ = triple.shape
    groups = width // 128
    block = (parts, 1, rows, 128)
    return pl.pallas_call(
        self_forward_kernel,
        out_shape=(
            jax.ShapeDtypeStruct((parts, clips, rows, width), BF),
            jax.ShapeDtypeStruct((clips, width // HEAD_DIM, parts, rows), F32),
        ),
        grid_spec=pltpu.PrefetchScalarGridSpec(
            num_scalar_prefetch=1,
            grid=(clips, groups),
            in_specs=[
                pl.BlockSpec(block, lambda i, j, p: (0, i, 0, j)),
                pl.BlockSpec(block, lambda i, j, p: (0, i, 0, groups + j)),
                pl.BlockSpec(block, lambda i, j, p: (0, i, 0, 2 * groups + j)),
            ],
            out_specs=[
                pl.BlockSpec(block, lambda i, j, p: (0, i, 0, j)),
                pl.BlockSpec((1, 2, parts, rows), lambda i, j, p: (i, j, 0, 0)),
            ],
        ),
        compiler_params=pltpu.CompilerParams(vmem_limit_bytes=40 << 20),
        cost_estimate=pl.CostEstimate(
            flops=clips * width * rows * rows * 10 * 4,
            bytes_accessed=clips * rows * parts * width * 8,
            transcendentals=clips * (width // HEAD_DIM) * rows * rows * 10,
        ),
        name="self_forward",
    )(place, triple, triple, triple)


def self_backward_kernel(place_ref, q_ref, k_ref, v_ref, g_ref, l_ref, out_ref, gk_ref, gv_ref):
    parts, rows = q_ref.shape[0], q_ref.shape[2]
    heads = q_ref.shape[3] // HEAD_DIM
    width = out_ref.shape[3] // 3
    scale = HEAD_DIM**-0.5
    column = pl.multiple_of(pl.program_id(1) * 128, 128)
    keys_at = lax.broadcasted_iota(jnp.int32, (rows, rows), 0)
    rows_at = lax.broadcasted_iota(jnp.int32, (rows, rows), 1)
    visible = keys_at <= rows_at
    for a in range(parts):
        here = place_ref[a]
        grads_q = []
        for h in range(heads):
            cols = slice(h * HEAD_DIM, (h + 1) * HEAD_DIM)
            q = q_ref[here, 0, :, cols] * scale
            grad = g_ref[here, 0, :, cols]
            level = l_ref[0, h, a : a + 1, :]
            probs, slopes = [], []
            inner = None
            for b in range(a + 1):
                s = dot_nt(k_ref[place_ref[b], 0, :, cols], q)
                if a == b:
                    s = jnp.where(visible, s, NEGATIVE)
                p = jnp.exp(s - level)
                dp = dot_nt(v_ref[place_ref[b], 0, :, cols], grad)
                term = jnp.sum(p * dp, axis=0, keepdims=True)
                inner = term if inner is None else inner + term
                probs.append(p)
                slopes.append(dp)
            gq = None
            for b in range(a + 1):
                ds = (probs[b] * (slopes[b] - inner)).astype(BF)
                term = dot_tn(k_ref[place_ref[b], 0, :, cols], ds)
                gq = term if gq is None else gq + term
                gk = dot_nn(ds, q)
                gv = dot_nn(probs[b].astype(BF), grad)
                if a == b:
                    gk_ref[b, :, cols] = gk
                    gv_ref[b, :, cols] = gv
                else:
                    gk_ref[b, :, cols] += gk
                    gv_ref[b, :, cols] += gv
            grads_q.append(gq * scale)
        out_ref[here, 0, :, pl.ds(column, 128)] = jnp.concatenate(grads_q, axis=0).T.astype(BF)
    for b in range(parts):
        here = place_ref[b]
        out_ref[here, 0, :, pl.ds(width + column, 128)] = gk_ref[b].astype(BF)
        out_ref[here, 0, :, pl.ds(2 * width + column, 128)] = gv_ref[b].astype(BF)


def self_backward(place, triple, grads, levels, width):
    parts, clips, rows, _ = triple.shape
    groups = width // 128
    block = (parts, 1, rows, 128)
    return pl.pallas_call(
        self_backward_kernel,
        out_shape=jax.ShapeDtypeStruct((parts, clips, rows, 3 * width), BF),
        grid_spec=pltpu.PrefetchScalarGridSpec(
            num_scalar_prefetch=1,
            grid=(clips, groups),
            in_specs=[
                pl.BlockSpec(block, lambda i, j, p: (0, i, 0, j)),
                pl.BlockSpec(block, lambda i, j, p: (0, i, 0, groups + j)),
                pl.BlockSpec(block, lambda i, j, p: (0, i, 0, 2 * groups + j)),
                pl.BlockSpec(block, lambda i, j, p: (0, i, 0, j)),
                pl.BlockSpec((1, 2, parts, rows), lambda i, j, p: (i, j, 0, 0)),
            ],
            out_specs=pl.BlockSpec((parts, 1, rows, 3 * width), lambda i, j, p: (0, i, 0, 0)),
            scratch_shapes=[
                pltpu.VMEM((parts, rows, 128), F32),
                pltpu.VMEM((parts, rows, 128), F32),
            ],
        ),
        compiler_params=pltpu.CompilerParams(vmem_limit_bytes=48 << 20),
        cost_estimate=pl.CostEstimate(
            flops=clips * width * rows * rows * 10 * 10,
            bytes_accessed=clips * rows * parts * width * 14,
            transcendentals=clips * (width // HEAD_DIM) * rows * rows * 10,
        ),
        name="self_backward",
    )(place, triple, triple, triple, grads, levels)


def cross_forward_kernel(q_ref, k_ref, v_ref, o_ref):
    width = q_ref.shape[2]
    k_all = k_ref[0, :, 0].reshape(-1, width)
    v_all = v_ref[0, :, 0].reshape(-1, width)
    for pair in range(width // 128):
        mixed = []
        for h in (2 * pair, 2 * pair + 1):
            cols = slice(h * HEAD_DIM, (h + 1) * HEAD_DIM)
            s = dot_nt(k_all[:, cols], q_ref[0, :, cols] * (HEAD_DIM**-0.5))
            e = jnp.exp(s - jnp.max(s, axis=0, keepdims=True))
            p = e * (1.0 / jnp.sum(e, axis=0, keepdims=True))
            mixed.append(dot_tn(v_all[:, cols], p.astype(BF)))
        o_ref[0, :, pair * 128 : (pair + 1) * 128] = jnp.concatenate(mixed, axis=0).T.astype(BF)


def cross_forward(query, text_kv):
    clips, rows, width = query.shape
    _, parts, _, tokens, _ = text_kv.shape
    step = 512
    groups = width // step
    return pl.pallas_call(
        cross_forward_kernel,
        out_shape=jax.ShapeDtypeStruct(query.shape, BF),
        grid=(clips, groups),
        in_specs=[
            pl.BlockSpec((1, rows, step), lambda i, j: (i, 0, j)),
            pl.BlockSpec((1, parts, 1, tokens, step), lambda i, j: (0, 0, i, 0, j)),
            pl.BlockSpec((1, parts, 1, tokens, step), lambda i, j: (1, 0, i, 0, j)),
        ],
        out_specs=pl.BlockSpec((1, rows, step), lambda i, j: (i, 0, j)),
        cost_estimate=pl.CostEstimate(
            flops=clips * rows * width * parts * tokens * 4,
            bytes_accessed=clips * rows * width * 4,
            transcendentals=clips * rows * parts * tokens * (width // HEAD_DIM),
        ),
        name="cross_forward",
    )(query, text_kv, text_kv)


def cross_backward_kernel(q_ref, k_ref, v_ref, g_ref, gq_ref, gk_ref, gv_ref):
    width = q_ref.shape[2]
    _, parts, _, tokens, _ = k_ref.shape
    scale = HEAD_DIM**-0.5
    k_all = k_ref[0, :, 0].reshape(-1, width)
    v_all = v_ref[0, :, 0].reshape(-1, width)
    for pair in range(width // 128):
        rows_q, rows_k, rows_v = [], [], []
        for h in (2 * pair, 2 * pair + 1):
            cols = slice(h * HEAD_DIM, (h + 1) * HEAD_DIM)
            q = q_ref[0, :, cols] * scale
            grad = g_ref[0, :, cols]
            s = dot_nt(k_all[:, cols], q)
            e = jnp.exp(s - jnp.max(s, axis=0, keepdims=True))
            p = e * (1.0 / jnp.sum(e, axis=0, keepdims=True))
            dp = dot_nt(v_all[:, cols], grad)
            inner = jnp.sum(p * dp, axis=0, keepdims=True)
            ds = (p * (dp - inner)).astype(BF)
            rows_q.append(dot_tn(k_all[:, cols], ds) * scale)
            rows_k.append(dot_nn(ds, q))
            rows_v.append(dot_nn(p.astype(BF), grad))
        span = slice(pair * 128, (pair + 1) * 128)
        gq_ref[0, :, span] = jnp.concatenate(rows_q, axis=0).T.astype(BF)
        gk_ref[:, 0, :, span] = jnp.concatenate(rows_k, axis=1).reshape(parts, tokens, 128)
        gv_ref[:, 0, :, span] = jnp.concatenate(rows_v, axis=1).reshape(parts, tokens, 128)


def cross_backward(query, text_kv, grads):
    clips, rows, width = query.shape
    _, parts, _, tokens, _ = text_kv.shape
    step = 512
    groups = width // step
    row_spec = pl.BlockSpec((1, rows, step), lambda i, j: (i, 0, j))
    text_block = (parts, 1, tokens, step)
    return pl.pallas_call(
        cross_backward_kernel,
        out_shape=(
            jax.ShapeDtypeStruct(query.shape, BF),
            jax.ShapeDtypeStruct((parts, clips, tokens, width), F32),
            jax.ShapeDtypeStruct((parts, clips, tokens, width), F32),
        ),
        grid=(clips, groups),
        in_specs=[
            row_spec,
            pl.BlockSpec((1,) + text_block, lambda i, j: (0, 0, i, 0, j)),
            pl.BlockSpec((1,) + text_block, lambda i, j: (1, 0, i, 0, j)),
            row_spec,
        ],
        out_specs=[
            row_spec,
            pl.BlockSpec(text_block, lambda i, j: (0, i, 0, j)),
            pl.BlockSpec(text_block, lambda i, j: (0, i, 0, j)),
        ],
        cost_estimate=pl.CostEstimate(
            flops=clips * rows * width * parts * tokens * 10,
            bytes_accessed=clips * rows * width * 6,
            transcendentals=clips * rows * parts * tokens * (width // HEAD_DIM),
        ),
        name="cross_backward",
    )(query, text_kv, text_kv, grads)


def gelu_and_slope(v):
    phi = 0.5 + 0.5 * lax.erf(v * (0.5**0.5))
    density = jnp.exp(-0.5 * v * v) * (2.0 * jnp.pi) ** -0.5
    return v * phi, phi + v * density


def middle_kernel(x_ref, c_ref, up_ref, down_ref, act_ref, grad_ref):
    active, slope = gelu_and_slope(dot_nn(x_ref[...], up_ref[...]))
    act_ref[...] = active.astype(BF)
    grad_ref[...] = (dot_nt(c_ref[...], down_ref[...]) * slope).astype(BF)


def middle(normed, cotangent, up, down):
    rows, width = normed.shape
    hidden = up.shape[1]
    tile_r, tile_h = min(512, rows), min(512, hidden)
    row_spec = pl.BlockSpec((tile_r, width), lambda j, i: (i, 0))
    out_spec = pl.BlockSpec((tile_r, tile_h), lambda j, i: (i, j))
    shape = jax.ShapeDtypeStruct((rows, hidden), BF)
    return pl.pallas_call(
        middle_kernel,
        out_shape=(shape, shape),
        grid=(hidden // tile_h, rows // tile_r),
        in_specs=[
            row_spec,
            row_spec,
            pl.BlockSpec((width, tile_h), lambda j, i: (0, j)),
            pl.BlockSpec((tile_h, width), lambda j, i: (j, 0)),
        ],
        out_specs=(out_spec, out_spec),
        compiler_params=pltpu.CompilerParams(vmem_limit_bytes=40 << 20),
        cost_estimate=pl.CostEstimate(
            flops=4 * rows * width * hidden,
            bytes_accessed=4 * rows * width * 3 + 4 * width * hidden + 4 * rows * hidden,
            transcendentals=2 * rows * hidden,
        ),
        name="middle",
    )(normed, cotangent, up, down)


def place_kernel(count, axis, starts_ref, *refs):
    pieces, out_ref, sems = refs[:count], refs[count], refs[count + 1]
    copies = []
    for i in range(count):
        size = pieces[i].shape[axis]
        where = [slice(None)] * len(out_ref.shape)
        where[axis] = pl.ds(pl.multiple_of(starts_ref[i] * size, size), size)
        copies.append(pltpu.make_async_copy(pieces[i], out_ref.at[tuple(where)], sems.at[i]))
    for copy in copies:
        copy.start()
    for copy in copies:
        copy.wait()


def place_pieces(pieces, starts, axis):
    shape = list(pieces[0].shape)
    shape[axis] *= len(pieces)
    any_spec = pl.BlockSpec(memory_space=pl.ANY)
    size = pieces[0].size * len(pieces) * pieces[0].dtype.itemsize
    return pl.pallas_call(
        functools.partial(place_kernel, len(pieces), axis),
        out_shape=jax.ShapeDtypeStruct(tuple(shape), pieces[0].dtype),
        in_specs=[pl.BlockSpec(memory_space=pltpu.SMEM)]
        + [pl.BlockSpec(memory_space=pltpu.VMEM)] * len(pieces),
        out_specs=any_spec,
        scratch_shapes=[pltpu.SemaphoreType.DMA((len(pieces),))],
        compiler_params=pltpu.CompilerParams(vmem_limit_bytes=2 * size + (4 << 20)),
        cost_estimate=pl.CostEstimate(flops=0, bytes_accessed=2 * size, transcendentals=0),
        name="place_pieces",
    )(jnp.stack([jnp.asarray(s, jnp.int32) for s in starts]), *pieces)


class Group:
    def __init__(self, count):
        self.count = count
        self.dp = lax.axis_index("dp")
        self.seq = lax.axis_index("seq")
        self.bits = (self.dp // 4, self.dp // 2 % 2, self.dp % 2)
        self.paired = count == 8

    def core(self, value):
        return lax.ppermute(value, "seq", [(i, i ^ 1) for i in range(4)])

    def across(self, value):
        return lax.ppermute(value, "seq", [(i, i ^ 2) for i in range(4)])

    def swap(self, value, bit):
        return lax.ppermute(value, "dp", [(i, i ^ bit) for i in range(self.count)])


    def near_step(self, value):
        if not self.paired:
            return lax.all_gather(value, "dp", axis=0)
        low = self.bits[1]
        return place_pieces([value[None], self.swap(value, 2)[None]], [low, 1 - low], 0)

    def far_step(self, value):
        if not self.paired:
            return value
        high = self.bits[0]
        return place_pieces([value[None], self.swap(value, 4)[None]], [high, 1 - high], 0)

    def side_step(self, value):
        return [value, self.swap(value, 1)] if self.paired else [value]

    def gathered(self, *halves):
        if not self.paired:
            parts = jnp.stack([h[0] for h in halves], axis=1)
            return parts.reshape((-1,) + parts.shape[3:])
        b, n = self.bits[2], len(halves)
        pieces = [h[i][:, :, None] for i in range(2) for h in halves]
        starts = [side * n + i for side in (b, 1 - b) for i in range(n)]
        whole = place_pieces(pieces, starts, 2)
        return whole.reshape((-1,) + whole.shape[4:])


    def halve(self, value, axis, place, bit):
        away = lax.dynamic_index_in_dim(value, 1 - place, axis=axis, keepdims=False)
        kept = lax.dynamic_index_in_dim(value, place, axis=axis, keepdims=False)
        return kept, self.swap(away, bit)

    def add(self, pair):
        return (pair[0].astype(F32) + pair[1].astype(F32)).astype(BF)

    def side_sum(self, value):
        if not self.paired:
            return value.reshape((-1,) + value.shape[2:]), None
        return self.halve(value.reshape((2, 2, 2) + value.shape[1:]), 2, self.bits[2], 1)

    def far_sum(self, pair):
        if not self.paired:
            return pair
        return self.halve(self.add(pair), 0, self.bits[0], 4)

    def near_sum(self, pair):
        if not self.paired:
            return lax.psum_scatter(pair[0], "dp", scatter_dimension=0, tiled=True), None
        return self.halve(self.add(pair), 0, self.bits[1], 2)

    def total(self, pair):
        return self.add(pair) if self.paired else pair[0]

    def sum_all_small(self, value):
        if not self.paired:
            return lax.psum(value, ("dp", "seq"))
        value = value + self.core(value)
        value = value + self.across(value)
        for bit in (1, 2, 4):
            value = value + self.swap(value, bit)
        return value


MESH = pl.DeviceIdType.MESH


def flip(index, bits):
    for bit in (1, 2, 4):
        if bits & bit:
            index = index + bit - 2 * bit * (index // bit % 2)
    return index


class Sender:
    def __init__(self, send, recv):
        self.send, self.recv, self.used = send, recv, 0
        self.dp, self.seq = lax.axis_index("dp"), lax.axis_index("seq")
        self.open = []

    def greet(self, dp_bits, seq_bits):
        barrier = pltpu.get_barrier_semaphore()
        peers = [self.peer(d, 0) for d in dp_bits] + [self.peer(0, s) for s in seq_bits]
        for peer in peers:
            pl.semaphore_signal(barrier, inc=1, device_id=peer, device_id_type=MESH)
        pl.semaphore_wait(barrier, len(peers))

    def peer(self, dp_bits, seq_bits):
        return (flip(self.dp, dp_bits), flip(self.seq, seq_bits))

    def copy(self, src, dst, dp_bits=0, seq_bits=0):
        one = pltpu.make_async_remote_copy(
            src_ref=src,
            dst_ref=dst,
            send_sem=self.send.at[self.used],
            recv_sem=self.recv.at[self.used],
            device_id=self.peer(dp_bits, seq_bits),
            device_id_type=MESH,
        )
        self.used += 1
        one.start()
        self.open.append(one)
        return one


CHUNKS = 3


def opening_kernel(qkv_ref, frames_ref, text_ref, norm_ref, w_ref, fa_ref, ta_ref, na_ref, local_sem, send, recv):
    s = Sender(send, recv)
    dp, seq = s.dp, s.seq
    part = w_ref.shape[2] // 3
    rows = qkv_ref.shape[0] // CHUNKS
    loads = []
    for i in range(3):
        at = pl.ds(pl.multiple_of((4 * i + seq) * part, 128), part)
        loads.append(
            pltpu.make_async_copy(qkv_ref.at[:, at], w_ref.at[dp, :, i * part : (i + 1) * part], local_sem.at[i])
        )
        loads[-1].start()
    s.greet((1, 2, 3, 4, 5, 6, 7), (1, 2))
    over = s.copy(frames_ref, fa_ref.at[1], 0, 2)
    near = s.copy(frames_ref, fa_ref.at[3], 0, 1)
    for one in loads:
        one.wait()

    def along(j):
        cut = pl.ds(j * rows, rows)
        return [s.copy(w_ref.at[dp, cut], w_ref.at[dp, cut], k) for k in (4, 6, 2)]

    line = [along(0)]
    side = [s.copy(w_ref.at[dp], w_ref.at[dp], 1)]
    norms = [s.copy(norm_ref, na_ref.at[dp], k) for k in (1, 2, 3, 4, 5, 6, 7)]
    text_over = s.copy(text_ref, ta_ref.at[seq], 0, 2)
    text_near = s.copy(text_ref, ta_ref.at[seq], 0, 1)
    fa_ref[0] = frames_ref[...]
    ta_ref[seq] = text_ref[...]
    na_ref[dp] = norm_ref[...]
    for j in range(CHUNKS):
        cut = pl.ds(j * rows, rows)
        if j + 1 < CHUNKS:
            for one in line[j]:
                one.wait_send()
            line.append(along(j + 1))
        for k, one in zip((4, 6, 2), line[j]):
            one.wait_recv()
            at = flip(dp, k)
            side.append(s.copy(w_ref.at[at, cut], w_ref.at[at, cut], 1))
    over.wait_recv()
    far = s.copy(fa_ref.at[1], fa_ref.at[2], 0, 1)
    text_over.wait_recv()
    at = flip(seq, 2)
    text_far = s.copy(ta_ref.at[at], ta_ref.at[at], 0, 1)
    for one in side + [near, text_near, far, text_far] + norms:
        one.wait_recv()
    sent = [one for j in range(CHUNKS - 1) for one in line[j]]
    for one in s.open:
        if not any(one is other for other in sent):
            one.wait_send()


def opening(qkv, frames, text, norms):
    vmem = pl.BlockSpec(memory_space=pltpu.VMEM)
    count = 8
    copies = 3 * CHUNKS + 1 + 3 * CHUNKS + 6 + 7
    share = (count, qkv.shape[0], qkv.shape[1] // 4)
    shapes = [share, (4,) + frames.shape, (4,) + text.shape, (count,) + norms.shape]
    return pl.pallas_call(
        opening_kernel,
        out_shape=[jax.ShapeDtypeStruct(sh, v.dtype) for sh, v in zip(shapes, (qkv, frames, text, norms))],
        in_specs=[pl.BlockSpec(memory_space=pl.ANY)] + [vmem] * 3,
        out_specs=[vmem] * 4,
        scratch_shapes=[
            pltpu.SemaphoreType.DMA((3,)),
            pltpu.SemaphoreType.DMA((copies,)),
            pltpu.SemaphoreType.DMA((copies,)),
        ],
        compiler_params=pltpu.CompilerParams(
            collective_id=0, has_side_effects=True, vmem_limit_bytes=32 << 20
        ),
        cost_estimate=pl.CostEstimate(flops=0, bytes_accessed=200 << 20, transcendentals=0),
        name="opening",
    )(qkv, frames, text, norms)


def exchange(kernel, value, shape, number, name, stage=None):
    vmem = pl.BlockSpec(memory_space=pltpu.VMEM)
    copies = 6
    return pl.pallas_call(
        kernel,
        out_shape=jax.ShapeDtypeStruct(shape, value.dtype),
        in_specs=[vmem],
        out_specs=vmem,
        scratch_shapes=([] if stage is None else [pltpu.VMEM(stage, value.dtype)])
        + [pltpu.SemaphoreType.DMA((copies,)), pltpu.SemaphoreType.DMA((copies,))],
        compiler_params=pltpu.CompilerParams(
            collective_id=number, has_side_effects=True, vmem_limit_bytes=24 << 20
        ),
        cost_estimate=pl.CostEstimate(flops=0, bytes_accessed=80 << 20, transcendentals=0),
        name=name,
    )(value)


def rows_to_all_kernel(x_ref, out_ref, send, recv):
    s = Sender(send, recv)
    s.greet((), (1, 2))
    half = x_ref.shape[0] // 2
    cuts = [pl.ds(0, half), pl.ds(half, half)]
    over = [s.copy(x_ref.at[cut], out_ref.at[1, cut], 0, 2) for cut in cuts]
    near = s.copy(x_ref, out_ref.at[3], 0, 1)
    out_ref[0] = x_ref[...]
    far = []
    for one, cut in zip(over, cuts):
        one.wait_recv()
        far.append(s.copy(out_ref.at[1, cut], out_ref.at[2, cut], 0, 1))
    for one in [near] + far:
        one.wait_recv()
    for one in s.open:
        one.wait_send()


def heads_to_rows_kernel(x_ref, out_ref, stage_ref, send, recv):
    s = Sender(send, recv)
    seq = s.seq
    part = x_ref.shape[2]
    s.greet((), (1, 2))

    def at(owner):
        return (slice(None), pl.ds(pl.multiple_of(owner * part, 128), part))

    relayed = s.copy(x_ref.at[2], stage_ref, 0, 2)
    over = s.copy(x_ref.at[1], out_ref.at[at(seq)], 0, 2)
    near = s.copy(x_ref.at[3], out_ref.at[at(seq)], 0, 1)
    out_ref[at(seq)] = x_ref[0]
    relayed.wait_recv()
    far = s.copy(stage_ref, out_ref.at[at(flip(seq, 2))], 0, 1)
    for one in (near, over, far):
        one.wait_recv()
    for one in s.open:
        one.wait_send()


def rows_to_heads_kernel(x_ref, out_ref, stage_ref, send, recv):
    s = Sender(send, recv)
    seq = s.seq
    part = out_ref.shape[2]
    s.greet((), (1, 2))

    def at(owner):
        return (slice(None), pl.ds(pl.multiple_of(owner * part, 128), part))

    relayed = s.copy(x_ref.at[at(flip(seq, 3))], stage_ref, 0, 2)
    over = s.copy(x_ref.at[at(flip(seq, 2))], out_ref.at[1], 0, 2)
    near = s.copy(x_ref.at[at(flip(seq, 1))], out_ref.at[3], 0, 1)
    out_ref[0] = x_ref[at(seq)]
    relayed.wait_recv()
    far = s.copy(stage_ref, out_ref.at[2], 0, 1)
    for one in (near, over, far):
        one.wait_recv()
    for one in s.open:
        one.wait_send()


def by_rows(total, step, body):
    def run(i, carry):
        body(pl.ds(pl.multiple_of(i * step, step), step))
        return carry

    lax.fori_loop(0, total // step, run, 0)


def closing_kernel(
    qkv_ref, pair_ref, grown_ref, far_ref, over_ref, own_ref, norm_ref,
    up_ref, qkv_out, pair_out, grown_out, norm_out,
    far_in, over_send, over_in, norm_seq, norm_mid, norm_dp,
    qkv_side, qkv_sum, qkv_line, qkv_all, qkv_got, pair_side, pair_sum, pair_line, pair_all, pair_got, grown_got,
    send, recv,
):
    s = Sender(send, recv)
    dp, seq = s.dp, s.seq
    order = (4, 6, 2, 0)
    s.greet((1, 2, 3, 4, 5, 6, 7), (1, 2, 3))
    far = [s.copy(far_ref.at[i], far_in.at[i], 0, 1) for i in range(2)]
    weights = (
        (qkv_ref, qkv_side, qkv_sum, qkv_line, qkv_all, qkv_got),
        (pair_ref, pair_side, pair_sum, pair_line, pair_all, pair_got),
    )
    jobs = [(w, i) for w in range(2) for i in range(4)]

    def to_side(job):
        w, i = job
        ref, side = weights[w][0], weights[w][1]
        return s.copy(ref.at[flip(dp, order[i] + 1)], side.at[i], 1)

    started = {job: to_side(job) for job in jobs[:2]}
    norm_copies = [s.copy(norm_ref, norm_seq.at[k - 1], 0, k) for k in (1, 2, 3)]

    def regroup(whole, got):
        size = got.shape[1]
        moves = []
        for k in (2, 3, 1):
            rows = pl.ds(pl.multiple_of(flip(seq, k) * size, size), size)
            moves.append(s.copy(whole.at[rows], got.at[seq], 0, k))
        got[seq] = whole[pl.ds(pl.multiple_of(seq * size, size), size)]
        return moves

    def in_columns(got, out, outer):
        inner = got.shape[2] // outer
        for j in range(outer):
            for k in range(4):
                at = (4 * j + k) * inner
                out[:, at : at + inner] = got[k, :, j * inner : (j + 1) * inner].astype(F32)

    far[0].wait_recv()

    def add_over(cut):
        over_send[cut] = (over_ref[cut] + far_in[0, cut].astype(F32)).astype(BF)

    by_rows(over_ref.shape[0], 64, add_over)
    crossed = s.copy(over_send, over_in, 0, 2)
    for one in norm_copies:
        one.wait_recv()
    norm_mid[...] = norm_ref[...] + norm_seq[0] + norm_seq[1] + norm_seq[2]
    norm_dp_copies = [s.copy(norm_mid, norm_dp.at[k - 1], k) for k in range(1, 8)]
    moved = [regroup(grown_ref, grown_got)]
    line_copies = {}

    def finish(w):
        ref, side, total, line, whole, got = weights[w]
        for i in range(3):
            line_copies[(w, i)].wait_recv()

        def add(cut):
            value = total[3, cut].astype(F32)
            for i in range(3):
                value = value + line[i, cut].astype(F32)
            whole[cut] = value.astype(BF)

        by_rows(whole.shape[0], 48, add)
        moved.append(regroup(whole, got))

    for n, job in enumerate(jobs):
        w, i = job
        ref, side, total, line, whole, got = weights[w]
        started[job].wait_recv()
        if n + 2 < len(jobs):
            started[jobs[n + 2]] = to_side(jobs[n + 2])
        at = flip(dp, order[i])

        def add(cut):
            total[i, cut] = (ref[at, cut].astype(F32) + side[i, cut].astype(F32)).astype(BF)

        by_rows(side.shape[1], 48, add)
        if i < 3:
            line_copies[job] = s.copy(total.at[i], line.at[i], order[i])
        if w == 1 and i == 2:
            finish(0)
    for one in moved[0]:
        one.wait_recv()
    in_columns(grown_got, grown_out, 8)
    far[1].wait_recv()
    crossed.wait_recv()

    def add_up(cut):
        up_ref[cut] = own_ref[cut] + far_in[1, cut].astype(F32) + over_in[cut].astype(F32)

    by_rows(up_ref.shape[0], 64, add_up)
    for one in norm_dp_copies:
        one.wait_recv()
    value = norm_mid[...]
    for k in range(7):
        value = value + norm_dp[k]
    norm_out[...] = value
    for one in moved[1]:
        one.wait_recv()
    in_columns(qkv_got, qkv_out, 3)
    finish(1)
    for one in moved[2]:
        one.wait_recv()
    in_columns(pair_got, pair_out, 2)
    for one in s.open:
        one.wait_send()


def closing(qkv, pair, grown, far, over, own, norms):
    vmem = pl.BlockSpec(memory_space=pltpu.VMEM)
    size = qkv.shape[1] // 4

    def parts(value):
        n = value.shape[2]
        rows = value.shape[1]
        return [
            pltpu.VMEM((4, rows, n), BF),
            pltpu.VMEM((4, rows, n), BF),
            pltpu.VMEM((3, rows, n), BF),
            pltpu.VMEM((rows, n), BF),
            pltpu.VMEM((4, rows // 4, n), BF),
        ]

    copies = 2 + 8 + 3 + 1 + 7 + 6 + 9
    return pl.pallas_call(
        closing_kernel,
        out_shape=[
            jax.ShapeDtypeStruct(own.shape, F32),
            jax.ShapeDtypeStruct((size, 4 * qkv.shape[2]), F32),
            jax.ShapeDtypeStruct((size, 4 * pair.shape[2]), F32),
            jax.ShapeDtypeStruct((size, 4 * grown.shape[1]), F32),
            jax.ShapeDtypeStruct(norms.shape, F32),
        ],
        in_specs=[vmem] * 7,
        out_specs=[vmem] * 5,
        scratch_shapes=[
            pltpu.VMEM(far.shape, BF),
            pltpu.VMEM(over.shape, BF),
            pltpu.VMEM(over.shape, BF),
            pltpu.VMEM((3,) + norms.shape, F32),
            pltpu.VMEM(norms.shape, F32),
            pltpu.VMEM((7,) + norms.shape, F32),
        ]
        + parts(qkv)
        + parts(pair)
        + [pltpu.VMEM((4, size, grown.shape[1]), BF)]
        + [pltpu.SemaphoreType.DMA((copies,)), pltpu.SemaphoreType.DMA((copies,))],
        compiler_params=pltpu.CompilerParams(
            collective_id=1, has_side_effects=True, vmem_limit_bytes=56 << 20
        ),
        cost_estimate=pl.CostEstimate(flops=0, bytes_accessed=300 << 20, transcendentals=0),
        name="closing",
    )(qkv, pair, grown, far, over, own, norms)


def normalized(values):
    center = jnp.mean(values, axis=-1, keepdims=True)
    centered = values - center
    spread = jnp.mean(centered * centered, axis=-1, keepdims=True)
    scale = lax.rsqrt(spread + EPSILON)
    return centered * scale, scale


def norm_input_grad(upstream, gain, xhat, scale):
    weighted = upstream * gain
    first = jnp.mean(weighted, axis=-1, keepdims=True)
    second = jnp.mean(weighted * xhat, axis=-1, keepdims=True)
    return scale * (weighted - first - xhat * second)


def norm_sums(upstream, xhat):
    return jnp.sum(upstream * xhat, axis=0), jnp.sum(upstream, axis=0)


def together(*values):
    return lax.optimization_barrier(values)


def local(
    count,
    frames,
    text,
    cotangent,
    norm_gains,
    norm_biases,
    qkv_weight,
    self_out,
    cross_query,
    cross_kv,
    cross_out,
    up_weight,
    down_weight,
):
    g = Group(count)
    clips, rows, width = frames.shape
    tokens = text.shape[1]
    part = width // 4
    held = width // count
    own_size = held // 4
    ff_rows = down_weight.shape[0] // 4
    near_rows = clips * rows
    seq = g.seq
    place = jnp.stack([jnp.asarray(PLACE, jnp.int32)[a ^ seq] for a in range(4)])
    orders = [seq ^ r for r in REL]

    def columns(weight, outer, inner):
        cut = weight.reshape(weight.shape[0], outer, 4, inner)
        return lax.dynamic_index_in_dim(cut, seq, axis=2, keepdims=False).reshape(weight.shape[0], outer * inner)

    def own_rows(weight):
        size = weight.shape[0] // 4
        return lax.dynamic_slice_in_dim(weight, seq * size, size, axis=0)

    def cut_rows(value):
        return value[:near_rows], value[near_rows : 2 * near_rows], value[2 * near_rows :]

    def piece(value, i, axis):
        return lax.dynamic_index_in_dim(value, orders[i], axis=axis, keepdims=False)

    frames_in = frames.reshape(near_rows, width)
    cot_in = cotangent.reshape(near_rows, width)
    text_in = text.reshape(clips * tokens, width)

    mix_own = jnp.stack([own_rows(self_out), own_rows(cross_query), own_rows(cross_out)])
    mix_whole = lax.all_gather(mix_own, ("dp", "seq"), axis=1, tiled=True)
    w_self, w_query, w_cross = mix_whole[0], mix_whole[1], mix_whole[2]

    norm_own = jnp.concatenate([norm_gains, norm_biases], axis=0)
    if g.paired:
        w_qkv, frames_all, text_all, norms = opening(qkv_weight, frames_in, text_in, norm_own)
        w_qkv = w_qkv.reshape(width, 3 * part)
        frames_all = frames_all.reshape(4 * near_rows, width)
        text_all = text_all.reshape(4 * clips * tokens, width)
        norms = norms.swapaxes(0, 1).reshape(6, width).astype(F32)
    else:
        w_qkv = lax.all_gather(columns(qkv_weight, 3, part), "dp", axis=0, tiled=True)
        frames_over, text_over = g.across(frames_in), g.across(text_in)
        frames_all = jnp.concatenate([frames_in, frames_over, g.core(frames_over), g.core(frames_in)], axis=0)
        text_all = place_pieces([text_in, text_over, g.core(text_over), g.core(text_in)], orders, 0)
        norms = lax.all_gather(norm_own, "dp", axis=1, tiled=True).astype(F32)
    gains, biases = norms[:3], norms[3:]
    w_qkv, frames_all, norms, up_here, down_here, pair_here, cot_here = together(
        w_qkv, frames_all, norms, up_weight, down_weight, cross_kv, cot_in
    )

    down = g.near_step(own_rows(down_here).reshape(2, ff_rows // 2, width))
    pair = g.near_step(columns(pair_here, 2, part))
    hat_all, _ = normalized(frames_all.astype(F32))
    first_low = (hat_all * gains[0] + biases[0]).astype(BF)
    triple = dot_nn(first_low, w_qkv).astype(BF).reshape(4, clips, rows, 3 * part)
    up_own = columns(up_here, count, ff_rows)
    triple, down, pair, up_own = together(triple, down, pair, up_own)
    w_up = lax.all_gather(up_own, "dp", axis=0, tiled=True)

    pair = g.far_step(pair)
    heads_out, levels = self_forward(place, triple, part)
    pair, heads_out, levels, down = together(pair, heads_out, levels, down)

    pair = g.side_step(pair)
    down_first = g.far_step(down[:, 0])
    heads_rows = heads_out.reshape(4, near_rows, part)
    self_mix = exchange(
        heads_to_rows_kernel, heads_rows, (near_rows, width), 2, "heads_to_rows", (near_rows, part)
    )
    pair, down_first, self_mix, down = together(pair, down_first, self_mix, down)

    down_last = g.far_step(down[:, 1])
    down_first = g.side_step(down_first)
    w_pair = g.gathered(pair)
    pair_part = dot_nn(text_all, w_pair).astype(BF).reshape(4 * clips * tokens, 2, part).swapaxes(0, 1)
    pair_over, pair_near = g.across(pair_part), g.core(pair_part)
    residual = frames_in.astype(F32)
    first_sum = residual + dot_nn(self_mix, w_self)
    hat_two, scale_two = normalized(first_sum)
    second_low = (hat_two * gains[1] + biases[1]).astype(BF)
    pair_over, pair_near, second_low = together(pair_over, pair_near, second_low)

    pair_far = g.core(pair_over)
    cot_over, cot_near = g.across(cot_here), g.core(cot_here)
    cross_q = dot_nn(second_low, w_query).astype(BF).reshape(clips, rows, width)
    pair_all = place_pieces([pair_part, pair_over, pair_far, pair_near], orders, 2).reshape(
        2, 4, clips, tokens, width
    )
    cross_mix = cross_forward(cross_q, pair_all).reshape(near_rows, width)
    second_sum = first_sum + dot_nn(cross_mix, w_cross)
    hat_three, scale_three = normalized(second_sum)
    third_own = (hat_three * gains[2] + biases[2]).astype(BF)
    third_own, down_first, down_last, cot_over, cot_near = together(
        third_own, down_first, down_last, cot_over, cot_near
    )

    cot_far = g.core(cot_over)
    down_last = g.side_step(down_last)
    third_low = exchange(
        rows_to_all_kernel, third_own, (4, near_rows, width), 3, "rows_to_all"
    ).reshape(4 * near_rows, width)
    w_down = g.gathered(down_first, down_last)
    cot_all = jnp.concatenate([cot_in, cot_over, cot_far, cot_near], axis=0)

    active_low, hidden_low = middle(third_low, cot_all, w_up, w_down)
    hidden_own, hidden_over, hidden_far = cut_rows(hidden_low)
    far = dot_nt(hidden_far, w_up).astype(BF)
    over = dot_nt(hidden_over, w_up)
    far, over, active_low, hidden_low = together(far, over, active_low, hidden_low)

    far = g.core(far)
    down_part = dot_tn(active_low, cot_all).astype(BF)
    half_columns = hidden_low.shape[1] // 2
    up_first = dot_tn(third_low, hidden_low[:, :half_columns]).astype(BF).reshape(count, held, -1)
    far, up_first, down_part, over = together(far, up_first, down_part, over)
    down_shard = lax.psum_scatter(down_part, "dp", scatter_dimension=0, tiled=True)

    half = far.shape[0] // 2
    crossed = g.across((over + far[:half].astype(F32)).astype(BF))
    up_first = g.side_sum(up_first)
    third_up = dot_nt(hidden_own, w_up) + far[half:].astype(F32)
    up_last = dot_tn(third_low, hidden_low[:, half_columns:]).astype(BF).reshape(count, held, -1)
    active_own, active_over, active_far = cut_rows(active_low)
    block_far = g.core(dot_nn(active_far, w_down).astype(BF))
    block_over = dot_nn(active_over, w_down)
    crossed, up_first, up_last, block_far, third_up, block_over = together(
        crossed, up_first, up_last, block_far, third_up, block_over
    )

    block_crossed = g.across((block_over + block_far[:half].astype(F32)).astype(BF))
    up_last = g.side_sum(up_last)
    up_first = g.far_sum(up_first)
    third_up = third_up + crossed.astype(F32)
    second_grad = cot_in.astype(F32) + norm_input_grad(third_up, gains[2], hat_three, scale_three)
    gain_third, bias_third = norm_sums(third_up, hat_three)
    second_in = second_grad.astype(BF)
    mix_grad = dot_nt(second_in, w_cross).astype(BF).reshape(clips, rows, width)
    query_back, key_sums, value_sums = cross_backward(cross_q, pair_all, mix_grad)
    query_back = query_back.reshape(near_rows, width)
    second_up = dot_nt(query_back, w_query)
    first_grad = second_grad + norm_input_grad(second_up, gains[1], hat_two, scale_two)
    gain_second, bias_second = norm_sums(second_up, hat_two)
    first_in = first_grad.astype(BF)
    self_grad = dot_nt(first_in, w_self).astype(BF)
    pair_sums = jnp.stack([key_sums, value_sums], axis=3).reshape(4 * clips * tokens, 2, 4, part)

    def pair_cut(i):
        return piece(pair_sums, i, 2).reshape(-1, 2 * part)

    pair_far = jnp.concatenate([pair_cut(2), pair_cut(3)], axis=0).astype(BF)
    self_grad, block_crossed, up_last, up_first, pair_far, first_in, query_back = together(
        self_grad, block_crossed, up_last, up_first, pair_far, first_in, query_back
    )

    pair_far = g.core(pair_far)
    up_first = g.near_sum(up_first)
    up_last = g.far_sum(up_last)
    mix_part = jnp.stack(
        [dot_tn(self_mix, first_in), dot_tn(second_low, query_back), dot_tn(cross_mix, second_in)]
    ).astype(BF)
    grads = exchange(
        rows_to_heads_kernel, self_grad, (4, near_rows, part), 4, "rows_to_heads", (near_rows, part)
    )
    grads, pair_far, up_first, mix_part = together(grads, pair_far, up_first, mix_part)
    mix_shard = lax.psum_scatter(mix_part, ("dp", "seq"), scatter_dimension=1, tiled=True)

    pair_half = pair_far.shape[0] // 2
    pair_crossed = g.across((pair_cut(1) + pair_far[:pair_half].astype(F32)).astype(BF))
    triple_back = self_backward(
        place, triple, grads.reshape(4, clips, rows, part), levels, part
    ).reshape(4 * near_rows, 3 * part)
    block_output = (
        second_sum + dot_nn(active_own, w_down) + block_far[half:].astype(F32) + block_crossed.astype(F32)
    ).astype(BF)
    triple_back, up_last, pair_crossed, block_output = together(triple_back, up_last, pair_crossed, block_output)
    pair_back = (pair_cut(0) + pair_far[pair_half:].astype(F32) + pair_crossed.astype(F32)).astype(BF)
    pair_grad = dot_tn(text_all, pair_back).astype(BF).reshape(count, held, -1)
    text_part = dot_nt(pair_back, w_pair).reshape(4, clips * tokens, width)

    up_last = g.near_sum(up_last)
    text_far = g.core(jnp.stack([piece(text_part, 2, 0), piece(text_part, 3, 0)]).astype(BF))
    back_own, back_over, back_far = cut_rows(triple_back)
    far_full = dot_nt(back_far, w_qkv)
    over_full = dot_nt(back_over, w_qkv)
    own_full = dot_nt(back_own, w_qkv)
    far = far_full.astype(BF)
    qkv_part = dot_tn(first_low, triple_back).astype(BF).reshape(count, held, -1)
    hat_own, hat_over, hat_far = cut_rows(hat_all)
    gain_first = (
        jnp.sum(own_full * hat_own, axis=0)
        + jnp.sum(over_full * hat_over, axis=0)
        + jnp.sum(far_full * hat_far, axis=0)
    )
    bias_first = jnp.sum(own_full, axis=0) + jnp.sum(over_full, axis=0) + jnp.sum(far_full, axis=0)
    norm_part = jnp.stack([gain_first, gain_second, gain_third, bias_first, bias_second, bias_third])
    far, qkv_part, up_last, norm_part, text_far, over_full, own_full = together(
        far, qkv_part, up_last, norm_part, text_far, over_full, own_full
    )

    def regroup_over(value):
        sends = [lax.dynamic_slice_in_dim(value, o * own_size, own_size, axis=0) for o in orders]
        return [sends[0], g.across(jnp.stack([sends[1], sends[2]])), g.core(sends[3])]

    def regroup(parts, outer, inner):
        own, over, near = parts
        out = jnp.zeros((4, own_size, outer, inner), BF)
        for one, order in zip((own, over[0], g.core(over[1]), near), orders):
            out = lax.dynamic_update_slice(out, one.reshape(1, own_size, outer, inner), (order, 0, 0, 0))
        return in_columns(out)

    def in_columns(value):
        return value.transpose(1, 2, 0, 3).reshape(value.shape[1], -1).astype(F32)

    up_grad = jnp.concatenate([g.total(up_first), g.total(up_last)], axis=-1)
    text_crossed = g.across((piece(text_part, 1, 0) + text_far[0].astype(F32)).astype(BF))
    if g.paired:
        padded = jnp.pad(norm_part, ((0, 2), (0, 0)))
        first_up, qkv_out, pair_out, up_out, norm_all = closing(
            qkv_part, pair_grad, up_grad, far.reshape(2, half, width), over_full, own_full, padded
        )
        norm_all = norm_all[:6]
    else:
        far = g.core(far)
        crossed = g.across((over_full + far[:half].astype(F32)).astype(BF))
        first_up = own_full + far[half:].astype(F32) + crossed.astype(F32)
        norm_all = lax.psum(norm_part, ("dp", "seq"))
        shards = [
            lax.psum_scatter(v.reshape(width, -1), "dp", scatter_dimension=0, tiled=True)
            for v in (qkv_part, pair_grad)
        ]
        qkv_out = regroup(regroup_over(shards[0]), 3, part)
        pair_out = regroup(regroup_over(shards[1]), 2, part)
        up_out = regroup(regroup_over(up_grad), count, ff_rows)
    hat_one, scale_one = normalized(residual)
    frame_grad = first_grad + norm_input_grad(first_up, gains[0], hat_one, scale_one)
    text_grad = piece(text_part, 0, 0) + text_far[1].astype(F32) + text_crossed.astype(F32)

    small = width // (4 * count)
    norm_shard = lax.dynamic_slice_in_dim(norm_all, (g.dp * 4 + seq) * small, small, axis=1)
    mix_shard = mix_shard.astype(F32)
    return (
        block_output.reshape(clips, rows, width),
        frame_grad.reshape(clips, rows, width),
        text_grad.reshape(clips, tokens, width),
        norm_shard[:3],
        norm_shard[3:],
        qkv_out,
        mix_shard[0],
        mix_shard[1],
        pair_out,
        mix_shard[2],
        up_out,
        down_shard.astype(F32),
    )


def solution(mesh):
    rows = P("dp", "seq", None)
    both = P(("dp", "seq"), None)
    return jax.shard_map(
        functools.partial(local, mesh.shape["dp"]),
        mesh=mesh,
        in_specs=(rows, rows, rows, P(None, "dp"), P(None, "dp")) + (P("dp", None),) * 7,
        out_specs=(rows, rows, rows, P(None, ("dp", "seq")), P(None, ("dp", "seq"))) + (both,) * 7,
        check_vma=False,
    )
```

```python
import functools

import jax
import jax.numpy as jnp
from jax import lax
from jax.experimental import pallas as pl
from jax.experimental.pallas import tpu as pltpu
from jax.sharding import PartitionSpec as P

HEAD_DIM = 64
EPSILON = 1e-05
NEGATIVE = -1e30
BF = jnp.bfloat16
F32 = jnp.float32

REL = (0, 2, 3, 1)
PLACE = (0, 3, 1, 2)


def dot_nn(a, b):
    return lax.dot_general(a, b, (((1,), (0,)), ((), ())), preferred_element_type=F32)


def dot_nt(a, b):
    return lax.dot_general(a, b, (((1,), (1,)), ((), ())), preferred_element_type=F32)


def dot_tn(a, b):
    return lax.dot_general(a, b, (((0,), (0,)), ((), ())), preferred_element_type=F32)


def after(value, *others):
    return lax.optimization_barrier((value,) + others)[0]


def self_forward_kernel(place_ref, q_ref, k_ref, v_ref, o_ref, l_ref):
    parts, rows = q_ref.shape[0], q_ref.shape[2]
    heads = q_ref.shape[3] // HEAD_DIM
    keys_at = lax.broadcasted_iota(jnp.int32, (rows, rows), 0)
    rows_at = lax.broadcasted_iota(jnp.int32, (rows, rows), 1)
    visible = keys_at <= rows_at
    for a in range(parts):
        here = place_ref[a]
        mixed = []
        for h in range(heads):
            cols = slice(h * HEAD_DIM, (h + 1) * HEAD_DIM)
            q = q_ref[here, 0, :, cols] * (HEAD_DIM**-0.5)
            scores = []
            for b in range(a + 1):
                s = dot_nt(k_ref[place_ref[b], 0, :, cols], q)
                if a == b:
                    s = jnp.where(visible, s, NEGATIVE)
                scores.append(s)
            top = functools.reduce(jnp.maximum, [jnp.max(s, axis=0, keepdims=True) for s in scores])
            raised = [jnp.exp(s - top) for s in scores]
            total = functools.reduce(jnp.add, [jnp.sum(e, axis=0, keepdims=True) for e in raised])
            share = 1.0 / total
            out = None
            for b in range(a + 1):
                p = (raised[b] * share).astype(BF)
                term = dot_tn(v_ref[place_ref[b], 0, :, cols], p)
                out = term if out is None else out + term
            mixed.append(out)
            l_ref[0, h, a : a + 1, :] = top + jnp.log(total)
        o_ref[here, 0] = jnp.concatenate(mixed, axis=0).T.astype(BF)


def self_forward(place, triple, width):
    parts, clips, rows, _ = triple.shape
    groups = width // 128
    block = (parts, 1, rows, 128)
    return pl.pallas_call(
        self_forward_kernel,
        out_shape=(
            jax.ShapeDtypeStruct((parts, clips, rows, width), BF),
            jax.ShapeDtypeStruct((clips, width // HEAD_DIM, parts, rows), F32),
        ),
        grid_spec=pltpu.PrefetchScalarGridSpec(
            num_scalar_prefetch=1,
            grid=(clips, groups),
            in_specs=[
                pl.BlockSpec(block, lambda i, j, p: (0, i, 0, j)),
                pl.BlockSpec(block, lambda i, j, p: (0, i, 0, groups + j)),
                pl.BlockSpec(block, lambda i, j, p: (0, i, 0, 2 * groups + j)),
            ],
            out_specs=[
                pl.BlockSpec(block, lambda i, j, p: (0, i, 0, j)),
                pl.BlockSpec((1, 2, parts, rows), lambda i, j, p: (i, j, 0, 0)),
            ],
        ),
        compiler_params=pltpu.CompilerParams(vmem_limit_bytes=40 << 20),
        cost_estimate=pl.CostEstimate(
            flops=clips * width * rows * rows * 10 * 4,
            bytes_accessed=clips * rows * parts * width * 8,
            transcendentals=clips * (width // HEAD_DIM) * rows * rows * 10,
        ),
        name="self_forward",
    )(place, triple, triple, triple)


def self_backward_kernel(place_ref, q_ref, k_ref, v_ref, g_ref, l_ref, out_ref, gk_ref, gv_ref):
    parts, rows = q_ref.shape[0], q_ref.shape[2]
    heads = q_ref.shape[3] // HEAD_DIM
    width = out_ref.shape[3] // 3
    scale = HEAD_DIM**-0.5
    column = pl.multiple_of(pl.program_id(1) * 128, 128)
    keys_at = lax.broadcasted_iota(jnp.int32, (rows, rows), 0)
    rows_at = lax.broadcasted_iota(jnp.int32, (rows, rows), 1)
    visible = keys_at <= rows_at
    for a in range(parts):
        here = place_ref[a]
        grads_q = []
        for h in range(heads):
            cols = slice(h * HEAD_DIM, (h + 1) * HEAD_DIM)
            q = q_ref[here, 0, :, cols] * scale
            grad = g_ref[here, 0, :, cols]
            level = l_ref[0, h, a : a + 1, :]
            probs, slopes = [], []
            inner = None
            for b in range(a + 1):
                s = dot_nt(k_ref[place_ref[b], 0, :, cols], q)
                if a == b:
                    s = jnp.where(visible, s, NEGATIVE)
                p = jnp.exp(s - level)
                dp = dot_nt(v_ref[place_ref[b], 0, :, cols], grad)
                term = jnp.sum(p * dp, axis=0, keepdims=True)
                inner = term if inner is None else inner + term
                probs.append(p)
                slopes.append(dp)
            gq = None
            for b in range(a + 1):
                ds = (probs[b] * (slopes[b] - inner)).astype(BF)
                term = dot_tn(k_ref[place_ref[b], 0, :, cols], ds)
                gq = term if gq is None else gq + term
                gk = dot_nn(ds, q)
                gv = dot_nn(probs[b].astype(BF), grad)
                if a == b:
                    gk_ref[b, :, cols] = gk
                    gv_ref[b, :, cols] = gv
                else:
                    gk_ref[b, :, cols] += gk
                    gv_ref[b, :, cols] += gv
            grads_q.append(gq * scale)
        out_ref[here, 0, :, pl.ds(column, 128)] = jnp.concatenate(grads_q, axis=0).T.astype(BF)
    for b in range(parts):
        here = place_ref[b]
        out_ref[here, 0, :, pl.ds(width + column, 128)] = gk_ref[b].astype(BF)
        out_ref[here, 0, :, pl.ds(2 * width + column, 128)] = gv_ref[b].astype(BF)


def self_backward(place, triple, grads, levels, width):
    parts, clips, rows, _ = triple.shape
    groups = width // 128
    block = (parts, 1, rows, 128)
    return pl.pallas_call(
        self_backward_kernel,
        out_shape=jax.ShapeDtypeStruct((parts, clips, rows, 3 * width), BF),
        grid_spec=pltpu.PrefetchScalarGridSpec(
            num_scalar_prefetch=1,
            grid=(clips, groups),
            in_specs=[
                pl.BlockSpec(block, lambda i, j, p: (0, i, 0, j)),
                pl.BlockSpec(block, lambda i, j, p: (0, i, 0, groups + j)),
                pl.BlockSpec(block, lambda i, j, p: (0, i, 0, 2 * groups + j)),
                pl.BlockSpec(block, lambda i, j, p: (0, i, 0, j)),
                pl.BlockSpec((1, 2, parts, rows), lambda i, j, p: (i, j, 0, 0)),
            ],
            out_specs=pl.BlockSpec((parts, 1, rows, 3 * width), lambda i, j, p: (0, i, 0, 0)),
            scratch_shapes=[
                pltpu.VMEM((parts, rows, 128), F32),
                pltpu.VMEM((parts, rows, 128), F32),
            ],
        ),
        compiler_params=pltpu.CompilerParams(vmem_limit_bytes=48 << 20),
        cost_estimate=pl.CostEstimate(
            flops=clips * width * rows * rows * 10 * 10,
            bytes_accessed=clips * rows * parts * width * 14,
            transcendentals=clips * (width // HEAD_DIM) * rows * rows * 10,
        ),
        name="self_backward",
    )(place, triple, triple, triple, grads, levels)


def cross_forward_kernel(q_ref, k_ref, v_ref, o_ref):
    width = q_ref.shape[2]
    k_all = k_ref[0, :, 0].reshape(-1, width)
    v_all = v_ref[0, :, 0].reshape(-1, width)
    for pair in range(width // 128):
        mixed = []
        for h in (2 * pair, 2 * pair + 1):
            cols = slice(h * HEAD_DIM, (h + 1) * HEAD_DIM)
            s = dot_nt(k_all[:, cols], q_ref[0, :, cols] * (HEAD_DIM**-0.5))
            e = jnp.exp(s - jnp.max(s, axis=0, keepdims=True))
            p = e * (1.0 / jnp.sum(e, axis=0, keepdims=True))
            mixed.append(dot_tn(v_all[:, cols], p.astype(BF)))
        o_ref[0, :, pair * 128 : (pair + 1) * 128] = jnp.concatenate(mixed, axis=0).T.astype(BF)


def cross_forward(query, text_kv):
    clips, rows, width = query.shape
    _, parts, _, tokens, _ = text_kv.shape
    step = 512
    groups = width // step
    return pl.pallas_call(
        cross_forward_kernel,
        out_shape=jax.ShapeDtypeStruct(query.shape, BF),
        grid=(clips, groups),
        in_specs=[
            pl.BlockSpec((1, rows, step), lambda i, j: (i, 0, j)),
            pl.BlockSpec((1, parts, 1, tokens, step), lambda i, j: (0, 0, i, 0, j)),
            pl.BlockSpec((1, parts, 1, tokens, step), lambda i, j: (1, 0, i, 0, j)),
        ],
        out_specs=pl.BlockSpec((1, rows, step), lambda i, j: (i, 0, j)),
        cost_estimate=pl.CostEstimate(
            flops=clips * rows * width * parts * tokens * 4,
            bytes_accessed=clips * rows * width * 4,
            transcendentals=clips * rows * parts * tokens * (width // HEAD_DIM),
        ),
        name="cross_forward",
    )(query, text_kv, text_kv)


def cross_backward_kernel(q_ref, k_ref, v_ref, g_ref, gq_ref, gk_ref, gv_ref):
    width = q_ref.shape[2]
    _, parts, _, tokens, _ = k_ref.shape
    scale = HEAD_DIM**-0.5
    k_all = k_ref[0, :, 0].reshape(-1, width)
    v_all = v_ref[0, :, 0].reshape(-1, width)
    for pair in range(width // 128):
        rows_q, rows_k, rows_v = [], [], []
        for h in (2 * pair, 2 * pair + 1):
            cols = slice(h * HEAD_DIM, (h + 1) * HEAD_DIM)
            q = q_ref[0, :, cols] * scale
            grad = g_ref[0, :, cols]
            s = dot_nt(k_all[:, cols], q)
            e = jnp.exp(s - jnp.max(s, axis=0, keepdims=True))
            p = e * (1.0 / jnp.sum(e, axis=0, keepdims=True))
            dp = dot_nt(v_all[:, cols], grad)
            inner = jnp.sum(p * dp, axis=0, keepdims=True)
            ds = (p * (dp - inner)).astype(BF)
            rows_q.append(dot_tn(k_all[:, cols], ds) * scale)
            rows_k.append(dot_nn(ds, q))
            rows_v.append(dot_nn(p.astype(BF), grad))
        span = slice(pair * 128, (pair + 1) * 128)
        gq_ref[0, :, span] = jnp.concatenate(rows_q, axis=0).T.astype(BF)
        gk_ref[:, 0, :, span] = jnp.concatenate(rows_k, axis=1).reshape(parts, tokens, 128)
        gv_ref[:, 0, :, span] = jnp.concatenate(rows_v, axis=1).reshape(parts, tokens, 128)


def cross_backward(query, text_kv, grads):
    clips, rows, width = query.shape
    _, parts, _, tokens, _ = text_kv.shape
    step = 512
    groups = width // step
    row_spec = pl.BlockSpec((1, rows, step), lambda i, j: (i, 0, j))
    text_block = (parts, 1, tokens, step)
    return pl.pallas_call(
        cross_backward_kernel,
        out_shape=(
            jax.ShapeDtypeStruct(query.shape, BF),
            jax.ShapeDtypeStruct((parts, clips, tokens, width), F32),
            jax.ShapeDtypeStruct((parts, clips, tokens, width), F32),
        ),
        grid=(clips, groups),
        in_specs=[
            row_spec,
            pl.BlockSpec((1,) + text_block, lambda i, j: (0, 0, i, 0, j)),
            pl.BlockSpec((1,) + text_block, lambda i, j: (1, 0, i, 0, j)),
            row_spec,
        ],
        out_specs=[
            row_spec,
            pl.BlockSpec(text_block, lambda i, j: (0, i, 0, j)),
            pl.BlockSpec(text_block, lambda i, j: (0, i, 0, j)),
        ],
        cost_estimate=pl.CostEstimate(
            flops=clips * rows * width * parts * tokens * 10,
            bytes_accessed=clips * rows * width * 6,
            transcendentals=clips * rows * parts * tokens * (width // HEAD_DIM),
        ),
        name="cross_backward",
    )(query, text_kv, text_kv, grads)


def gelu_and_slope(v):
    phi = 0.5 + 0.5 * lax.erf(v * (0.5**0.5))
    density = jnp.exp(-0.5 * v * v) * (2.0 * jnp.pi) ** -0.5
    return v * phi, phi + v * density


def middle_kernel(x_ref, c_ref, up_ref, down_ref, act_ref, grad_ref):
    active, slope = gelu_and_slope(dot_nn(x_ref[...], up_ref[...]))
    act_ref[...] = active.astype(BF)
    grad_ref[...] = (dot_nt(c_ref[...], down_ref[...]) * slope).astype(BF)


def middle(normed, cotangent, both):
    rows, width = normed.shape
    hidden = both.shape[2]
    tile_r, tile_h = min(512, rows), min(512, hidden)
    row_spec = pl.BlockSpec((tile_r, width), lambda j, i: (i, 0))
    out_spec = pl.BlockSpec((tile_r, tile_h), lambda j, i: (i, j))
    shape = jax.ShapeDtypeStruct((rows, hidden), BF)
    return pl.pallas_call(
        middle_kernel,
        out_shape=(shape, shape),
        grid=(hidden // tile_h, rows // tile_r),
        in_specs=[
            row_spec,
            row_spec,
            pl.BlockSpec((None, width, tile_h), lambda j, i: (0, 0, j)),
            pl.BlockSpec((None, tile_h, width), lambda j, i: (1, j, 0)),
        ],
        out_specs=(out_spec, out_spec),
        compiler_params=pltpu.CompilerParams(vmem_limit_bytes=40 << 20),
        cost_estimate=pl.CostEstimate(
            flops=4 * rows * width * hidden,
            bytes_accessed=4 * rows * width * 3 + 4 * width * hidden + 4 * rows * hidden,
            transcendentals=2 * rows * hidden,
        ),
        name="middle",
    )(normed, cotangent, both, both)


def place_kernel(count, axis, starts_ref, *refs):
    pieces, out_ref, sems = refs[:count], refs[count], refs[count + 1]
    copies = []
    for i in range(count):
        size = pieces[i].shape[axis]
        where = [slice(None)] * len(out_ref.shape)
        where[axis] = pl.ds(pl.multiple_of(starts_ref[i] * size, size), size)
        copies.append(pltpu.make_async_copy(pieces[i], out_ref.at[tuple(where)], sems.at[i]))
    for copy in copies:
        copy.start()
    for copy in copies:
        copy.wait()


def place_pieces(pieces, starts, axis):
    shape = list(pieces[0].shape)
    shape[axis] *= len(pieces)
    any_spec = pl.BlockSpec(memory_space=pl.ANY)
    size = pieces[0].size * len(pieces) * pieces[0].dtype.itemsize
    return pl.pallas_call(
        functools.partial(place_kernel, len(pieces), axis),
        out_shape=jax.ShapeDtypeStruct(tuple(shape), pieces[0].dtype),
        in_specs=[pl.BlockSpec(memory_space=pltpu.SMEM)]
        + [pl.BlockSpec(memory_space=pltpu.VMEM)] * len(pieces),
        out_specs=any_spec,
        scratch_shapes=[pltpu.SemaphoreType.DMA((len(pieces),))],
        compiler_params=pltpu.CompilerParams(vmem_limit_bytes=2 * size + (4 << 20)),
        cost_estimate=pl.CostEstimate(flops=0, bytes_accessed=2 * size, transcendentals=0),
        name="place_pieces",
    )(jnp.stack([jnp.asarray(s, jnp.int32) for s in starts]), *pieces)


class Group:
    def __init__(self, count):
        self.count = count
        self.dp = lax.axis_index("dp")
        self.seq = lax.axis_index("seq")
        self.bits = (self.dp // 4, self.dp // 2 % 2, self.dp % 2)
        self.paired = count == 8

    def core(self, value):
        return lax.ppermute(value, "seq", [(i, i ^ 1) for i in range(4)])

    def across(self, value):
        return lax.ppermute(value, "seq", [(i, i ^ 2) for i in range(4)])

    def swap(self, value, bit):
        return lax.ppermute(value, "dp", [(i, i ^ bit) for i in range(self.count)])


    def halve(self, value, axis, place, bit):
        away = lax.dynamic_index_in_dim(value, 1 - place, axis=axis, keepdims=False)
        kept = lax.dynamic_index_in_dim(value, place, axis=axis, keepdims=False)
        return kept, self.swap(away, bit)

    def add(self, pair):
        return (pair[0].astype(F32) + pair[1].astype(F32)).astype(BF)

    def side_sum(self, value):
        if not self.paired:
            return value.reshape((-1,) + value.shape[2:]), None
        return self.halve(value.reshape((2, 2, 2) + value.shape[1:]), 2, self.bits[2], 1)

    def far_sum(self, pair):
        if not self.paired:
            return pair
        return self.halve(self.add(pair), 0, self.bits[0], 4)

    def near_sum(self, pair):
        if not self.paired:
            return lax.psum_scatter(pair[0], "dp", scatter_dimension=0, tiled=True), None
        return self.halve(self.add(pair), 0, self.bits[1], 2)

    def total(self, pair):
        return self.add(pair) if self.paired else pair[0]

    def sum_all_small(self, value):
        if not self.paired:
            return lax.psum(value, ("dp", "seq"))
        value = value + self.core(value)
        value = value + self.across(value)
        for bit in (1, 2, 4):
            value = value + self.swap(value, bit)
        return value


MESH = pl.DeviceIdType.MESH


def flip(index, bits):
    for bit in (1, 2, 4):
        if bits & bit:
            index = index + bit - 2 * bit * (index // bit % 2)
    return index


class Sender:
    def __init__(self, send, recv):
        self.send, self.recv, self.used = send, recv, 0
        self.dp, self.seq = lax.axis_index("dp"), lax.axis_index("seq")
        self.open = []

    def greet(self, dp_bits, seq_bits):
        barrier = pltpu.get_barrier_semaphore()
        peers = [self.peer(d, 0) for d in dp_bits] + [self.peer(0, s) for s in seq_bits]
        for peer in peers:
            pl.semaphore_signal(barrier, inc=1, device_id=peer, device_id_type=MESH)
        pl.semaphore_wait(barrier, len(peers))

    def peer(self, dp_bits, seq_bits):
        return (flip(self.dp, dp_bits), flip(self.seq, seq_bits))

    def copy(self, src, dst, dp_bits=0, seq_bits=0):
        one = pltpu.make_async_remote_copy(
            src_ref=src,
            dst_ref=dst,
            send_sem=self.send.at[self.used],
            recv_sem=self.recv.at[self.used],
            device_id=self.peer(dp_bits, seq_bits),
            device_id_type=MESH,
        )
        self.used += 1
        one.start()
        self.open.append(one)
        return one


def opening_kernel(
    qkv_ref, kv_ref, up_ref, down_ref, frames_ref, cot_ref, text_ref, norm_ref,
    w_ref, p_ref, both_ref, fa_ref, low_ref, mean_ref, scale_ref, ca_ref, ta_ref, na_ref,
    gain_ref, local_sem, send, recv,
):
    s = Sender(send, recv)
    dp, seq = s.dp, s.seq
    held = norm_ref.shape[1]
    part = w_ref.shape[2] // 3
    own = both_ref.shape[1]
    loads = []

    def load(src, dst):
        loads.append(pltpu.make_async_copy(src, dst, local_sem.at[len(loads)]))
        loads[-1].start()

    for i in range(3):
        at = pl.ds(pl.multiple_of((4 * i + seq) * part, 128), part)
        load(qkv_ref.at[:, at], w_ref.at[dp, :, i * part : (i + 1) * part])
    for i in range(2):
        at = pl.ds(pl.multiple_of((4 * i + seq) * part, 128), part)
        load(kv_ref.at[:, at], p_ref.at[dp, :, i * part : (i + 1) * part])
    load(down_ref.at[pl.ds(pl.multiple_of(seq * own, own), own)], both_ref.at[1])
    s.greet((1, 2, 3, 4, 5, 6, 7), (1, 2))
    over = s.copy(frames_ref, fa_ref.at[1], 0, 2)
    near = s.copy(frames_ref, fa_ref.at[3], 0, 1)
    for one in loads:
        one.wait()

    chunks = []
    for ref, count in ((w_ref, 3), (p_ref, 2)):
        rows = ref.shape[1] // count
        chunks += [(ref, pl.ds(j * rows, rows)) for j in range(count)]

    def along(j):
        ref, cut = chunks[j]
        return [s.copy(ref.at[dp, cut], ref.at[dp, cut], k) for k in (4, 6, 2)]

    line = [along(0)]
    side = [s.copy(ref.at[dp], ref.at[dp], 1) for ref in (w_ref, p_ref)]
    norms = [s.copy(norm_ref, na_ref.at[dp], k) for k in (1, 2, 3, 4, 5, 6, 7)]
    text_over = s.copy(text_ref, ta_ref.at[seq], 0, 2)
    text_near = s.copy(text_ref, ta_ref.at[seq], 0, 1)
    fa_ref[0] = frames_ref[...]
    ca_ref[0] = cot_ref[...]
    ta_ref[seq] = text_ref[...]
    na_ref[dp] = norm_ref[...]
    for k in range(4):

        @pl.when(seq == k)
        def _():
            for d in range(up_ref.shape[1] // (4 * own)):
                at = (4 * d + k) * own
                both_ref[0, :, d * own : (d + 1) * own] = up_ref[:, at : at + own]

    def normalize(slot):
        def run(i, carry):
            cut = pl.ds(pl.multiple_of(i * 32, 32), 32)
            x = fa_ref[slot, cut].astype(F32)
            center = jnp.mean(x, axis=-1, keepdims=True)
            x = x - center
            scale = lax.rsqrt(jnp.mean(x * x, axis=-1, keepdims=True) + EPSILON)
            low_ref[slot, cut] = (x * scale * gain_ref[0:1] + gain_ref[3:4]).astype(BF)
            mean_ref[slot, cut] = jnp.broadcast_to(center, (32, 128))
            scale_ref[slot, cut] = jnp.broadcast_to(scale, (32, 128))
            return carry

        lax.fori_loop(0, fa_ref.shape[1] // 32, run, 0)

    waited = []
    far = cot_over = cot_near = None
    for j, (ref, cut) in enumerate(chunks):
        if j + 1 < len(chunks):
            for one in line[j]:
                one.wait_send()
            waited += line[j]
            line.append(along(j + 1))
        for k, one in zip((4, 6, 2), line[j]):
            one.wait_recv()
            at = flip(dp, k)
            side.append(s.copy(ref.at[at, cut], ref.at[at, cut], 1))
        if j == 0:
            for one in norms:
                one.wait_recv()
            for d in range(na_ref.shape[0]):
                gain_ref[:, d * held : (d + 1) * held] = na_ref[d].astype(F32)
            normalize(0)
            near.wait_recv()
            normalize(3)
        if j == 2:
            over.wait_recv()
            far = s.copy(fa_ref.at[1], fa_ref.at[2], 0, 1)
            cot_over = s.copy(cot_ref, ca_ref.at[1], 0, 2)
            cot_near = s.copy(cot_ref, ca_ref.at[3], 0, 1)
            normalize(1)
            text_over.wait_recv()
            at = flip(seq, 2)
            text_far = s.copy(ta_ref.at[at], ta_ref.at[at], 0, 1)
            far.wait_recv()
            normalize(2)
    cot_over.wait_recv()
    cot_far = s.copy(ca_ref.at[1], ca_ref.at[2], 0, 1)
    for one in side + [text_near, text_far, cot_near, cot_far]:
        one.wait_recv()
    for one in s.open:
        if not any(one is other for other in waited):
            one.wait_send()


def opening(qkv, kv, up, down, frames, cot, text, norms):
    vmem = pl.BlockSpec(memory_space=pltpu.VMEM)
    hbm = pl.BlockSpec(memory_space=pl.ANY)
    count = 8
    copies = 3 * 5 + 2 + 3 * 5 + 9 + 7
    held = qkv.shape[0]
    four = (4,) + frames.shape
    bf = [
        (count, held, qkv.shape[1] // 4),
        (count, held, kv.shape[1] // 4),
        (2, down.shape[0] // 4, down.shape[1]),
        four,
        four,
    ]
    shapes = [jax.ShapeDtypeStruct(sh, BF) for sh in bf]
    shapes += [jax.ShapeDtypeStruct(four[:2] + (128,), F32)] * 2
    shapes += [jax.ShapeDtypeStruct(sh, BF) for sh in (four, (4,) + text.shape, (count,) + norms.shape)]
    return pl.pallas_call(
        opening_kernel,
        out_shape=shapes,
        in_specs=[hbm, hbm, vmem, hbm] + [vmem] * 4,
        out_specs=[vmem] * len(shapes),
        scratch_shapes=[
            pltpu.VMEM((6, count * held), F32),
            pltpu.SemaphoreType.DMA((6,)),
            pltpu.SemaphoreType.DMA((copies,)),
            pltpu.SemaphoreType.DMA((copies,)),
        ],
        compiler_params=pltpu.CompilerParams(
            collective_id=0, has_side_effects=True, vmem_limit_bytes=52 << 20
        ),
        cost_estimate=pl.CostEstimate(flops=0, bytes_accessed=300 << 20, transcendentals=0),
        name="opening",
    )(qkv, kv, up, down, frames, cot, text, norms)


def exchange(kernel, value, shape, number, name, stage=None):
    vmem = pl.BlockSpec(memory_space=pltpu.VMEM)
    copies = 6
    return pl.pallas_call(
        kernel,
        out_shape=jax.ShapeDtypeStruct(shape, value.dtype),
        in_specs=[vmem],
        out_specs=vmem,
        scratch_shapes=([] if stage is None else [pltpu.VMEM(stage, value.dtype)])
        + [pltpu.SemaphoreType.DMA((copies,)), pltpu.SemaphoreType.DMA((copies,))],
        compiler_params=pltpu.CompilerParams(
            collective_id=number, has_side_effects=True, vmem_limit_bytes=24 << 20
        ),
        cost_estimate=pl.CostEstimate(flops=0, bytes_accessed=80 << 20, transcendentals=0),
        name=name,
    )(value)


def rows_to_all_kernel(x_ref, out_ref, send, recv):
    s = Sender(send, recv)
    s.greet((), (1, 2))
    half = x_ref.shape[0] // 2
    cuts = [pl.ds(0, half), pl.ds(half, half)]
    over = [s.copy(x_ref.at[cut], out_ref.at[1, cut], 0, 2) for cut in cuts]
    near = s.copy(x_ref, out_ref.at[3], 0, 1)
    out_ref[0] = x_ref[...]
    far = []
    for one, cut in zip(over, cuts):
        one.wait_recv()
        far.append(s.copy(out_ref.at[1, cut], out_ref.at[2, cut], 0, 1))
    for one in [near] + far:
        one.wait_recv()
    for one in s.open:
        one.wait_send()


def heads_to_rows_kernel(x_ref, out_ref, stage_ref, send, recv):
    s = Sender(send, recv)
    seq = s.seq
    part = x_ref.shape[2]
    s.greet((), (1, 2))

    def at(owner):
        return (slice(None), pl.ds(pl.multiple_of(owner * part, 128), part))

    relayed = s.copy(x_ref.at[2], stage_ref, 0, 2)
    over = s.copy(x_ref.at[1], out_ref.at[at(seq)], 0, 2)
    near = s.copy(x_ref.at[3], out_ref.at[at(seq)], 0, 1)
    out_ref[at(seq)] = x_ref[0]
    relayed.wait_recv()
    far = s.copy(stage_ref, out_ref.at[at(flip(seq, 2))], 0, 1)
    for one in (near, over, far):
        one.wait_recv()
    for one in s.open:
        one.wait_send()


def rows_to_heads_kernel(
    x_ref, key_ref, value_ref, out_ref, pair_ref, stage_ref, low_ref, got_ref, add_ref, last_ref, send, recv
):
    s = Sender(send, recv)
    seq = s.seq
    part = out_ref.shape[2]

    def at(owner):
        return (slice(None), pl.ds(pl.multiple_of(owner * part, 128), part))

    sums = (key_ref, value_ref)
    for t in range(2):
        low_ref[t, 0] = sums[t][at(flip(seq, 3))].astype(BF)
        low_ref[t, 1] = sums[t][at(flip(seq, 1))].astype(BF)
    s.greet((), (1, 2))
    pair_near = [s.copy(low_ref.at[t], got_ref.at[t], 0, 1) for t in range(2)]
    relayed = s.copy(x_ref.at[at(flip(seq, 3))], stage_ref, 0, 2)
    near = s.copy(x_ref.at[at(flip(seq, 1))], out_ref.at[3], 0, 1)
    for t in range(2):
        pair_near[t].wait_recv()
        add_ref[t] = (sums[t][at(flip(seq, 2))] + got_ref[t, 0].astype(F32)).astype(BF)
    pair_over = s.copy(add_ref, last_ref, 0, 2)
    over = s.copy(x_ref.at[at(flip(seq, 2))], out_ref.at[1], 0, 2)
    out_ref[0] = x_ref[at(seq)]
    relayed.wait_recv()
    far = s.copy(stage_ref, out_ref.at[2], 0, 1)
    pair_over.wait_recv()
    for t in range(2):
        total = sums[t][at(seq)] + got_ref[t, 1].astype(F32) + last_ref[t].astype(F32)
        pair_ref[:, t * part : (t + 1) * part] = total.astype(BF)
    for one in (near, over, far):
        one.wait_recv()
    for one in s.open:
        one.wait_send()


def rows_to_heads(value, keys, values):
    rows, width = value.shape
    part = width // 4
    tokens = keys.shape[0]
    vmem = pl.BlockSpec(memory_space=pltpu.VMEM)
    copies = 7
    return pl.pallas_call(
        rows_to_heads_kernel,
        out_shape=[
            jax.ShapeDtypeStruct((4, rows, part), BF),
            jax.ShapeDtypeStruct((tokens, 2 * part), BF),
        ],
        in_specs=[vmem] * 3,
        out_specs=[vmem] * 2,
        scratch_shapes=[
            pltpu.VMEM((rows, part), BF),
            pltpu.VMEM((2, 2, tokens, part), BF),
            pltpu.VMEM((2, 2, tokens, part), BF),
            pltpu.VMEM((2, tokens, part), BF),
            pltpu.VMEM((2, tokens, part), BF),
            pltpu.SemaphoreType.DMA((copies,)),
            pltpu.SemaphoreType.DMA((copies,)),
        ],
        compiler_params=pltpu.CompilerParams(
            collective_id=4, has_side_effects=True, vmem_limit_bytes=24 << 20
        ),
        cost_estimate=pl.CostEstimate(flops=0, bytes_accessed=80 << 20, transcendentals=0),
        name="rows_to_heads",
    )(value, keys, values)


def by_rows(total, step, body):
    def run(i, carry):
        body(pl.ds(pl.multiple_of(i * step, step), step))
        return carry

    lax.fori_loop(0, total // step, run, 0)


def closing_kernel(
    back_ref, w_ref, low_ref, fa_ref, mean_ref, scale_ref, pair_ref, first_ref, last_ref, norm_ref,
    up_ref, qkv_out, pair_out, grown_out, norm_out,
    far_send, far_in, over_send, over_in, norm_own, norm_seq, norm_mid, norm_dp,
    qkv_ref, side, total, line, whole, qkv_got, pair_line, pair_whole, pair_got, last_in, grown_ref, grown_got,
    send, recv,
):
    s = Sender(send, recv)
    dp, seq = s.dp, s.seq
    order = (4, 6, 2, 0)
    low_bit = dp // 2 % 2
    near_rows = up_ref.shape[0]
    held = side.shape[1]
    tile = 256
    s.greet((1, 2, 3, 4, 5, 6, 7), (1, 2, 3))
    last_copy = s.copy(last_ref.at[1 - low_bit], last_in, 2)
    pair_copies = [s.copy(pair_ref.at[flip(dp, order[i]) // 2], pair_line.at[i], order[i]) for i in range(3)]
    norm_own[...] = norm_ref[...]
    norm_own[0:1] = jnp.zeros_like(norm_own[0:1])
    norm_own[3:4] = jnp.zeros_like(norm_own[3:4])

    def product(first, count, store):
        def run(i, carry):
            at = pl.ds(pl.multiple_of(first + i * tile, tile), tile)
            u = dot_nt(back_ref[at], w_ref[...])
            hat = (fa_ref[at].astype(F32) - mean_ref[at][:, :1]) * scale_ref[at][:, :1]
            norm_own[0:1] += jnp.sum(u * hat, axis=0, keepdims=True)
            norm_own[3:4] += jnp.sum(u, axis=0, keepdims=True)
            store(i, u)
            return carry

        lax.fori_loop(0, count // tile, run, 0)

    def cut_at(i):
        return pl.ds(pl.multiple_of(i * tile, tile), tile)

    def store_far(i, u):
        far_send[cut_at(i)] = u.astype(BF)

    product(2 * near_rows, 2 * near_rows, store_far)
    far = [
        s.copy(far_send.at[pl.ds(i * near_rows, near_rows)], far_in.at[pl.ds(i * near_rows, near_rows)], 0, 1)
        for i in range(2)
    ]

    def to_side(i):
        block = flip(dp, order[i]) // 2
        at = pl.ds(pl.multiple_of(block * 2 * held, 128), 2 * held)
        qkv_ref[i] = dot_tn(low_ref[:, at], back_ref[...]).astype(BF)
        rows = pl.ds(pl.multiple_of((1 - dp % 2) * held, held), held)
        return s.copy(qkv_ref.at[i, rows], side.at[i], 1)

    started = [to_side(0)]
    far[0].wait_recv()

    def store_over(i, u):
        at = cut_at(i)
        over_send[at] = (u + far_in[at].astype(F32)).astype(BF)

    product(near_rows, near_rows, store_over)
    crossed = s.copy(over_send, over_in, 0, 2)
    started.append(to_side(1))

    def regroup(value, got):
        size = got.shape[1]
        moves = []
        for k in (2, 3, 1):
            rows = pl.ds(pl.multiple_of(flip(seq, k) * size, size), size)
            moves.append(s.copy(value.at[rows], got.at[seq], 0, k))
        got[seq] = value[pl.ds(pl.multiple_of(seq * size, size), size)]
        return moves

    def in_columns(got, out, outer):
        inner = got.shape[2] // outer
        for j in range(outer):
            for k in range(4):
                at = (4 * j + k) * inner
                out[:, at : at + inner] = got[k, :, j * inner : (j + 1) * inner]

    far[1].wait_recv()

    def store_own(i, u):
        at = cut_at(i)
        below = pl.ds(pl.multiple_of(near_rows + i * tile, tile), tile)
        up_ref[at] = u + far_in[below].astype(F32)

    product(0, near_rows, store_own)
    norm_copies = [s.copy(norm_own, norm_seq.at[k - 1], 0, k) for k in (1, 2, 3)]
    line_copies = []
    norm_dp_copies = []
    for i in range(4):
        if i + 2 < 4:
            started.append(to_side(i + 2))
        started[i].wait_recv()
        offset = dp % 2 * held

        def add(cut):
            mine = qkv_ref[i, pl.ds(pl.multiple_of(offset + cut.start, 48), cut.size)]
            total[i, cut] = (mine.astype(F32) + side[i, cut].astype(F32)).astype(BF)

        by_rows(held, 48, add)
        if i < 3:
            line_copies.append(s.copy(total.at[i], line.at[i], order[i]))
        if i == 1:
            for one in norm_copies:
                one.wait_recv()
            norm_mid[...] = norm_own[...] + norm_seq[0] + norm_seq[1] + norm_seq[2]
            norm_dp_copies = [s.copy(norm_mid, norm_dp.at[k - 1], k) for k in range(1, 8)]
    last_copy.wait_recv()
    columns = first_ref.shape[1]

    def add_last(cut):
        grown_ref[cut, :columns] = first_ref[cut]
        grown_ref[cut, columns:] = (last_ref[low_bit, cut].astype(F32) + last_in[cut].astype(F32)).astype(BF)

    by_rows(held, 48, add_last)
    moved = [regroup(grown_ref, grown_got)]
    for one in pair_copies:
        one.wait_recv()

    def add_pair(cut):
        value = pair_ref[dp // 2, cut].astype(F32)
        for i in range(3):
            value = value + pair_line[i, cut].astype(F32)
        pair_whole[cut] = value.astype(BF)

    by_rows(held, 48, add_pair)
    moved.append(regroup(pair_whole, pair_got))
    crossed.wait_recv()

    def add_up(cut):
        up_ref[cut] = up_ref[cut] + over_in[cut].astype(F32)

    by_rows(near_rows, 64, add_up)
    for one in norm_dp_copies:
        one.wait_recv()
    value = norm_mid[...]
    for k in range(7):
        value = value + norm_dp[k]
    norm_out[...] = value
    for one in line_copies:
        one.wait_recv()

    def add_line(cut):
        value = total[3, cut].astype(F32)
        for i in range(3):
            value = value + line[i, cut].astype(F32)
        whole[cut] = value.astype(BF)

    by_rows(held, 48, add_line)
    moved.append(regroup(whole, qkv_got))
    for got, out, outer, moves in (
        (grown_got, grown_out, 8, moved[0]), (pair_got, pair_out, 2, moved[1]), (qkv_got, qkv_out, 3, moved[2])
    ):
        for one in moves:
            one.wait_recv()
        in_columns(got, out, outer)
    for one in s.open:
        one.wait_send()


def closing(back, w, low, frames, mean, scale, pair, first, last, norms):
    vmem = pl.BlockSpec(memory_space=pltpu.VMEM)
    held = pair.shape[1]
    size = held // 4
    n = back.shape[1]
    width = low.shape[1]
    near_rows = low.shape[0] // 4
    grown = (held, first.shape[1] + last.shape[2])
    copies = 2 + 4 + 3 + 1 + 7 + 3 + 9 + 3 + 1
    return pl.pallas_call(
        closing_kernel,
        out_shape=[
            jax.ShapeDtypeStruct((near_rows, width), F32),
            jax.ShapeDtypeStruct((size, 4 * n), BF),
            jax.ShapeDtypeStruct((size, 4 * pair.shape[2]), BF),
            jax.ShapeDtypeStruct((size, 4 * grown[1]), BF),
            jax.ShapeDtypeStruct(norms.shape, F32),
        ],
        in_specs=[vmem] * 10,
        out_specs=[vmem] * 5,
        scratch_shapes=[
            pltpu.VMEM((2 * near_rows, width), BF),
            pltpu.VMEM((2 * near_rows, width), BF),
            pltpu.VMEM((near_rows, width), BF),
            pltpu.VMEM((near_rows, width), BF),
            pltpu.VMEM(norms.shape, F32),
            pltpu.VMEM((3,) + norms.shape, F32),
            pltpu.VMEM(norms.shape, F32),
            pltpu.VMEM((7,) + norms.shape, F32),
            pltpu.VMEM((4, 2 * held, n), BF),
            pltpu.VMEM((4, held, n), BF),
            pltpu.VMEM((4, held, n), BF),
            pltpu.VMEM((3, held, n), BF),
            pltpu.VMEM((held, n), BF),
            pltpu.VMEM((4, size, n), BF),
            pltpu.VMEM((3, held, pair.shape[2]), BF),
            pltpu.VMEM((held, pair.shape[2]), BF),
            pltpu.VMEM((4, size, pair.shape[2]), BF),
            pltpu.VMEM(last.shape[1:], BF),
            pltpu.VMEM(grown, BF),
            pltpu.VMEM((4, size, grown[1]), BF),
            pltpu.SemaphoreType.DMA((copies,)),
            pltpu.SemaphoreType.DMA((copies,)),
        ],
        compiler_params=pltpu.CompilerParams(
            collective_id=1, has_side_effects=True, vmem_limit_bytes=60 << 20
        ),
        cost_estimate=pl.CostEstimate(
            flops=4 * low.shape[0] * width * n, bytes_accessed=300 << 20, transcendentals=0
        ),
        name="closing",
    )(back, w, low, frames, mean, scale, pair, first, last, norms)


def normalized(values):
    center = jnp.mean(values, axis=-1, keepdims=True)
    centered = values - center
    spread = jnp.mean(centered * centered, axis=-1, keepdims=True)
    scale = lax.rsqrt(spread + EPSILON)
    return centered * scale, scale


def norm_input_grad(upstream, gain, xhat, scale):
    weighted = upstream * gain
    first = jnp.mean(weighted, axis=-1, keepdims=True)
    second = jnp.mean(weighted * xhat, axis=-1, keepdims=True)
    return scale * (weighted - first - xhat * second)


def norm_sums(upstream, xhat):
    return jnp.sum(upstream * xhat, axis=0), jnp.sum(upstream, axis=0)


def together(*values):
    return lax.optimization_barrier(values)


def local(
    count,
    frames,
    text,
    cotangent,
    norm_gains,
    norm_biases,
    qkv_weight,
    self_out,
    cross_query,
    cross_kv,
    cross_out,
    up_weight,
    down_weight,
):
    g = Group(count)
    clips, rows, width = frames.shape
    tokens = text.shape[1]
    part = width // 4
    held = width // count
    own_size = held // 4
    ff_rows = down_weight.shape[0] // 4
    near_rows = clips * rows
    seq = g.seq
    place = jnp.stack([jnp.asarray(PLACE, jnp.int32)[a ^ seq] for a in range(4)])
    orders = [seq ^ r for r in REL]

    def columns(weight, outer, inner):
        cut = weight.reshape(weight.shape[0], outer, 4, inner)
        return lax.dynamic_index_in_dim(cut, seq, axis=2, keepdims=False).reshape(weight.shape[0], outer * inner)

    def own_rows(weight):
        size = weight.shape[0] // 4
        return lax.dynamic_slice_in_dim(weight, seq * size, size, axis=0)

    def cut_rows(value):
        return value[:near_rows], value[near_rows : 2 * near_rows], value[2 * near_rows :]

    def piece(value, i, axis):
        return lax.dynamic_index_in_dim(value, orders[i], axis=axis, keepdims=False)

    frames_in = frames.reshape(near_rows, width)
    cot_in = cotangent.reshape(near_rows, width)
    text_in = text.reshape(clips * tokens, width)

    mix_own = jnp.stack([own_rows(self_out), own_rows(cross_query), own_rows(cross_out)])
    mix_whole = lax.all_gather(mix_own, ("dp", "seq"), axis=1, tiled=True)
    w_self, w_query, w_cross = mix_whole[0], mix_whole[1], mix_whole[2]

    norm_own = jnp.concatenate([norm_gains, norm_biases], axis=0)
    if g.paired:
        w_qkv, w_pair, both_own, frames_all, first_low, center, scale_all, cot_all, text_all, norms = opening(
            qkv_weight, cross_kv, up_weight, down_weight, frames_in, cot_in, text_in, norm_own
        )
        w_qkv, w_pair = w_qkv.reshape(width, 3 * part), w_pair.reshape(width, 2 * part)
        frames_all = frames_all.reshape(4 * near_rows, width)
        cot_all = cot_all.reshape(4 * near_rows, width)
        first_low = first_low.reshape(4 * near_rows, width)
        text_all = text_all.reshape(4 * clips * tokens, width)
        norms = norms.swapaxes(0, 1).reshape(6, width).astype(F32)
        center, scale_all = center.reshape(4 * near_rows, 128), scale_all.reshape(4 * near_rows, 128)
        gains, biases = norms[:3], norms[3:]
    else:
        w_qkv = lax.all_gather(columns(qkv_weight, 3, part), "dp", axis=0, tiled=True)
        w_pair = lax.all_gather(columns(cross_kv, 2, part), "dp", axis=0, tiled=True)
        both_own = jnp.stack([columns(up_weight, count, ff_rows), own_rows(down_weight)])

        def to_all(value):
            over = g.across(value)
            return [value, over, g.core(over), g.core(value)]

        frames_all = jnp.concatenate(to_all(frames_in), axis=0)
        cot_all = jnp.concatenate(to_all(cot_in), axis=0)
        text_all = place_pieces(to_all(text_in), orders, 0)
        norms = lax.all_gather(norm_own, "dp", axis=1, tiled=True).astype(F32)
        gains, biases = norms[:3], norms[3:]
        hat_all, _ = normalized(frames_all.astype(F32))
        first_low = (hat_all * gains[0] + biases[0]).astype(BF)
    w_both = lax.all_gather(both_own, "dp", axis=1, tiled=True)
    w_up, w_down = w_both[0], w_both[1]

    pair_part = dot_nn(text_all, w_pair).astype(BF).reshape(4 * clips * tokens, 2, part).swapaxes(0, 1)
    triple = dot_nn(first_low, w_qkv).astype(BF).reshape(4, clips, rows, 3 * part)
    triple, pair_part = together(triple, pair_part)

    pair_over, pair_near = g.across(pair_part), g.core(pair_part)
    heads_out, levels = self_forward(place, triple, part)
    heads_out, levels, pair_over, pair_near = together(heads_out, levels, pair_over, pair_near)

    pair_far = g.core(pair_over)
    heads_rows = heads_out.reshape(4, near_rows, part)
    self_mix = exchange(
        heads_to_rows_kernel, heads_rows, (near_rows, width), 2, "heads_to_rows", (near_rows, part)
    )
    pair_all = place_pieces([pair_part, pair_over, pair_far, pair_near], orders, 2).reshape(
        2, 4, clips, tokens, width
    )
    residual = frames_in.astype(F32)
    first_sum = residual + dot_nn(self_mix, w_self)
    hat_two, scale_two = normalized(first_sum)
    second_low = (hat_two * gains[1] + biases[1]).astype(BF)

    cross_q = dot_nn(second_low, w_query).astype(BF).reshape(clips, rows, width)
    cross_mix = cross_forward(cross_q, pair_all).reshape(near_rows, width)
    second_sum = first_sum + dot_nn(cross_mix, w_cross)
    hat_three, scale_three = normalized(second_sum)
    third_own = (hat_three * gains[2] + biases[2]).astype(BF)
    third_low = exchange(
        rows_to_all_kernel, third_own, (4, near_rows, width), 3, "rows_to_all"
    ).reshape(4 * near_rows, width)

    active_low, hidden_low = middle(third_low, cot_all, w_both)
    hidden_own, hidden_over, hidden_far = cut_rows(hidden_low)
    far = dot_nt(hidden_far, w_up).astype(BF)
    far, hidden_over, hidden_own, active_low = together(far, hidden_over, hidden_own, active_low)

    far = g.core(far)
    over = dot_nt(hidden_over, w_up)
    far, over, active_low, hidden_low, hidden_own = together(far, over, active_low, hidden_low, hidden_own)
    half = far.shape[0] // 2
    over = (over + far[:half].astype(F32)).astype(BF)
    over, active_low, hidden_low, hidden_own, far = together(over, active_low, hidden_low, hidden_own, far)

    crossed = g.across(over)
    down_part = dot_tn(active_low, cot_all).astype(BF)
    down_shard = lax.psum_scatter(down_part, "dp", scatter_dimension=0, tiled=True)
    half_columns = hidden_low.shape[1] // 2
    third_up = dot_nt(hidden_own, w_up) + far[half:].astype(F32)
    up_first = dot_tn(third_low, hidden_low[:, :half_columns]).astype(BF).reshape(count, held, -1)
    up_last = dot_tn(third_low, hidden_low[:, half_columns:]).astype(BF).reshape(count, held, -1)
    active_own, active_over, active_far = cut_rows(active_low)
    block_far = g.core(dot_nn(active_far, w_down).astype(BF))
    crossed, up_first, up_last, block_far, third_up, active_over, active_own = together(
        crossed, up_first, up_last, block_far, third_up, active_over, active_own
    )
    block_over = dot_nn(active_over, w_down)

    block_crossed = g.across((block_over + block_far[:half].astype(F32)).astype(BF))
    up_first = g.side_sum(up_first)
    third_up = third_up + crossed.astype(F32)
    second_grad = cot_in.astype(F32) + norm_input_grad(third_up, gains[2], hat_three, scale_three)
    gain_third, bias_third = norm_sums(third_up, hat_three)
    second_in = second_grad.astype(BF)
    mix_grad = dot_nt(second_in, w_cross).astype(BF).reshape(clips, rows, width)
    query_back, key_sums, value_sums = cross_backward(cross_q, pair_all, mix_grad)
    query_back = query_back.reshape(near_rows, width)
    second_up = dot_nt(query_back, w_query)
    first_grad = second_grad + norm_input_grad(second_up, gains[1], hat_two, scale_two)
    gain_second, bias_second = norm_sums(second_up, hat_two)
    first_in = first_grad.astype(BF)
    self_grad = dot_nt(first_in, w_self).astype(BF)
    self_grad, block_crossed, up_last, up_first, first_in, query_back = together(
        self_grad, block_crossed, up_last, up_first, first_in, query_back
    )

    up_first = g.far_sum(up_first)
    up_last = g.side_sum(up_last)
    mix_part = jnp.stack(
        [dot_tn(self_mix, first_in), dot_tn(second_low, query_back), dot_tn(cross_mix, second_in)]
    ).astype(BF)
    mix_part, self_grad = together(mix_part, self_grad)
    mix_shard = lax.psum_scatter(mix_part, ("dp", "seq"), scatter_dimension=1, tiled=True)
    flat_tokens = 4 * clips * tokens
    grads, pair_back = rows_to_heads(
        self_grad, key_sums.reshape(flat_tokens, width), value_sums.reshape(flat_tokens, width)
    )
    grads, pair_back, up_first, up_last = together(grads, pair_back, up_first, up_last)
    pair_grad = dot_tn(text_all, pair_back).astype(BF).reshape(count, held, -1)
    pair_grad, grads = together(pair_grad, grads)

    pair_sum = g.side_sum(pair_grad)
    up_last = g.far_sum(up_last)
    up_first = g.near_sum(up_first)
    triple_back = self_backward(
        place, triple, grads.reshape(4, clips, rows, part), levels, part
    ).reshape(4 * near_rows, 3 * part)
    triple_back, up_first, up_last, pair_sum = together(triple_back, up_first, up_last, pair_sum)
    pair_half = g.add(pair_sum).reshape(4, held, -1) if g.paired else None

    text_part = dot_nt(pair_back, w_pair).reshape(4, clips * tokens, width)
    text_far = g.core(jnp.stack([piece(text_part, 2, 0), piece(text_part, 3, 0)]).astype(BF))
    block_output = (
        second_sum + dot_nn(active_own, w_down) + block_far[half:].astype(F32) + block_crossed.astype(F32)
    ).astype(BF)

    def regroup_over(value):
        sends = [lax.dynamic_slice_in_dim(value, o * own_size, own_size, axis=0) for o in orders]
        return [sends[0], g.across(jnp.stack([sends[1], sends[2]])), g.core(sends[3])]

    def regroup(parts, outer, inner):
        own, over, near = parts
        out = jnp.zeros((4, own_size, outer, inner), BF)
        for one, order in zip((own, over[0], g.core(over[1]), near), orders):
            out = lax.dynamic_update_slice(out, one.reshape(1, own_size, outer, inner), (order, 0, 0, 0))
        return in_columns(out)

    def in_columns(value):
        return value.transpose(1, 2, 0, 3).reshape(value.shape[1], -1).astype(F32)

    text_crossed = g.across((piece(text_part, 1, 0) + text_far[0].astype(F32)).astype(BF))
    if g.paired:
        blank = jnp.zeros((width,), F32)
        norm_part = jnp.stack(
            [blank, gain_second, gain_third, blank, bias_second, bias_third, blank, blank]
        )
        first_up, qkv_out, pair_out, up_out, norm_all = closing(
            triple_back, w_qkv, first_low, frames_all, center, scale_all, pair_half, g.total(up_first),
            g.add(up_last), norm_part,
        )
        qkv_out, pair_out, up_out = (v.astype(F32) for v in (qkv_out, pair_out, up_out))
        norm_all = norm_all[:6]
    else:
        full = dot_nt(triple_back, w_qkv)
        own_full, over_full, far_full = cut_rows(full)
        far = g.core(far_full.astype(BF))
        crossed = g.across((over_full + far[:half].astype(F32)).astype(BF))
        first_up = own_full + far[half:].astype(F32) + crossed.astype(F32)
        qkv_part = dot_tn(first_low, triple_back).astype(BF)
        gain_first, bias_first = norm_sums(full, hat_all)
        norm_part = jnp.stack([gain_first, gain_second, gain_third, bias_first, bias_second, bias_third])
        norm_all = lax.psum(norm_part, ("dp", "seq"))
        qkv_shard = lax.psum_scatter(qkv_part.reshape(width, -1), "dp", scatter_dimension=0, tiled=True)
        qkv_out = regroup(regroup_over(qkv_shard), 3, part)
        pair_shard = lax.psum_scatter(pair_grad.reshape(width, -1), "dp", scatter_dimension=0, tiled=True)
        pair_out = regroup(regroup_over(pair_shard), 2, part)
        up_grad = jnp.concatenate([g.total(up_first), g.total(g.near_sum(up_last))], axis=-1)
        up_out = regroup(regroup_over(up_grad), count, ff_rows)
    hat_one, scale_one = normalized(residual)
    frame_grad = first_grad + norm_input_grad(first_up, gains[0], hat_one, scale_one)
    text_grad = piece(text_part, 0, 0) + text_far[1].astype(F32) + text_crossed.astype(F32)

    small = width // (4 * count)
    norm_shard = lax.dynamic_slice_in_dim(norm_all, (g.dp * 4 + seq) * small, small, axis=1)
    mix_shard = mix_shard.astype(F32)
    return (
        block_output.reshape(clips, rows, width),
        frame_grad.reshape(clips, rows, width),
        text_grad.reshape(clips, tokens, width),
        norm_shard[:3],
        norm_shard[3:],
        qkv_out,
        mix_shard[0],
        mix_shard[1],
        pair_out,
        mix_shard[2],
        up_out,
        down_shard.astype(F32),
    )


def solution(mesh):
    rows = P("dp", "seq", None)
    both = P(("dp", "seq"), None)
    return jax.shard_map(
        functools.partial(local, mesh.shape["dp"]),
        mesh=mesh,
        in_specs=(rows, rows, rows, P(None, "dp"), P(None, "dp")) + (P("dp", None),) * 7,
        out_specs=(rows, rows, rows, P(None, ("dp", "seq")), P(None, ("dp", "seq"))) + (both,) * 7,
        check_vma=False,
    )
```

```python
import functools

import jax
import jax.numpy as jnp
from jax import lax
from jax.experimental import pallas as pl
from jax.experimental.pallas import tpu as pltpu
from jax.sharding import PartitionSpec as P

HEAD_DIM = 64
EPSILON = 1e-05
NEGATIVE = -1e30
BF = jnp.bfloat16
F32 = jnp.float32

REL = (0, 2, 3, 1)
PLACE = (0, 3, 1, 2)


def dot_nn(a, b):
    return lax.dot_general(a, b, (((1,), (0,)), ((), ())), preferred_element_type=F32)


def dot_nt(a, b):
    return lax.dot_general(a, b, (((1,), (1,)), ((), ())), preferred_element_type=F32)


def dot_tn(a, b):
    return lax.dot_general(a, b, (((0,), (0,)), ((), ())), preferred_element_type=F32)


def after(value, *others):
    return lax.optimization_barrier((value,) + others)[0]


def self_forward_kernel(place_ref, q_ref, k_ref, v_ref, o_ref, l_ref):
    parts, rows = q_ref.shape[0], q_ref.shape[2]
    heads = q_ref.shape[3] // HEAD_DIM
    keys_at = lax.broadcasted_iota(jnp.int32, (rows, rows), 0)
    rows_at = lax.broadcasted_iota(jnp.int32, (rows, rows), 1)
    visible = keys_at <= rows_at
    for a in range(parts):
        here = place_ref[a]
        mixed = []
        for h in range(heads):
            cols = slice(h * HEAD_DIM, (h + 1) * HEAD_DIM)
            q = q_ref[here, 0, :, cols] * (HEAD_DIM**-0.5)
            scores = []
            for b in range(a + 1):
                s = dot_nt(k_ref[place_ref[b], 0, :, cols], q)
                if a == b:
                    s = jnp.where(visible, s, NEGATIVE)
                scores.append(s)
            top = functools.reduce(jnp.maximum, [jnp.max(s, axis=0, keepdims=True) for s in scores])
            raised = [jnp.exp(s - top) for s in scores]
            total = functools.reduce(jnp.add, [jnp.sum(e, axis=0, keepdims=True) for e in raised])
            share = 1.0 / total
            out = None
            for b in range(a + 1):
                p = (raised[b] * share).astype(BF)
                term = dot_tn(v_ref[place_ref[b], 0, :, cols], p)
                out = term if out is None else out + term
            mixed.append(out)
            l_ref[0, h, a : a + 1, :] = top + jnp.log(total)
        o_ref[here, 0] = jnp.concatenate(mixed, axis=0).T.astype(BF)


def self_forward(place, triple, width):
    parts, clips, rows, _ = triple.shape
    groups = width // 128
    block = (parts, 1, rows, 128)
    return pl.pallas_call(
        self_forward_kernel,
        out_shape=(
            jax.ShapeDtypeStruct((parts, clips, rows, width), BF),
            jax.ShapeDtypeStruct((clips, width // HEAD_DIM, parts, rows), F32),
        ),
        grid_spec=pltpu.PrefetchScalarGridSpec(
            num_scalar_prefetch=1,
            grid=(clips, groups),
            in_specs=[
                pl.BlockSpec(block, lambda i, j, p: (0, i, 0, j)),
                pl.BlockSpec(block, lambda i, j, p: (0, i, 0, groups + j)),
                pl.BlockSpec(block, lambda i, j, p: (0, i, 0, 2 * groups + j)),
            ],
            out_specs=[
                pl.BlockSpec(block, lambda i, j, p: (0, i, 0, j)),
                pl.BlockSpec((1, 2, parts, rows), lambda i, j, p: (i, j, 0, 0)),
            ],
        ),
        compiler_params=pltpu.CompilerParams(vmem_limit_bytes=40 << 20),
        cost_estimate=pl.CostEstimate(
            flops=clips * width * rows * rows * 10 * 4,
            bytes_accessed=clips * rows * parts * width * 8,
            transcendentals=clips * (width // HEAD_DIM) * rows * rows * 10,
        ),
        name="self_forward",
    )(place, triple, triple, triple)


def self_backward_kernel(place_ref, q_ref, k_ref, v_ref, g_ref, l_ref, out_ref, gk_ref, gv_ref):
    parts, rows = q_ref.shape[0], q_ref.shape[2]
    heads = q_ref.shape[3] // HEAD_DIM
    width = out_ref.shape[3] // 3
    scale = HEAD_DIM**-0.5
    column = pl.multiple_of(pl.program_id(1) * 128, 128)
    keys_at = lax.broadcasted_iota(jnp.int32, (rows, rows), 0)
    rows_at = lax.broadcasted_iota(jnp.int32, (rows, rows), 1)
    visible = keys_at <= rows_at
    for a in range(parts):
        here = place_ref[a]
        grads_q = []
        for h in range(heads):
            cols = slice(h * HEAD_DIM, (h + 1) * HEAD_DIM)
            q = q_ref[here, 0, :, cols] * scale
            grad = g_ref[here, 0, :, cols]
            level = l_ref[0, h, a : a + 1, :]
            probs, slopes = [], []
            inner = None
            for b in range(a + 1):
                s = dot_nt(k_ref[place_ref[b], 0, :, cols], q)
                if a == b:
                    s = jnp.where(visible, s, NEGATIVE)
                p = jnp.exp(s - level)
                dp = dot_nt(v_ref[place_ref[b], 0, :, cols], grad)
                term = jnp.sum(p * dp, axis=0, keepdims=True)
                inner = term if inner is None else inner + term
                probs.append(p)
                slopes.append(dp)
            gq = None
            for b in range(a + 1):
                ds = (probs[b] * (slopes[b] - inner)).astype(BF)
                term = dot_tn(k_ref[place_ref[b], 0, :, cols], ds)
                gq = term if gq is None else gq + term
                gk = dot_nn(ds, q)
                gv = dot_nn(probs[b].astype(BF), grad)
                if a == b:
                    gk_ref[b, :, cols] = gk
                    gv_ref[b, :, cols] = gv
                else:
                    gk_ref[b, :, cols] += gk
                    gv_ref[b, :, cols] += gv
            grads_q.append(gq * scale)
        out_ref[here, 0, :, pl.ds(column, 128)] = jnp.concatenate(grads_q, axis=0).T.astype(BF)
    for b in range(parts):
        here = place_ref[b]
        out_ref[here, 0, :, pl.ds(width + column, 128)] = gk_ref[b].astype(BF)
        out_ref[here, 0, :, pl.ds(2 * width + column, 128)] = gv_ref[b].astype(BF)


def self_backward(place, triple, grads, levels, width):
    parts, clips, rows, _ = triple.shape
    groups = width // 128
    block = (parts, 1, rows, 128)
    return pl.pallas_call(
        self_backward_kernel,
        out_shape=jax.ShapeDtypeStruct((parts, clips, rows, 3 * width), BF),
        grid_spec=pltpu.PrefetchScalarGridSpec(
            num_scalar_prefetch=1,
            grid=(clips, groups),
            in_specs=[
                pl.BlockSpec(block, lambda i, j, p: (0, i, 0, j)),
                pl.BlockSpec(block, lambda i, j, p: (0, i, 0, groups + j)),
                pl.BlockSpec(block, lambda i, j, p: (0, i, 0, 2 * groups + j)),
                pl.BlockSpec(block, lambda i, j, p: (0, i, 0, j)),
                pl.BlockSpec((1, 2, parts, rows), lambda i, j, p: (i, j, 0, 0)),
            ],
            out_specs=pl.BlockSpec((parts, 1, rows, 3 * width), lambda i, j, p: (0, i, 0, 0)),
            scratch_shapes=[
                pltpu.VMEM((parts, rows, 128), F32),
                pltpu.VMEM((parts, rows, 128), F32),
            ],
        ),
        compiler_params=pltpu.CompilerParams(vmem_limit_bytes=48 << 20),
        cost_estimate=pl.CostEstimate(
            flops=clips * width * rows * rows * 10 * 10,
            bytes_accessed=clips * rows * parts * width * 14,
            transcendentals=clips * (width // HEAD_DIM) * rows * rows * 10,
        ),
        name="self_backward",
    )(place, triple, triple, triple, grads, levels)


def cross_forward_kernel(q_ref, k_ref, v_ref, o_ref):
    width = q_ref.shape[2]
    def run(pair, carry):
        span = pl.ds(pl.multiple_of(pair * 128, 128), 128)
        k_all = k_ref[0, :, 0, :, span].reshape(-1, 128)
        v_all = v_ref[0, :, 0, :, span].reshape(-1, 128)
        q_all = q_ref[0, :, span]
        mixed = []
        for h in range(2):
            cols = slice(h * HEAD_DIM, (h + 1) * HEAD_DIM)
            s = dot_nt(k_all[:, cols], q_all[:, cols] * (HEAD_DIM**-0.5))
            e = jnp.exp(s - jnp.max(s, axis=0, keepdims=True))
            p = e * (1.0 / jnp.sum(e, axis=0, keepdims=True))
            mixed.append(dot_tn(v_all[:, cols], p.astype(BF)))
        o_ref[0, :, span] = jnp.concatenate(mixed, axis=0).T.astype(BF)
        return carry

    lax.fori_loop(0, width // 128, run, 0, unroll=2)


def cross_forward(query, text_kv):
    clips, rows, width = query.shape
    _, parts, _, tokens, _ = text_kv.shape
    step = 512
    groups = width // step
    return pl.pallas_call(
        cross_forward_kernel,
        out_shape=jax.ShapeDtypeStruct(query.shape, BF),
        grid=(clips, groups),
        in_specs=[
            pl.BlockSpec((1, rows, step), lambda i, j: (i, 0, j)),
            pl.BlockSpec((1, parts, 1, tokens, step), lambda i, j: (0, 0, i, 0, j)),
            pl.BlockSpec((1, parts, 1, tokens, step), lambda i, j: (1, 0, i, 0, j)),
        ],
        out_specs=pl.BlockSpec((1, rows, step), lambda i, j: (i, 0, j)),
        cost_estimate=pl.CostEstimate(
            flops=clips * rows * width * parts * tokens * 4,
            bytes_accessed=clips * rows * width * 4,
            transcendentals=clips * rows * parts * tokens * (width // HEAD_DIM),
        ),
        name="cross_forward",
    )(query, text_kv, text_kv)


def cross_backward_kernel(q_ref, k_ref, v_ref, g_ref, gq_ref, gk_ref, gv_ref):
    width = q_ref.shape[2]
    _, parts, _, tokens, _ = k_ref.shape
    scale = HEAD_DIM**-0.5
    k_all = k_ref[0, :, 0].reshape(-1, width)
    v_all = v_ref[0, :, 0].reshape(-1, width)
    for pair in range(width // 128):
        rows_q, rows_k, rows_v = [], [], []
        for h in (2 * pair, 2 * pair + 1):
            cols = slice(h * HEAD_DIM, (h + 1) * HEAD_DIM)
            q = q_ref[0, :, cols] * scale
            grad = g_ref[0, :, cols]
            s = dot_nt(k_all[:, cols], q)
            e = jnp.exp(s - jnp.max(s, axis=0, keepdims=True))
            p = e * (1.0 / jnp.sum(e, axis=0, keepdims=True))
            dp = dot_nt(v_all[:, cols], grad)
            inner = jnp.sum(p * dp, axis=0, keepdims=True)
            ds = (p * (dp - inner)).astype(BF)
            rows_q.append(dot_tn(k_all[:, cols], ds) * scale)
            rows_k.append(dot_nn(ds, q))
            rows_v.append(dot_nn(p.astype(BF), grad))
        span = slice(pair * 128, (pair + 1) * 128)
        gq_ref[0, :, span] = jnp.concatenate(rows_q, axis=0).T.astype(BF)
        gk_ref[:, 0, :, span] = jnp.concatenate(rows_k, axis=1).reshape(parts, tokens, 128)
        gv_ref[:, 0, :, span] = jnp.concatenate(rows_v, axis=1).reshape(parts, tokens, 128)


def cross_backward(query, text_kv, grads):
    clips, rows, width = query.shape
    _, parts, _, tokens, _ = text_kv.shape
    step = 512
    groups = width // step
    row_spec = pl.BlockSpec((1, rows, step), lambda i, j: (i, 0, j))
    text_block = (parts, 1, tokens, step)
    return pl.pallas_call(
        cross_backward_kernel,
        out_shape=(
            jax.ShapeDtypeStruct(query.shape, BF),
            jax.ShapeDtypeStruct((parts, clips, tokens, width), F32),
            jax.ShapeDtypeStruct((parts, clips, tokens, width), F32),
        ),
        grid=(clips, groups),
        in_specs=[
            row_spec,
            pl.BlockSpec((1,) + text_block, lambda i, j: (0, 0, i, 0, j)),
            pl.BlockSpec((1,) + text_block, lambda i, j: (1, 0, i, 0, j)),
            row_spec,
        ],
        out_specs=[
            row_spec,
            pl.BlockSpec(text_block, lambda i, j: (0, i, 0, j)),
            pl.BlockSpec(text_block, lambda i, j: (0, i, 0, j)),
        ],
        cost_estimate=pl.CostEstimate(
            flops=clips * rows * width * parts * tokens * 10,
            bytes_accessed=clips * rows * width * 6,
            transcendentals=clips * rows * parts * tokens * (width // HEAD_DIM),
        ),
        name="cross_backward",
    )(query, text_kv, text_kv, grads)


def gelu_and_slope(v):
    phi = 0.5 + 0.5 * lax.erf(v * (0.5**0.5))
    density = jnp.exp(-0.5 * v * v) * (2.0 * jnp.pi) ** -0.5
    return v * phi, phi + v * density


def middle_kernel(x_ref, c_ref, up_ref, down_ref, act_ref, grad_ref):
    active, slope = gelu_and_slope(dot_nn(x_ref[...], up_ref[...]))
    act_ref[...] = active.astype(BF)
    grad_ref[...] = (dot_nt(c_ref[...], down_ref[...]) * slope).astype(BF)


def middle(normed, cotangent, both):
    rows, width = normed.shape
    hidden = both.shape[2]
    tile_r, tile_h = min(512, rows), min(512, hidden)
    row_spec = pl.BlockSpec((tile_r, width), lambda j, i: (i, 0))
    out_spec = pl.BlockSpec((tile_r, tile_h), lambda j, i: (i, j))
    shape = jax.ShapeDtypeStruct((rows, hidden), BF)
    return pl.pallas_call(
        middle_kernel,
        out_shape=(shape, shape),
        grid=(hidden // tile_h, rows // tile_r),
        in_specs=[
            row_spec,
            row_spec,
            pl.BlockSpec((None, width, tile_h), lambda j, i: (0, 0, j)),
            pl.BlockSpec((None, tile_h, width), lambda j, i: (1, j, 0)),
        ],
        out_specs=(out_spec, out_spec),
        compiler_params=pltpu.CompilerParams(vmem_limit_bytes=40 << 20),
        cost_estimate=pl.CostEstimate(
            flops=4 * rows * width * hidden,
            bytes_accessed=4 * rows * width * 3 + 4 * width * hidden + 4 * rows * hidden,
            transcendentals=2 * rows * hidden,
        ),
        name="middle",
    )(normed, cotangent, both, both)


def place_kernel(count, axis, starts_ref, *refs):
    pieces, out_ref, sems = refs[:count], refs[count], refs[count + 1]
    copies = []
    for i in range(count):
        size = pieces[i].shape[axis]
        where = [slice(None)] * len(out_ref.shape)
        where[axis] = pl.ds(pl.multiple_of(starts_ref[i] * size, size), size)
        copies.append(pltpu.make_async_copy(pieces[i], out_ref.at[tuple(where)], sems.at[i]))
    for copy in copies:
        copy.start()
    for copy in copies:
        copy.wait()


def place_pieces(pieces, starts, axis):
    shape = list(pieces[0].shape)
    shape[axis] *= len(pieces)
    any_spec = pl.BlockSpec(memory_space=pl.ANY)
    size = pieces[0].size * len(pieces) * pieces[0].dtype.itemsize
    return pl.pallas_call(
        functools.partial(place_kernel, len(pieces), axis),
        out_shape=jax.ShapeDtypeStruct(tuple(shape), pieces[0].dtype),
        in_specs=[pl.BlockSpec(memory_space=pltpu.SMEM)]
        + [pl.BlockSpec(memory_space=pltpu.VMEM)] * len(pieces),
        out_specs=any_spec,
        scratch_shapes=[pltpu.SemaphoreType.DMA((len(pieces),))],
        compiler_params=pltpu.CompilerParams(vmem_limit_bytes=2 * size + (4 << 20)),
        cost_estimate=pl.CostEstimate(flops=0, bytes_accessed=2 * size, transcendentals=0),
        name="place_pieces",
    )(jnp.stack([jnp.asarray(s, jnp.int32) for s in starts]), *pieces)


class Group:
    def __init__(self, count):
        self.count = count
        self.dp = lax.axis_index("dp")
        self.seq = lax.axis_index("seq")
        self.bits = (self.dp // 4, self.dp // 2 % 2, self.dp % 2)
        self.paired = count == 8

    def core(self, value):
        return lax.ppermute(value, "seq", [(i, i ^ 1) for i in range(4)])

    def across(self, value):
        return lax.ppermute(value, "seq", [(i, i ^ 2) for i in range(4)])

    def swap(self, value, bit):
        return lax.ppermute(value, "dp", [(i, i ^ bit) for i in range(self.count)])


    def halve(self, value, axis, place, bit):
        away = lax.dynamic_index_in_dim(value, 1 - place, axis=axis, keepdims=False)
        kept = lax.dynamic_index_in_dim(value, place, axis=axis, keepdims=False)
        return kept, self.swap(away, bit)

    def add(self, pair):
        return (pair[0].astype(F32) + pair[1].astype(F32)).astype(BF)

    def side_sum(self, value):
        if not self.paired:
            return value.reshape((-1,) + value.shape[2:]), None
        return self.halve(value.reshape((2, 2, 2) + value.shape[1:]), 2, self.bits[2], 1)

    def far_sum(self, pair):
        if not self.paired:
            return pair
        return self.halve(self.add(pair), 0, self.bits[0], 4)

    def near_sum(self, pair):
        if not self.paired:
            return lax.psum_scatter(pair[0], "dp", scatter_dimension=0, tiled=True), None
        return self.halve(self.add(pair), 0, self.bits[1], 2)

    def total(self, pair):
        return self.add(pair) if self.paired else pair[0]

    def sum_all_small(self, value):
        if not self.paired:
            return lax.psum(value, ("dp", "seq"))
        value = value + self.core(value)
        value = value + self.across(value)
        for bit in (1, 2, 4):
            value = value + self.swap(value, bit)
        return value


MESH = pl.DeviceIdType.MESH


def flip(index, bits):
    for bit in (1, 2, 4):
        if bits & bit:
            index = index + bit - 2 * bit * (index // bit % 2)
    return index


class Sender:
    def __init__(self, send, recv):
        self.send, self.recv, self.used = send, recv, 0
        self.dp, self.seq = lax.axis_index("dp"), lax.axis_index("seq")
        self.open = []

    def greet(self, dp_bits, seq_bits):
        self.call(dp_bits, seq_bits)
        self.meet()

    def call(self, dp_bits, seq_bits):
        self.peers = [self.peer(d, 0) for d in dp_bits] + [self.peer(0, s) for s in seq_bits]
        for peer in self.peers:
            pl.semaphore_signal(
                pltpu.get_barrier_semaphore(), inc=1, device_id=peer, device_id_type=MESH
            )

    def meet(self):
        pl.semaphore_wait(pltpu.get_barrier_semaphore(), len(self.peers))

    def peer(self, dp_bits, seq_bits):
        return (flip(self.dp, dp_bits), flip(self.seq, seq_bits))

    def copy(self, src, dst, dp_bits=0, seq_bits=0):
        one = pltpu.make_async_remote_copy(
            src_ref=src,
            dst_ref=dst,
            send_sem=self.send.at[self.used],
            recv_sem=self.recv.at[self.used],
            device_id=self.peer(dp_bits, seq_bits),
            device_id_type=MESH,
        )
        self.used += 1
        one.start()
        self.open.append(one)
        return one


def opening_kernel(
    qkv_ref, kv_ref, up_ref, down_ref, frames_ref, text_ref, norm_ref,
    w_ref, p_ref, both_ref, fa_ref, low_ref, mean_ref, scale_ref, ta_ref, na_ref,
    gain_ref, local_sem, send, recv,
):
    s = Sender(send, recv)
    dp, seq = s.dp, s.seq
    held = norm_ref.shape[1]
    part = w_ref.shape[2] // 3
    own = both_ref.shape[1]
    loads = []

    def load(src, dst):
        loads.append(pltpu.make_async_copy(src, dst, local_sem.at[len(loads)]))
        loads[-1].start()

    for i in range(3):
        at = pl.ds(pl.multiple_of((4 * i + seq) * part, 128), part)
        load(qkv_ref.at[:, at], w_ref.at[dp, :, i * part : (i + 1) * part])
    for i in range(2):
        at = pl.ds(pl.multiple_of((4 * i + seq) * part, 128), part)
        load(kv_ref.at[:, at], p_ref.at[dp, :, i * part : (i + 1) * part])
    load(down_ref.at[pl.ds(pl.multiple_of(seq * own, own), own)], both_ref.at[1])
    s.greet((1, 2, 3, 4, 5, 6, 7), (1, 2))
    over = s.copy(frames_ref, fa_ref.at[1], 0, 2)
    near = s.copy(frames_ref, fa_ref.at[3], 0, 1)
    for one in loads:
        one.wait()

    chunks = []
    for ref, count in ((w_ref, 3), (p_ref, 2)):
        rows = ref.shape[1] // count
        chunks += [(ref, pl.ds(j * rows, rows)) for j in range(count)]

    def along(j):
        ref, cut = chunks[j]
        return [s.copy(ref.at[dp, cut], ref.at[dp, cut], k) for k in (4, 6, 2)]

    line = [along(0)]
    side = [s.copy(ref.at[dp], ref.at[dp], 1) for ref in (w_ref, p_ref)]
    norms = [s.copy(norm_ref, na_ref.at[dp], k) for k in (1, 2, 3, 4, 5, 6, 7)]
    text_over = s.copy(text_ref, ta_ref.at[seq], 0, 2)
    text_near = s.copy(text_ref, ta_ref.at[seq], 0, 1)
    fa_ref[0] = frames_ref[...]
    ta_ref[seq] = text_ref[...]
    na_ref[dp] = norm_ref[...]
    for k in range(4):

        @pl.when(seq == k)
        def _():
            for d in range(up_ref.shape[1] // (4 * own)):
                at = (4 * d + k) * own
                both_ref[0, :, d * own : (d + 1) * own] = up_ref[:, at : at + own]

    def normalize(slot):
        def run(i, carry):
            cut = pl.ds(pl.multiple_of(i * 32, 32), 32)
            x = fa_ref[slot, cut].astype(F32)
            center = jnp.mean(x, axis=-1, keepdims=True)
            x = x - center
            scale = lax.rsqrt(jnp.mean(x * x, axis=-1, keepdims=True) + EPSILON)
            low_ref[slot, cut] = (x * scale * gain_ref[0:1] + gain_ref[3:4]).astype(BF)
            mean_ref[slot, cut] = jnp.broadcast_to(center, (32, 128))
            scale_ref[slot, cut] = jnp.broadcast_to(scale, (32, 128))
            return carry

        lax.fori_loop(0, fa_ref.shape[1] // 32, run, 0)

    waited = []
    for j, (ref, cut) in enumerate(chunks):
        if j + 1 < len(chunks):
            for one in line[j]:
                one.wait_send()
            waited += line[j]
            line.append(along(j + 1))
        for k, one in zip((4, 6, 2), line[j]):
            one.wait_recv()
            at = flip(dp, k)
            side.append(s.copy(ref.at[at, cut], ref.at[at, cut], 1))
        if j == 0:
            for one in norms:
                one.wait_recv()
            for d in range(na_ref.shape[0]):
                gain_ref[:, d * held : (d + 1) * held] = na_ref[d].astype(F32)
            normalize(0)
            near.wait_recv()
            normalize(3)
        if j == 2:
            over.wait_recv()
            far = s.copy(fa_ref.at[1], fa_ref.at[2], 0, 1)
            normalize(1)
            text_over.wait_recv()
            at = flip(seq, 2)
            text_far = s.copy(ta_ref.at[at], ta_ref.at[at], 0, 1)
            far.wait_recv()
            normalize(2)
    for one in side + [text_near, text_far]:
        one.wait_recv()
    for one in s.open:
        if not any(one is other for other in waited):
            one.wait_send()


def opening(qkv, kv, up, down, frames, text, norms):
    vmem = pl.BlockSpec(memory_space=pltpu.VMEM)
    hbm = pl.BlockSpec(memory_space=pl.ANY)
    count = 8
    copies = 3 * 5 + 2 + 3 * 5 + 6 + 7
    held = qkv.shape[0]
    four = (4,) + frames.shape
    bf = [
        (count, held, qkv.shape[1] // 4),
        (count, held, kv.shape[1] // 4),
        (2, down.shape[0] // 4, down.shape[1]),
        four,
        four,
    ]
    shapes = [jax.ShapeDtypeStruct(sh, BF) for sh in bf]
    shapes += [jax.ShapeDtypeStruct(four[:2] + (128,), F32)] * 2
    shapes += [jax.ShapeDtypeStruct(sh, BF) for sh in ((4,) + text.shape, (count,) + norms.shape)]
    return pl.pallas_call(
        opening_kernel,
        out_shape=shapes,
        in_specs=[hbm, hbm, vmem, hbm] + [vmem] * 3,
        out_specs=[vmem] * len(shapes),
        scratch_shapes=[
            pltpu.VMEM((6, count * held), F32),
            pltpu.SemaphoreType.DMA((6,)),
            pltpu.SemaphoreType.DMA((copies,)),
            pltpu.SemaphoreType.DMA((copies,)),
        ],
        compiler_params=pltpu.CompilerParams(
            collective_id=0, has_side_effects=True, vmem_limit_bytes=52 << 20
        ),
        cost_estimate=pl.CostEstimate(flops=0, bytes_accessed=300 << 20, transcendentals=0),
        name="opening",
    )(qkv, kv, up, down, frames, text, norms)


def exchange(kernel, value, shape, number, name, stage=None):
    vmem = pl.BlockSpec(memory_space=pltpu.VMEM)
    copies = 6
    return pl.pallas_call(
        kernel,
        out_shape=jax.ShapeDtypeStruct(shape, value.dtype),
        in_specs=[vmem],
        out_specs=vmem,
        scratch_shapes=([] if stage is None else [pltpu.VMEM(stage, value.dtype)])
        + [pltpu.SemaphoreType.DMA((copies,)), pltpu.SemaphoreType.DMA((copies,))],
        compiler_params=pltpu.CompilerParams(
            collective_id=number, has_side_effects=True, vmem_limit_bytes=24 << 20
        ),
        cost_estimate=pl.CostEstimate(flops=0, bytes_accessed=80 << 20, transcendentals=0),
        name=name,
    )(value)


def rows_to_all_kernel(x_ref, cot_ref, over_ref, out_ref, all_ref, send, recv):
    s = Sender(send, recv)
    half = x_ref.shape[0] // 2
    cuts = [pl.ds(0, half), pl.ds(half, half)]
    s.greet((), (1, 2))
    over = [s.copy(x_ref.at[cut], out_ref.at[1, cut], 0, 2) for cut in cuts]
    near = s.copy(x_ref, out_ref.at[3], 0, 1)
    cots = [s.copy(cot_ref, all_ref.at[3], 0, 1), s.copy(over_ref, all_ref.at[2], 0, 1)]
    out_ref[0] = x_ref[...]
    all_ref[0] = cot_ref[...]
    all_ref[1] = over_ref[...]
    far = []
    for one, cut in zip(over, cuts):
        one.wait_recv()
        far.append(s.copy(out_ref.at[1, cut], out_ref.at[2, cut], 0, 1))
    for one in [near] + cots + far:
        one.wait_recv()
    for one in s.open:
        one.wait_send()


def rows_to_all(value, cot, over):
    vmem = pl.BlockSpec(memory_space=pltpu.VMEM)
    copies = 7
    shape = jax.ShapeDtypeStruct((4,) + value.shape, BF)
    return pl.pallas_call(
        rows_to_all_kernel,
        out_shape=[shape, shape],
        in_specs=[vmem] * 3,
        out_specs=[vmem] * 2,
        scratch_shapes=[pltpu.SemaphoreType.DMA((copies,)), pltpu.SemaphoreType.DMA((copies,))],
        compiler_params=pltpu.CompilerParams(
            collective_id=3, has_side_effects=True, vmem_limit_bytes=32 << 20
        ),
        cost_estimate=pl.CostEstimate(flops=0, bytes_accessed=80 << 20, transcendentals=0),
        name="rows_to_all",
    )(value, cot, over)


def heads_to_rows_kernel(x_ref, out_ref, stage_ref, send, recv):
    s = Sender(send, recv)
    seq = s.seq
    part = x_ref.shape[2]
    s.greet((), (1, 2))

    def at(owner):
        return (slice(None), pl.ds(pl.multiple_of(owner * part, 128), part))

    relayed = s.copy(x_ref.at[2], stage_ref, 0, 2)
    over = s.copy(x_ref.at[1], out_ref.at[at(seq)], 0, 2)
    near = s.copy(x_ref.at[3], out_ref.at[at(seq)], 0, 1)
    out_ref[at(seq)] = x_ref[0]
    relayed.wait_recv()
    far = s.copy(stage_ref, out_ref.at[at(flip(seq, 2))], 0, 1)
    for one in (near, over, far):
        one.wait_recv()
    for one in s.open:
        one.wait_send()


def rows_to_heads_kernel(
    x_ref, key_ref, value_ref, act_ref, both_ref, second_ref, far_ref, crossed_ref,
    out_ref, pair_ref, block_ref,
    stage_ref, low_ref, got_ref, add_ref, last_ref, act_in, w_in, far_in, local_sem, send, recv,
):
    s = Sender(send, recv)
    near = pl.ds(0, x_ref.shape[0])
    loads = [
        pltpu.make_async_copy(act_ref.at[near], act_in, local_sem.at[0]),
        pltpu.make_async_copy(both_ref.at[1], w_in, local_sem.at[1]),
        pltpu.make_async_copy(far_ref.at[pl.ds(x_ref.shape[0], x_ref.shape[0])], far_in, local_sem.at[2]),
    ]
    for one in loads:
        one.start()
    seq = s.seq
    part = out_ref.shape[2]

    def at(owner):
        return (slice(None), pl.ds(pl.multiple_of(owner * part, 128), part))

    sums = (key_ref, value_ref)
    for t in range(2):
        low_ref[t, 0] = sums[t][at(flip(seq, 3))].astype(BF)
        low_ref[t, 1] = sums[t][at(flip(seq, 1))].astype(BF)
    s.greet((), (1, 2))
    pair_near = [s.copy(low_ref.at[t], got_ref.at[t], 0, 1) for t in range(2)]
    relayed = s.copy(x_ref.at[at(flip(seq, 3))], stage_ref, 0, 2)
    near = s.copy(x_ref.at[at(flip(seq, 1))], out_ref.at[3], 0, 1)
    for t in range(2):
        pair_near[t].wait_recv()
        add_ref[t] = (sums[t][at(flip(seq, 2))] + got_ref[t, 0].astype(F32)).astype(BF)
    pair_over = s.copy(add_ref, last_ref, 0, 2)
    over = s.copy(x_ref.at[at(flip(seq, 2))], out_ref.at[1], 0, 2)
    out_ref[0] = x_ref[at(seq)]
    for one in loads:
        one.wait()

    def block(cut):
        value = second_ref[cut] + dot_nn(act_in[cut], w_in[...])
        value = value + far_in[cut].astype(F32) + crossed_ref[cut].astype(F32)
        block_ref[cut] = value.astype(BF)

    by_rows(x_ref.shape[0], 256, block)
    relayed.wait_recv()
    far = s.copy(stage_ref, out_ref.at[2], 0, 1)
    pair_over.wait_recv()
    for t in range(2):
        total = sums[t][at(seq)] + got_ref[t, 1].astype(F32) + last_ref[t].astype(F32)
        pair_ref[:, t * part : (t + 1) * part] = total.astype(BF)
    for one in (near, over, far):
        one.wait_recv()
    for one in s.open:
        one.wait_send()


def rows_to_heads(value, keys, values, active, both, second, far, crossed):
    rows, width = value.shape
    part = width // 4
    tokens = keys.shape[0]
    vmem = pl.BlockSpec(memory_space=pltpu.VMEM)
    hbm = pl.BlockSpec(memory_space=pl.ANY)
    copies = 7
    return pl.pallas_call(
        rows_to_heads_kernel,
        out_shape=[
            jax.ShapeDtypeStruct((4, rows, part), BF),
            jax.ShapeDtypeStruct((tokens, 2 * part), BF),
            jax.ShapeDtypeStruct((rows, width), BF),
        ],
        in_specs=[vmem] * 3 + [hbm, hbm, vmem, hbm, vmem],
        out_specs=[vmem] * 3,
        scratch_shapes=[
            pltpu.VMEM((rows, part), BF),
            pltpu.VMEM((2, 2, tokens, part), BF),
            pltpu.VMEM((2, 2, tokens, part), BF),
            pltpu.VMEM((2, tokens, part), BF),
            pltpu.VMEM((2, tokens, part), BF),
            pltpu.VMEM((rows, width), BF),
            pltpu.VMEM((width, width), BF),
            pltpu.VMEM((rows, width), BF),
            pltpu.SemaphoreType.DMA((3,)),
            pltpu.SemaphoreType.DMA((copies,)),
            pltpu.SemaphoreType.DMA((copies,)),
        ],
        compiler_params=pltpu.CompilerParams(
            collective_id=4, has_side_effects=True, vmem_limit_bytes=40 << 20
        ),
        cost_estimate=pl.CostEstimate(flops=0, bytes_accessed=80 << 20, transcendentals=0),
        name="rows_to_heads",
    )(value, keys, values, active, both, second, far, crossed)


def by_rows(total, step, body):
    def run(i, carry):
        body(pl.ds(pl.multiple_of(i * step, step), step))
        return carry

    lax.fori_loop(0, total // step, run, 0)


def closing_kernel(
    back_ref, w_from, low_ref, fa_from, mean_from, scale_from, pair_ref, first_ref, last_ref, norm_ref, norms_ref,
    up_ref, qkv_out, pair_out, grown_out, norm_out,
    far_send, far_in, over_send, over_in, norm_own, norm_seq, norm_mid, norm_dp,
    qkv_ref, side, total, line, whole, qkv_got, pair_line, pair_whole, pair_got, last_in, grown_ref, grown_got,
    w_ref, fa_ref, mean_ref, scale_ref, local_sem, send, recv,
):
    s = Sender(send, recv)
    s.call((1, 2, 3, 4, 5, 6, 7), (1, 2, 3))
    loads = [
        pltpu.make_async_copy(a, b, local_sem.at[i])
        for i, (a, b) in enumerate(
            (
                (w_from, w_ref), (fa_from, fa_ref), (mean_from, mean_ref), (scale_from, scale_ref),
            )
        )
    ]
    for one in loads:
        one.start()
    dp, seq = s.dp, s.seq
    order = (4, 6, 2, 0)
    low_bit = dp // 2 % 2
    near_rows = up_ref.shape[0]
    held = side.shape[1]
    tile = 128

    def compute_block(i):
        block = flip(dp, order[i]) // 2
        at = pl.ds(pl.multiple_of(block * 2 * held, 128), 2 * held)
        third = back_ref.shape[1] // 3

        def run(j, carry):
            across = pl.ds(pl.multiple_of(j * third, 128), third)
            qkv_ref[i, :, across] = dot_tn(low_ref[:, at], back_ref[:, across]).astype(BF)
            return carry

        lax.fori_loop(0, 3, run, 0)

    def to_side(i):
        rows = pl.ds(pl.multiple_of((1 - dp % 2) * held, held), held)
        return s.copy(qkv_ref.at[i, rows], side.at[i], 1)

    compute_block(0)
    s.meet()
    started = [to_side(0)]
    last_copy = s.copy(last_ref.at[1 - low_bit], last_in, 2)
    pair_copies = [s.copy(pair_ref.at[flip(dp, order[i]) // 2], pair_line.at[i], order[i]) for i in range(3)]
    norm_own[...] = norm_ref[...]
    norm_own[0:1] = jnp.zeros_like(norm_own[0:1])
    norm_own[3:4] = jnp.zeros_like(norm_own[3:4])

    def product(first, count, store):
        def run(i, carry):
            at = pl.ds(pl.multiple_of(first + i * tile, tile), tile)
            u = dot_nt(back_ref[at], w_ref[...])
            hat = (fa_ref[at].astype(F32) - mean_ref[at][:, :1]) * scale_ref[at][:, :1]
            norm_own[0:1] += jnp.sum(u * hat, axis=0, keepdims=True)
            norm_own[3:4] += jnp.sum(u, axis=0, keepdims=True)
            store(i, u)
            return carry

        lax.fori_loop(0, count // tile, run, 0)

    def cut_at(i):
        return pl.ds(pl.multiple_of(i * tile, tile), tile)

    def store_far(i, u):
        far_send[cut_at(i)] = u.astype(BF)

    compute_block(1)
    started.append(to_side(1))
    for one in loads:
        one.wait()
    product(2 * near_rows, 2 * near_rows, store_far)
    far = [
        s.copy(far_send.at[pl.ds(i * near_rows, near_rows)], far_in.at[pl.ds(i * near_rows, near_rows)], 0, 1)
        for i in range(2)
    ]

    far[0].wait_recv()

    def store_over(i, u):
        at = cut_at(i)
        over_send[at] = (u + far_in[at].astype(F32)).astype(BF)

    product(near_rows, near_rows, store_over)
    crossed = s.copy(over_send, over_in, 0, 2)
    compute_block(2)

    def regroup(value, got):
        size = got.shape[1]
        moves = []
        for k in (2, 3, 1):
            rows = pl.ds(pl.multiple_of(flip(seq, k) * size, size), size)
            moves.append(s.copy(value.at[rows], got.at[seq], 0, k))
        got[seq] = value[pl.ds(pl.multiple_of(seq * size, size), size)]
        return moves

    def in_columns(got, out, outer):
        inner = got.shape[2] // outer
        for j in range(outer):
            for k in range(4):
                at = (4 * j + k) * inner
                out[:, at : at + inner] = got[k, :, j * inner : (j + 1) * inner]

    far[1].wait_recv()

    def store_own(i, u):
        at = cut_at(i)
        below = pl.ds(pl.multiple_of(near_rows + i * tile, tile), tile)
        up_ref[at] = u + far_in[below].astype(F32)

    product(0, near_rows, store_own)
    norm_copies = [s.copy(norm_own, norm_seq.at[k - 1], 0, k) for k in (1, 2, 3)]
    line_copies = []
    norm_dp_copies = []
    for i in range(4):
        started[i].wait_recv()
        if i + 2 < 4:
            started.append(to_side(i + 2))
        if i == 0:
            compute_block(3)
        offset = dp % 2 * held

        def add(cut):
            mine = qkv_ref[i, pl.ds(pl.multiple_of(offset + cut.start, 48), cut.size)]
            total[i, cut] = (mine.astype(F32) + side[i, cut].astype(F32)).astype(BF)

        by_rows(held, 48, add)
        if i < 3:
            line_copies.append(s.copy(total.at[i], line.at[i], order[i]))
        if i == 1:
            for one in norm_copies:
                one.wait_recv()
            norm_mid[...] = norm_own[...] + norm_seq[0] + norm_seq[1] + norm_seq[2]
            norm_dp_copies = [s.copy(norm_mid, norm_dp.at[k - 1], k) for k in range(1, 8)]
    last_copy.wait_recv()
    columns = first_ref.shape[1]

    def add_last(cut):
        grown_ref[cut, :columns] = first_ref[cut]
        grown_ref[cut, columns:] = (last_ref[low_bit, cut].astype(F32) + last_in[cut].astype(F32)).astype(BF)

    by_rows(held, 48, add_last)
    moved = [regroup(grown_ref, grown_got)]
    for one in pair_copies:
        one.wait_recv()

    def add_pair(cut):
        value = pair_ref[dp // 2, cut].astype(F32)
        for i in range(3):
            value = value + pair_line[i, cut].astype(F32)
        pair_whole[cut] = value.astype(BF)

    by_rows(held, 48, add_pair)
    moved.append(regroup(pair_whole, pair_got))
    crossed.wait_recv()

    def add_up(cut):
        hat = (fa_ref[cut].astype(F32) - mean_ref[cut][:, :1]) * scale_ref[cut][:, :1]
        weighted = (up_ref[cut] + over_in[cut].astype(F32)) * norms_ref[0:1]
        first = jnp.mean(weighted, axis=-1, keepdims=True)
        second = jnp.mean(weighted * hat, axis=-1, keepdims=True)
        up_ref[cut] = scale_ref[cut][:, :1] * (weighted - first - hat * second)

    by_rows(near_rows, 32, add_up)
    for one in norm_dp_copies:
        one.wait_recv()
    value = norm_mid[...]
    for k in range(7):
        value = value + norm_dp[k]
    norm_out[...] = value
    for one in line_copies:
        one.wait_recv()

    def add_line(cut):
        value = total[3, cut].astype(F32)
        for i in range(3):
            value = value + line[i, cut].astype(F32)
        whole[cut] = value.astype(BF)

    by_rows(held, 48, add_line)
    moved.append(regroup(whole, qkv_got))
    for got, out, outer, moves in (
        (grown_got, grown_out, 8, moved[0]), (pair_got, pair_out, 2, moved[1]), (qkv_got, qkv_out, 3, moved[2])
    ):
        for one in moves:
            one.wait_recv()
        in_columns(got, out, outer)
    for one in s.open:
        one.wait_send()


def closing(back, w, low, frames, mean, scale, pair, first, last, norms, gains):
    vmem = pl.BlockSpec(memory_space=pltpu.VMEM)
    hbm = pl.BlockSpec(memory_space=pl.ANY)
    held = pair.shape[1]
    size = held // 4
    n = back.shape[1]
    width = low.shape[1]
    near_rows = low.shape[0] // 4
    grown = (held, first.shape[1] + last.shape[2])
    copies = 2 + 4 + 3 + 1 + 7 + 3 + 9 + 3 + 1
    return pl.pallas_call(
        closing_kernel,
        out_shape=[
            jax.ShapeDtypeStruct((near_rows, width), F32),
            jax.ShapeDtypeStruct((size, 4 * n), BF),
            jax.ShapeDtypeStruct((size, 4 * pair.shape[2]), BF),
            jax.ShapeDtypeStruct((size, 4 * grown[1]), BF),
            jax.ShapeDtypeStruct(norms.shape, F32),
        ],
        in_specs=[vmem, hbm, vmem, hbm, hbm, hbm] + [vmem] * 5,
        out_specs=[vmem] * 5,
        scratch_shapes=[
            pltpu.VMEM((2 * near_rows, width), BF),
            pltpu.VMEM((2 * near_rows, width), BF),
            pltpu.VMEM((near_rows, width), BF),
            pltpu.VMEM((near_rows, width), BF),
            pltpu.VMEM(norms.shape, F32),
            pltpu.VMEM((3,) + norms.shape, F32),
            pltpu.VMEM(norms.shape, F32),
            pltpu.VMEM((7,) + norms.shape, F32),
            pltpu.VMEM((4, 2 * held, n), BF),
            pltpu.VMEM((4, held, n), BF),
            pltpu.VMEM((4, held, n), BF),
            pltpu.VMEM((3, held, n), BF),
            pltpu.VMEM((held, n), BF),
            pltpu.VMEM((4, size, n), BF),
            pltpu.VMEM((3, held, pair.shape[2]), BF),
            pltpu.VMEM((held, pair.shape[2]), BF),
            pltpu.VMEM((4, size, pair.shape[2]), BF),
            pltpu.VMEM(last.shape[1:], BF),
            pltpu.VMEM(grown, BF),
            pltpu.VMEM((4, size, grown[1]), BF),
            pltpu.VMEM(w.shape, BF),
            pltpu.VMEM(frames.shape, BF),
            pltpu.VMEM(mean.shape, F32),
            pltpu.VMEM(scale.shape, F32),
            pltpu.SemaphoreType.DMA((4,)),
            pltpu.SemaphoreType.DMA((copies,)),
            pltpu.SemaphoreType.DMA((copies,)),
        ],
        compiler_params=pltpu.CompilerParams(
            collective_id=1, has_side_effects=True, vmem_limit_bytes=60 << 20
        ),
        cost_estimate=pl.CostEstimate(
            flops=4 * low.shape[0] * width * n, bytes_accessed=300 << 20, transcendentals=0
        ),
        name="closing",
    )(back, w, low, frames, mean, scale, pair, first, last, norms, gains)


def normalized(values):
    center = jnp.mean(values, axis=-1, keepdims=True)
    centered = values - center
    spread = jnp.mean(centered * centered, axis=-1, keepdims=True)
    scale = lax.rsqrt(spread + EPSILON)
    return centered * scale, scale


def norm_input_grad(upstream, gain, xhat, scale):
    weighted = upstream * gain
    first = jnp.mean(weighted, axis=-1, keepdims=True)
    second = jnp.mean(weighted * xhat, axis=-1, keepdims=True)
    return scale * (weighted - first - xhat * second)


def norm_sums(upstream, xhat):
    return jnp.sum(upstream * xhat, axis=0), jnp.sum(upstream, axis=0)


def together(*values):
    return lax.optimization_barrier(values)


def local(
    count,
    frames,
    text,
    cotangent,
    norm_gains,
    norm_biases,
    qkv_weight,
    self_out,
    cross_query,
    cross_kv,
    cross_out,
    up_weight,
    down_weight,
):
    g = Group(count)
    clips, rows, width = frames.shape
    tokens = text.shape[1]
    part = width // 4
    held = width // count
    own_size = held // 4
    ff_rows = down_weight.shape[0] // 4
    near_rows = clips * rows
    seq = g.seq
    place = jnp.stack([jnp.asarray(PLACE, jnp.int32)[a ^ seq] for a in range(4)])
    orders = [seq ^ r for r in REL]

    def columns(weight, outer, inner):
        cut = weight.reshape(weight.shape[0], outer, 4, inner)
        return lax.dynamic_index_in_dim(cut, seq, axis=2, keepdims=False).reshape(weight.shape[0], outer * inner)

    def own_rows(weight):
        size = weight.shape[0] // 4
        return lax.dynamic_slice_in_dim(weight, seq * size, size, axis=0)

    def cut_rows(value):
        return value[:near_rows], value[near_rows : 2 * near_rows], value[2 * near_rows :]

    def piece(value, i, axis):
        return lax.dynamic_index_in_dim(value, orders[i], axis=axis, keepdims=False)

    frames_in = frames.reshape(near_rows, width)
    cot_in = cotangent.reshape(near_rows, width)
    text_in = text.reshape(clips * tokens, width)

    mix_own = jnp.stack([own_rows(self_out), own_rows(cross_query), own_rows(cross_out)])
    mix_whole = lax.all_gather(mix_own, ("dp", "seq"), axis=1, tiled=True)
    w_self, w_query, w_cross = mix_whole[0], mix_whole[1], mix_whole[2]

    norm_own = jnp.concatenate([norm_gains, norm_biases], axis=0)
    if g.paired:
        w_qkv, w_pair, both_own, frames_all, first_low, center, scale_all, text_all, norms = opening(
            qkv_weight, cross_kv, up_weight, down_weight, frames_in, text_in, norm_own
        )
        w_qkv, w_pair = w_qkv.reshape(width, 3 * part), w_pair.reshape(width, 2 * part)
        frames_all = frames_all.reshape(4 * near_rows, width)
        first_low = first_low.reshape(4 * near_rows, width)
        text_all = text_all.reshape(4 * clips * tokens, width)
        norms = norms.swapaxes(0, 1).reshape(6, width).astype(F32)
        center, scale_all = center.reshape(4 * near_rows, 128), scale_all.reshape(4 * near_rows, 128)
        gains, biases = norms[:3], norms[3:]
    else:
        w_qkv = lax.all_gather(columns(qkv_weight, 3, part), "dp", axis=0, tiled=True)
        w_pair = lax.all_gather(columns(cross_kv, 2, part), "dp", axis=0, tiled=True)
        both_own = jnp.stack([columns(up_weight, count, ff_rows), own_rows(down_weight)])

        def to_all(value):
            over = g.across(value)
            return [value, over, g.core(over), g.core(value)]

        frames_all = jnp.concatenate(to_all(frames_in), axis=0)
        text_all = place_pieces(to_all(text_in), orders, 0)
        norms = lax.all_gather(norm_own, "dp", axis=1, tiled=True).astype(F32)
        gains, biases = norms[:3], norms[3:]
        hat_all, _ = normalized(frames_all.astype(F32))
        first_low = (hat_all * gains[0] + biases[0]).astype(BF)
    w_both = lax.all_gather(both_own, "dp", axis=1, tiled=True)
    w_up, w_down = w_both[0], w_both[1]

    pair_part = dot_nn(text_all, w_pair).astype(BF).reshape(4 * clips * tokens, 2, part).swapaxes(0, 1)
    triple = dot_nn(first_low, w_qkv).astype(BF).reshape(4, clips, rows, 3 * part)
    triple, pair_part, cot_here = together(triple, pair_part, cot_in)

    pair_over, pair_near = g.across(pair_part), g.core(pair_part)
    heads_out, levels = self_forward(place, triple, part)
    cot_over = g.across(cot_here)
    heads_out, levels, pair_over, pair_near, cot_over = together(
        heads_out, levels, pair_over, pair_near, cot_over
    )

    pair_far = g.core(pair_over)
    heads_rows = heads_out.reshape(4, near_rows, part)
    self_mix = exchange(
        heads_to_rows_kernel, heads_rows, (near_rows, width), 2, "heads_to_rows", (near_rows, part)
    )
    pair_all = place_pieces([pair_part, pair_over, pair_far, pair_near], orders, 2).reshape(
        2, 4, clips, tokens, width
    )
    residual = frames_in.astype(F32)
    first_sum = residual + dot_nn(self_mix, w_self)
    hat_two, scale_two = normalized(first_sum)
    second_low = (hat_two * gains[1] + biases[1]).astype(BF)

    cross_q = dot_nn(second_low, w_query).astype(BF).reshape(clips, rows, width)
    cross_mix = cross_forward(cross_q, pair_all).reshape(near_rows, width)
    second_sum = first_sum + dot_nn(cross_mix, w_cross)
    hat_three, scale_three = normalized(second_sum)
    third_own = (hat_three * gains[2] + biases[2]).astype(BF)
    third_low, cot_all = (v.reshape(4 * near_rows, width) for v in rows_to_all(third_own, cot_in, cot_over))

    active_low, hidden_low = middle(third_low, cot_all, w_both)
    hidden_own, hidden_over, hidden_far = cut_rows(hidden_low)
    far = dot_nt(hidden_far, w_up).astype(BF)
    far, hidden_over, hidden_own, active_low = together(far, hidden_over, hidden_own, active_low)

    far = g.core(far)
    over = dot_nt(hidden_over, w_up)
    far, over, active_low, hidden_low, hidden_own = together(far, over, active_low, hidden_low, hidden_own)
    half = far.shape[0] // 2
    over = (over + far[:half].astype(F32)).astype(BF)
    over, active_low, hidden_low, hidden_own, far = together(over, active_low, hidden_low, hidden_own, far)

    crossed = g.across(over)
    down_part = dot_tn(active_low, cot_all).astype(BF)
    down_part, hidden_low, active_low, hidden_own = together(down_part, hidden_low, active_low, hidden_own)
    down_shard = lax.psum_scatter(down_part, "dp", scatter_dimension=0, tiled=True)
    half_columns = hidden_low.shape[1] // 2
    third_up = dot_nt(hidden_own, w_up) + far[half:].astype(F32)
    up_first = dot_tn(third_low, hidden_low[:, :half_columns]).astype(BF).reshape(count, held, -1)
    up_last = dot_tn(third_low, hidden_low[:, half_columns:]).astype(BF).reshape(count, held, -1)
    _, active_over, active_far = cut_rows(active_low)
    block_far = g.core(dot_nn(active_far, w_down).astype(BF))
    crossed, up_first, up_last, block_far, third_up, active_over = together(
        crossed, up_first, up_last, block_far, third_up, active_over
    )
    block_over = dot_nn(active_over, w_down)

    block_crossed = g.across((block_over + block_far[:half].astype(F32)).astype(BF))
    up_first = g.side_sum(up_first)
    third_up = third_up + crossed.astype(F32)
    second_grad = cot_in.astype(F32) + norm_input_grad(third_up, gains[2], hat_three, scale_three)
    gain_third, bias_third = norm_sums(third_up, hat_three)
    second_in = second_grad.astype(BF)
    mix_grad = dot_nt(second_in, w_cross).astype(BF).reshape(clips, rows, width)
    query_back, key_sums, value_sums = cross_backward(cross_q, pair_all, mix_grad)
    query_back = query_back.reshape(near_rows, width)
    second_up = dot_nt(query_back, w_query)
    first_grad = second_grad + norm_input_grad(second_up, gains[1], hat_two, scale_two)
    gain_second, bias_second = norm_sums(second_up, hat_two)
    first_in = first_grad.astype(BF)
    self_grad = dot_nt(first_in, w_self).astype(BF)
    self_grad, block_crossed, up_last, up_first, first_in, query_back = together(
        self_grad, block_crossed, up_last, up_first, first_in, query_back
    )

    up_first = g.far_sum(up_first)
    up_last = g.side_sum(up_last)
    mix_part = jnp.stack(
        [dot_tn(self_mix, first_in), dot_tn(second_low, query_back), dot_tn(cross_mix, second_in)]
    ).astype(BF)
    mix_part, self_grad = together(mix_part, self_grad)
    mix_shard = lax.psum_scatter(mix_part, ("dp", "seq"), scatter_dimension=1, tiled=True)
    flat_tokens = 4 * clips * tokens
    grads, pair_back, block_output = rows_to_heads(
        self_grad, key_sums.reshape(flat_tokens, width), value_sums.reshape(flat_tokens, width),
        active_low, w_both, second_sum, block_far, block_crossed,
    )
    grads, pair_back, up_first, up_last = together(grads, pair_back, up_first, up_last)
    pair_grad = dot_tn(text_all, pair_back).astype(BF).reshape(count, held, -1)
    pair_grad, grads = together(pair_grad, grads)

    pair_sum = g.side_sum(pair_grad)
    up_last = g.far_sum(up_last)
    up_first = g.near_sum(up_first)
    triple_back = self_backward(
        place, triple, grads.reshape(4, clips, rows, part), levels, part
    ).reshape(4 * near_rows, 3 * part)
    triple_back, up_first, up_last, pair_sum = together(triple_back, up_first, up_last, pair_sum)
    pair_half = g.add(pair_sum).reshape(4, held, -1) if g.paired else None

    text_part = dot_nt(pair_back, w_pair).reshape(4, clips * tokens, width)
    text_far = g.core(jnp.stack([piece(text_part, 2, 0), piece(text_part, 3, 0)]).astype(BF))
    def regroup_over(value):
        sends = [lax.dynamic_slice_in_dim(value, o * own_size, own_size, axis=0) for o in orders]
        return [sends[0], g.across(jnp.stack([sends[1], sends[2]])), g.core(sends[3])]

    def regroup(parts, outer, inner):
        own, over, near = parts
        out = jnp.zeros((4, own_size, outer, inner), BF)
        for one, order in zip((own, over[0], g.core(over[1]), near), orders):
            out = lax.dynamic_update_slice(out, one.reshape(1, own_size, outer, inner), (order, 0, 0, 0))
        return in_columns(out)

    def in_columns(value):
        return value.transpose(1, 2, 0, 3).reshape(value.shape[1], -1).astype(F32)

    text_crossed = g.across((piece(text_part, 1, 0) + text_far[0].astype(F32)).astype(BF))
    if g.paired:
        blank = jnp.zeros((width,), F32)
        norm_part = jnp.stack(
            [blank, gain_second, gain_third, blank, bias_second, bias_third, blank, blank]
        )
        frame_grad, qkv_out, pair_out, up_out, norm_all = closing(
            triple_back, w_qkv, first_low, frames_all, center, scale_all, pair_half, g.total(up_first),
            g.add(up_last), norm_part, norms,
        )
        frame_grad = first_grad + frame_grad
        qkv_out, pair_out, up_out = (v.astype(F32) for v in (qkv_out, pair_out, up_out))
        norm_all = norm_all[:6]
    else:
        full = dot_nt(triple_back, w_qkv)
        own_full, over_full, far_full = cut_rows(full)
        far = g.core(far_full.astype(BF))
        crossed = g.across((over_full + far[:half].astype(F32)).astype(BF))
        first_up = own_full + far[half:].astype(F32) + crossed.astype(F32)
        qkv_part = dot_tn(first_low, triple_back).astype(BF)
        hat_one, scale_one = normalized(residual)
        frame_grad = first_grad + norm_input_grad(first_up, gains[0], hat_one, scale_one)
        gain_first, bias_first = norm_sums(full, hat_all)
        norm_part = jnp.stack([gain_first, gain_second, gain_third, bias_first, bias_second, bias_third])
        norm_all = lax.psum(norm_part, ("dp", "seq"))
        qkv_shard = lax.psum_scatter(qkv_part.reshape(width, -1), "dp", scatter_dimension=0, tiled=True)
        qkv_out = regroup(regroup_over(qkv_shard), 3, part)
        pair_shard = lax.psum_scatter(pair_grad.reshape(width, -1), "dp", scatter_dimension=0, tiled=True)
        pair_out = regroup(regroup_over(pair_shard), 2, part)
        up_grad = jnp.concatenate([g.total(up_first), g.total(g.near_sum(up_last))], axis=-1)
        up_out = regroup(regroup_over(up_grad), count, ff_rows)
    text_grad = piece(text_part, 0, 0) + text_far[1].astype(F32) + text_crossed.astype(F32)

    small = width // (4 * count)
    norm_shard = lax.dynamic_slice_in_dim(norm_all, (g.dp * 4 + seq) * small, small, axis=1)
    mix_shard = mix_shard.astype(F32)
    return (
        block_output.reshape(clips, rows, width),
        frame_grad.reshape(clips, rows, width),
        text_grad.reshape(clips, tokens, width),
        norm_shard[:3],
        norm_shard[3:],
        qkv_out,
        mix_shard[0],
        mix_shard[1],
        pair_out,
        mix_shard[2],
        up_out,
        down_shard.astype(F32),
    )


def solution(mesh):
    rows = P("dp", "seq", None)
    both = P(("dp", "seq"), None)
    return jax.shard_map(
        functools.partial(local, mesh.shape["dp"]),
        mesh=mesh,
        in_specs=(rows, rows, rows, P(None, "dp"), P(None, "dp")) + (P("dp", None),) * 7,
        out_specs=(rows, rows, rows, P(None, ("dp", "seq")), P(None, ("dp", "seq"))) + (both,) * 7,
        check_vma=False,
    )
```
